128 devices in a mesh: seq: 32 (over z, x, y_hi), head: 4 (over y_lo, core).
Axes of the slice: x: 4, y: 4 (y_hi: 2, y_lo: 2; y = y_hi * 2 + y_lo), z: 4, core: 2. Of those that a mesh axis runs over, the one named last changes fastest.
Arguments:
- tokens: bfloat16 [8192, 2048], P('seq'), may hold values from -6 to 6
- input_gain: float32 [2048], replicated, may hold values from 0.1 to 1.9
- w_query: bfloat16 [2048, 4096], P(None, 'head'), may hold values from -0.125 to 0.125
- w_key: bfloat16 [2048, 512], P(None, 'head'), may hold values from -0.125 to 0.125
- w_value: bfloat16 [2048, 512], P(None, 'head'), may hold values from -0.125 to 0.125
- query_gain: float32 [128], replicated, may hold values from 1 to 8
- key_gain: float32 [128], replicated, may hold values from 1 to 8
- w_out: bfloat16 [4096, 2048], P('head'), may hold values from -0.09375 to 0.09375
- post_gain: float32 [2048], replicated, may hold values from 0.1 to 1.9
- expert_ids: int32 [8192, 8], P(('seq', 'head')), may hold values from 0 to 127, all different within a row; in each aligned block of 64 rows (0 to 63, 64 to 127, ...) at most 6 rows name the same one
- route_weights: float32 [8192, 8], P(('seq', 'head')), may hold values from 0.05 to 1
- w_gate: bfloat16 [128, 2048, 768], P(('seq', 'head')), may hold values from -0.125 to 0.125
- w_up: bfloat16 [128, 2048, 768], P(('seq', 'head')), may hold values from -0.125 to 0.125
- w_down: bfloat16 [128, 768, 2048], P(('seq', 'head')), may hold values from -0.21875 to 0.21875
Outputs:
- layer_out: bfloat16 [8192, 2048], P(('seq', 'head'))
The draws below stay inside these ranges and needn't reach their ends.
Inputs may be any that keep to these rules, and one draw needn't show every extreme that they name: `expert_ids`: the 8 experts of a token differ. In the rows of one device (64 tokens, aligned blocks), no expert is named more than 6 times.
All inputs are finite; a program needn't handle non-finite values.
Results may differ from the reference program's by a relative error of at most 0.012.
The reference program's roundings to bfloat16 on the way (of `normed`, `value_rows`, `probs`, `attended`, `routed`, `hidden` and `expert_rows`) count: a program that leaves them out, or rounds other values in their place, can miss the bound.
Values may be sent and summed in bfloat16 or wider, within the bound.
A program may use at most 128 MiB of HBM per device.

```python
import math
import jax
import jax.numpy as jnp
import numpy as np
from jax import lax

D = 2048
HEADS = 32
KV_HEADS = 4
HEAD_DIM = 128
FF = 768
TOPK = 8
TOKENS = 8192
EXPERTS = 128
ROWS = 64
CAP = 6


def gain_values(base_key):
    return jnp.exp(jax.random.uniform(base_key, (HEAD_DIM,), jnp.float32, 0.0, 1.0986))


def draw_query_gain(key, part):
    return gain_values(jax.random.fold_in(key, 11))


def draw_key_gain(key, part):
    return gain_values(jax.random.fold_in(key, 23))


def block_scale(key, shape, cuts, low, high):
    def one(dim, parts):
        heights = jax.random.uniform(jax.random.fold_in(jax.random.fold_in(key, 6), dim), (parts,), jnp.float32, low / len(cuts), high / len(cuts))
        return jnp.repeat(jnp.exp(heights), shape[dim] // parts).reshape((-1,) + (1,) * (len(shape) - dim - 1))

    factor_of = one(*cuts[0])
    for cut in cuts[1:]:
        factor_of = factor_of * one(*cut)
    return factor_of


def routed_block(stream_key, own, number, rows, count, top, limit, slope):
    ranking = jax.random.permutation(stream_key, count)
    packed, common = portions_of(count, rows * top, limit, slope, True), portions_of(count, rows * top, limit, slope, False)
    places = jnp.arange(count)

    def named(tallies, turn):
        used = int((tallies > 0).sum())
        fixed = max(1, used // 4)
        passed = fixed + (places - fixed + turn * (used - fixed)) % max(1, count - fixed)
        return jnp.zeros((count,), jnp.int32).at[ranking[jnp.where(places < fixed, places, passed)]].set(jnp.asarray(tallies, jnp.int32))

    tallies = jnp.where(number % 4 == 0, named(packed, number // 4), named(common, number - number // 4 - 1))
    mixed = jax.random.permutation(jax.random.fold_in(own, 3), count)
    giver, receiver = mixed[0:count // 2 * 2:2], mixed[1:count // 2 * 2:2]
    margin = jnp.minimum(tallies[giver] - 1, limit - tallies[receiver]) // 2
    margin = jnp.where((giver == ranking[0]) | (receiver == ranking[0]) | (tallies[receiver] == 0), 0, jnp.maximum(margin, 0))
    passed = jax.random.randint(jax.random.fold_in(own, 4), (count // 2,), 0, 1 << 20) % (margin + 1)
    tallies = tallies.at[giver].add(-passed).at[receiver].add(passed)
    labels = jnp.searchsorted(jnp.cumsum(tallies), jnp.arange(rows * top), side="right").astype(jnp.int32)
    listing = labels.reshape(top, rows).T
    listing = listing[jax.random.permutation(jax.random.fold_in(own, 1), rows)]
    turn = jax.random.randint(jax.random.fold_in(own, 2), (rows, 1), 0, top)
    return jnp.take_along_axis(listing, (jnp.arange(top)[None, :] + turn) % top, axis=1)


def portions_of(count, total, most, slope, full):
    weights = [(1 << 20) // math.isqrt(rank ** slope) + 1 for rank in range(1, count + 1)]
    largest = most if full else min(most, max(-(-total // count), total * weights[0] // sum(weights)))
    least = 1 if total - largest >= count - 1 else 0
    counts, surplus = [largest] + [least] * (count - 1), total - largest - least * (count - 1)
    while surplus > 0:
        candidates = [i for i in range(1, count) if counts[i] < largest] or [i for i in range(1, count) if counts[i] < most]
        whole, left = sum([weights[i] for i in candidates]), surplus
        for i in candidates:
            more = min(most - counts[i], max(1, left * weights[i] // whole), surplus)
            counts[i] = counts[i] + more
            surplus = surplus - more
    return np.array(counts)


def bell_draw(rng, shape, scale, reach, shards=(), kind=jnp.bfloat16):
    level = block_scale(rng, shape, shards, -0.22, 0.18) if shards else 1.0
    result = jax.random.normal(rng, shape, jnp.float32) * scale * level
    return jnp.minimum(jnp.maximum(result, -reach), reach).astype(kind)


def setup_inputs(seed: int = 0) -> dict:
    arg_keys = jax.random.split(jax.random.key(seed), 15)
    tokens = bell_draw(arg_keys[0], (TOKENS, D), 1.0, 6.0, ((0, 32),))
    input_gain = jnp.clip(1.0 + 0.18 * jax.random.normal(arg_keys[1], (D,), jnp.float32), 0.1, 1.9)
    w_query = bell_draw(arg_keys[2], (D, HEADS * HEAD_DIM), D ** -0.5, 0.125, ((1, 4),))
    w_key = bell_draw(arg_keys[3], (D, KV_HEADS * HEAD_DIM), D ** -0.5, 0.125, ((1, 4),))
    w_value = bell_draw(arg_keys[4], (D, KV_HEADS * HEAD_DIM), D ** -0.5, 0.125, ((1, 4),))
    query_gain = draw_query_gain(jax.random.fold_in(arg_keys[14], 71), 0)
    key_gain = draw_key_gain(jax.random.fold_in(arg_keys[14], 71), 0)
    w_out = bell_draw(arg_keys[7], (HEADS * HEAD_DIM, D), (HEADS * HEAD_DIM) ** -0.5, 0.09375, ((0, 4),))
    post_gain = jnp.clip(1.0 + 0.18 * jax.random.normal(arg_keys[8], (D,), jnp.float32), 0.1, 1.9)
    expert_ids_keys = jax.random.split(jax.random.fold_in(arg_keys[9], 1), TOKENS // ROWS)
    expert_ids_turns = jax.random.permutation(jax.random.fold_in(arg_keys[9], 3), TOKENS // ROWS)
    expert_ids = jax.vmap(lambda own, number: routed_block(jax.random.fold_in(arg_keys[9], 2), own, number, ROWS, EXPERTS, TOPK, CAP, 2))(expert_ids_keys, expert_ids_turns).reshape((TOKENS, TOPK))
    route_weights = jnp.clip(jnp.exp(math.log(1.0) - 2.9957323 * jax.random.uniform(arg_keys[10], (TOKENS, TOPK), jnp.float32) ** block_scale(arg_keys[10], (TOKENS, TOPK), ((0, 128),), -0.2, 0.2)), 0.05, 1.0)
    w_gate = bell_draw(arg_keys[11], (EXPERTS, D, FF), D ** -0.5, 0.125, ((0, 128),))
    w_up = bell_draw(arg_keys[12], (EXPERTS, D, FF), D ** -0.5, 0.125, ((0, 128),))
    w_down = bell_draw(arg_keys[13], (EXPERTS, FF, D), FF ** -0.5, 0.21875, ((0, 128),))
    return {"tokens": tokens, "input_gain": input_gain, "w_query": w_query, "w_key": w_key, "w_value": w_value, "query_gain": query_gain, "key_gain": key_gain, "w_out": w_out, "post_gain": post_gain, "expert_ids": expert_ids, "route_weights": route_weights, "w_gate": w_gate, "w_up": w_up, "w_down": w_down}


EPSILON = 1e-06
THETA = 1000000.0

def rms_scale(vectors, gain_vector):
    mean_sq = lax.optimization_barrier(jnp.mean(vectors * vectors, axis=-1, keepdims=True))
    return vectors * lax.rsqrt(mean_sq + EPSILON) * gain_vector

def rotate(vectors, positions):
    half_dim = vectors.shape[-1] // 2
    frequency = THETA ** (-jnp.arange(half_dim, dtype=jnp.float32) * 2.0 / vectors.shape[-1])
    angles = positions[:, None] * frequency[None, :]
    cosine_table = jnp.cos(angles)[:, None, :]
    sine_table = jnp.sin(angles)[:, None, :]
    front_half = vectors[..., :half_dim]
    back_half = vectors[..., half_dim:]
    return jnp.concatenate([front_half * cosine_table - back_half * sine_table, back_half * cosine_table + front_half * sine_table], axis=-1)

def reference(tokens, input_gain, w_query, w_key, w_value, query_gain, key_gain, w_out, post_gain, expert_ids, route_weights, w_gate, w_up, w_down):
    normed = rms_scale(tokens.astype(jnp.float32), input_gain).astype(jnp.bfloat16)
    positions = jnp.arange(TOKENS, dtype=jnp.int32).astype(jnp.float32)
    queries = jnp.dot(normed, w_query, preferred_element_type=jnp.float32).reshape(TOKENS, HEADS, HEAD_DIM)
    key_rows = jnp.dot(normed, w_key, preferred_element_type=jnp.float32).reshape(TOKENS, KV_HEADS, HEAD_DIM)
    value_rows = jnp.dot(normed, w_value, preferred_element_type=jnp.float32).astype(jnp.bfloat16).reshape(TOKENS, KV_HEADS, HEAD_DIM)
    rot_q = rotate(rms_scale(queries, query_gain), positions).astype(jnp.bfloat16)
    rot_k = rotate(rms_scale(key_rows, key_gain), positions).astype(jnp.bfloat16)
    group_size = HEADS // KV_HEADS
    block_rows = math.gcd(TOKENS, 512)
    block_count = TOKENS // block_rows
    score_scale = HEAD_DIM ** (-0.5)
    key_float = rot_k.astype(jnp.float32)
    value_float = value_rows.astype(jnp.float32)
    key_positions = jnp.arange(TOKENS, dtype=jnp.int32)

    def attend(block_index):
        row_start = (block_index * block_rows).astype(jnp.int32)
        query_block = lax.dynamic_slice_in_dim(rot_q, row_start, block_rows, 0).astype(jnp.float32)
        query_positions = row_start + jnp.arange(block_rows, dtype=jnp.int32)
        allowed = key_positions[None, :] <= query_positions[:, None]
        outputs = []
        for kv_head in range(KV_HEADS):
            query_part = query_block[:, kv_head * group_size:(kv_head + 1) * group_size, :]
            scores = jnp.einsum('bhd,ud->hbu', query_part, key_float[:, kv_head, :], precision=lax.Precision.HIGHEST) * score_scale
            scores = jnp.where(allowed[None], scores, -jnp.inf)
            row_max = lax.optimization_barrier(jnp.max(scores, axis=-1, keepdims=True))
            expw = jnp.exp(scores - row_max)
            weight_sum = lax.optimization_barrier(jnp.sum(expw, axis=-1))
            probs = expw.astype(jnp.bfloat16).astype(jnp.float32)
            mixed = jnp.einsum('hbu,ud->bhd', probs, value_float[:, kv_head, :], precision=lax.Precision.HIGHEST)
            outputs.append(mixed / jnp.transpose(weight_sum)[:, :, None])
        return jnp.concatenate(outputs, axis=1).reshape(block_rows, HEADS * HEAD_DIM).astype(jnp.bfloat16)
    attended = lax.map(attend, jnp.arange(block_count, dtype=jnp.int32)).reshape(TOKENS, HEADS * HEAD_DIM)
    residual = tokens.astype(jnp.float32) + jnp.dot(attended, w_out, preferred_element_type=jnp.float32)
    routed = rms_scale(residual, post_gain).astype(jnp.bfloat16)
    mixing = route_weights / lax.optimization_barrier(jnp.sum(route_weights, axis=-1, keepdims=True))
    part_count = TOKENS // ROWS
    grouped_ids = expert_ids.reshape(part_count, ROWS * TOPK)
    onehot = (grouped_ids[..., None] == jnp.arange(EXPERTS, dtype=jnp.int32)[None, None, :]).astype(jnp.int32)
    rank_table = jnp.cumsum(onehot, axis=1) - onehot
    slot_index = lax.optimization_barrier(jnp.sum(rank_table * onehot, axis=-1))
    slot_place = (jnp.arange(part_count, dtype=jnp.int32)[:, None] * CAP + slot_index).reshape(-1).astype(jnp.int32)
    flat_experts = expert_ids.reshape(-1).astype(jnp.int32)
    copy_index = jnp.arange(TOKENS * TOPK, dtype=jnp.int32)
    copy_table = jnp.full((EXPERTS, part_count * CAP), TOKENS * TOPK, jnp.int32).at[flat_experts, slot_place].set(copy_index)
    padded_rows = jnp.concatenate([routed, jnp.zeros((1, D), jnp.bfloat16)], axis=0)
    mix_flat = jnp.concatenate([mixing.reshape(-1), jnp.zeros((1,), jnp.float32)])

    def run_expert(combined, inputs):
        copy_ids, gate_weight, up_weight, down_weight = inputs
        token_ids = copy_ids // TOPK
        rows_in = padded_rows[token_ids].astype(jnp.float32)
        gate_proj = jnp.dot(rows_in, gate_weight.astype(jnp.float32), precision=lax.Precision.HIGHEST)
        up_proj = jnp.dot(rows_in, up_weight.astype(jnp.float32), precision=lax.Precision.HIGHEST)
        hidden = (jax.nn.silu(gate_proj) * up_proj).astype(jnp.bfloat16).astype(jnp.float32)
        expert_rows = jnp.dot(hidden, down_weight.astype(jnp.float32), precision=lax.Precision.HIGHEST).astype(jnp.bfloat16)
        weighted = expert_rows.astype(jnp.float32) * mix_flat[copy_ids][:, None]
        return (combined.at[token_ids].add(weighted), None)
    combined, _ = lax.scan(run_expert, jnp.zeros((TOKENS + 1, D), jnp.float32), (copy_table, w_gate, w_up, w_down))
    return (residual + combined[:TOKENS]).astype(jnp.bfloat16)
```

```python
import functools

import jax
import jax.numpy as jnp
from jax import lax
from jax.experimental import pallas as pl
from jax.experimental.pallas import tpu as pltpu
from jax.sharding import PartitionSpec as P

MESH = pl.DeviceIdType.MESH
EPSILON = 1e-06
THETA = 1000000.0
LOG2E = 1.4426950408889634
GROUP = 4


def attention_kernel(
    seq_count, heads, rows, dim, kv_ref, q_ref, out_ref, kvbuf, m_s, l_s, acc, send_sem, recv_sem, own_sem
):
    i = lax.axis_index("seq")
    h = lax.axis_index("head")
    barrier = pltpu.get_barrier_semaphore()

    def greet(j, c):
        @pl.when(j != i)
        def _():
            pl.semaphore_signal(barrier, inc=1, device_id=(j, h), device_id_type=MESH)

        return c

    lax.fori_loop(0, seq_count, greet, 0)
    own = pltpu.make_async_copy(kv_ref, kvbuf.at[i], own_sem)
    own.start()
    first_group = i // GROUP
    for u in range(GROUP):

        @pl.when(first_group * GROUP + u > i)
        def _():
            kvbuf[first_group * GROUP + u] = jnp.zeros(kvbuf.shape[1:], kvbuf.dtype)

    pl.semaphore_wait(barrier, seq_count - 1)

    def push(peer):
        return pltpu.make_async_remote_copy(
            src_ref=kv_ref,
            dst_ref=kvbuf.at[i],
            send_sem=send_sem.at[peer],
            recv_sem=recv_sem.at[i],
            device_id=(peer, h),
            device_id_type=MESH,
        )

    def arrival(source):
        return pltpu.make_async_remote_copy(
            src_ref=kv_ref,
            dst_ref=kvbuf.at[source],
            send_sem=send_sem.at[source],
            recv_sem=recv_sem.at[source],
            device_id=(source, h),
            device_id_type=MESH,
        )

    def start(t, c):
        peer = lax.rem(i + t * 13, seq_count)

        @pl.when(peer > i)
        def _():
            push(peer).start()

        return c

    lax.fori_loop(1, seq_count, start, 0)
    own.wait()
    scale = dim ** (-0.5) * LOG2E

    def group(g, masked):
        for u in range(GROUP):

            @pl.when(g * GROUP + u < i)
            def _():
                arrival(g * GROUP + u).wait_recv()

        keys = jnp.concatenate([kvbuf[g * GROUP + u, 0:rows, :] for u in range(GROUP)], axis=0)
        halves = [
            kvbuf[g * GROUP + u, rows + dim * w : rows + dim * (w + 1), :]
            for u in range(GROUP)
            for w in range(rows // dim)
        ]
        values = jnp.concatenate(halves, axis=1)
        values = jnp.concatenate([values, jnp.ones((16, values.shape[1]), values.dtype)], axis=0)
        scores = jnp.dot(keys, q_ref[...], preferred_element_type=jnp.float32)
        if masked:
            key_at = lax.broadcasted_iota(jnp.int32, scores.shape, 0)
            query_at = lax.broadcasted_iota(jnp.int32, scores.shape, 1) % rows + (i - g * GROUP) * rows
            scores = jnp.where(key_at <= query_at, scores, -1e30)
        top = jnp.max(scores, axis=0, keepdims=True)
        if not masked:
            top = jnp.maximum(top, m_s[...])
        weights = jnp.exp2(scores * scale - top * scale)
        mixed = jnp.dot(values, weights.astype(jnp.bfloat16), preferred_element_type=jnp.float32)
        if masked:
            l_s[...] = mixed[dim : dim + 1]
            acc[...] = mixed[:dim]
        else:
            shrink = jnp.exp2((m_s[...] - top) * scale)
            l_s[...] = l_s[...] * shrink + mixed[dim : dim + 1]
            acc[...] = acc[...] * shrink + mixed[:dim]
        m_s[...] = top

    group(first_group, True)

    def earlier(t, c):
        group(first_group - t, False)
        return c

    lax.fori_loop(1, first_group + 1, earlier, 0)
    for head in range(heads):
        columns = slice(head * rows, (head + 1) * rows)
        part = acc[:, columns] / l_s[:, columns]
        out_ref[:, head * dim : (head + 1) * dim] = part.T.astype(jnp.bfloat16)

    def finish(peer, c):
        @pl.when(peer > i)
        def _():
            push(peer).wait_send()

        return c

    lax.fori_loop(0, seq_count, finish, 0)


def attention(kv, q, seq_count, heads, rows, dim):
    return pl.pallas_call(
        functools.partial(attention_kernel, seq_count, heads, rows, dim),
        out_shape=jax.ShapeDtypeStruct((rows, heads * dim), jnp.bfloat16),
        in_specs=[pl.BlockSpec(memory_space=pltpu.VMEM)] * 2,
        out_specs=pl.BlockSpec(memory_space=pltpu.VMEM),
        scratch_shapes=[
            pltpu.VMEM((seq_count,) + kv.shape, jnp.bfloat16),
            pltpu.VMEM((1, heads * rows), jnp.float32),
            pltpu.VMEM((1, heads * rows), jnp.float32),
            pltpu.VMEM((dim, heads * rows), jnp.float32),
            pltpu.SemaphoreType.DMA((seq_count,)),
            pltpu.SemaphoreType.DMA((seq_count,)),
            pltpu.SemaphoreType.DMA,
        ],
        compiler_params=pltpu.CompilerParams(
            collective_id=0, has_side_effects=True, vmem_limit_bytes=50 << 20
        ),
        name="attention",
    )(kv, q)


def cut_along(array, dim, devices):
    dims = array.shape
    blocks = array.reshape(*dims[:dim], devices, dims[dim] // devices, *dims[dim + 1 :])
    return jnp.moveaxis(blocks, dim, 0)


def summed_on_arrival(array, axis, dim):
    blocks = cut_along(array, dim, lax.axis_size(axis))
    arrived = lax.all_to_all(blocks, axis, split_axis=0, concat_axis=0, tiled=True)
    return arrived.astype(jnp.float32).sum(axis=0)


def joined_along(blocks, dim):
    blocks = jnp.moveaxis(blocks, 0, dim)
    dims = blocks.shape
    return blocks.reshape(*dims[:dim], dims[dim] * dims[dim + 1], *dims[dim + 2 :])


def one_exchange(array, axis, axes, splits, concats):
    sizes = [lax.axis_size(a) for a in axes]
    blocks = cut_along(array, splits[0], sizes[0])
    blocks = jnp.moveaxis(cut_along(blocks, splits[1] + 1, sizes[1]), 0, 1)
    inside = blocks.shape[2:]
    blocks = blocks.reshape(-1, *inside)
    blocks = lax.all_to_all(blocks, axis, split_axis=0, concat_axis=0, tiled=True)
    blocks = joined_along(blocks.reshape(*sizes, *inside), concats[0] + 1)
    return joined_along(blocks, concats[1])


def rms_scale(vectors, gain_vector):
    mean_sq = jnp.mean(vectors * vectors, axis=-1, keepdims=True)
    return vectors * lax.rsqrt(mean_sq + EPSILON) * gain_vector


def rotate(vectors, positions):
    half_dim = vectors.shape[-1] // 2
    frequency = THETA ** (-jnp.arange(half_dim, dtype=jnp.float32) * 2.0 / vectors.shape[-1])
    angles = positions[:, None] * frequency[None, :]
    cosine_table = jnp.cos(angles)[:, None, :]
    sine_table = jnp.sin(angles)[:, None, :]
    front_half = vectors[..., :half_dim]
    back_half = vectors[..., half_dim:]
    return jnp.concatenate(
        [
            front_half * cosine_table - back_half * sine_table,
            back_half * cosine_table + front_half * sine_table,
        ],
        axis=-1,
    )


def body(
    tokens,
    input_gain,
    w_query,
    w_key,
    w_value,
    query_gain,
    key_gain,
    w_out,
    post_gain,
    expert_ids,
    route_weights,
    w_gate,
    w_up,
    w_down,
):
    tok_rows, width = tokens.shape
    head_dim = query_gain.shape[0]
    heads_here = w_query.shape[1] // head_dim
    seq_count = lax.axis_size("seq")
    seq_index = lax.axis_index("seq")
    head_count = lax.axis_size("head")
    head_index = lax.axis_index("head")
    normed = rms_scale(tokens.astype(jnp.float32), input_gain).astype(jnp.bfloat16)
    offset = seq_index * tok_rows
    positions = (offset + jnp.arange(tok_rows, dtype=jnp.int32)).astype(jnp.float32)
    queries = jnp.dot(normed, w_query, preferred_element_type=jnp.float32).reshape(
        tok_rows, heads_here, head_dim
    )
    queries = rotate(rms_scale(queries, query_gain), positions).astype(jnp.bfloat16)
    key_rows = jnp.dot(normed, w_key, preferred_element_type=jnp.float32).reshape(
        tok_rows, 1, head_dim
    )
    key_rows = (
        rotate(rms_scale(key_rows, key_gain), positions)
        .astype(jnp.bfloat16)
        .reshape(tok_rows, head_dim)
    )
    value_rows = jnp.dot(normed, w_value, preferred_element_type=jnp.float32).astype(jnp.bfloat16)
    queries = queries.transpose(2, 1, 0).reshape(head_dim, heads_here * tok_rows)
    value_t = value_rows.T.reshape(head_dim, tok_rows // head_dim, head_dim)
    value_t = value_t.transpose(1, 0, 2).reshape(tok_rows, head_dim)
    kv_block = jnp.concatenate([key_rows, value_t], axis=0)
    attended = attention(kv_block, queries, seq_count, heads_here, tok_rows, head_dim)
    rows_here = tok_rows // head_count
    own_rows = lax.dynamic_slice_in_dim(tokens, head_index * rows_here, rows_here, 0)
    part_rows = attended
    attn_part = summed_on_arrival(
        jnp.dot(part_rows, w_out, preferred_element_type=jnp.float32).astype(jnp.bfloat16),
        "head",
        0,
    )
    residual = own_rows.astype(jnp.float32) + attn_part
    routed = rms_scale(residual, post_gain).astype(jnp.bfloat16)
    local_count = w_gate.shape[0]
    experts_all = local_count * seq_count * head_count
    top_count = expert_ids.shape[1]
    copies = rows_here * top_count
    capacity = max(2, 3 * rows_here * top_count // (2 * experts_all))
    flat_ids = expert_ids.reshape(copies)
    onehot = (flat_ids[:, None] == jnp.arange(experts_all, dtype=jnp.int32)[None, :]).astype(
        jnp.bfloat16
    )
    earlier = (jnp.arange(copies)[:, None] > jnp.arange(copies)[None, :]).astype(jnp.bfloat16)
    rank_table = jnp.dot(earlier, onehot, preferred_element_type=jnp.float32)
    slot_index = jnp.sum(rank_table * onehot, axis=1).astype(jnp.int32)
    slot_place = flat_ids * capacity + slot_index
    copy_rows = routed[jnp.arange(copies, dtype=jnp.int32) // top_count]
    outgoing = (
        jnp.zeros((experts_all * capacity, width), jnp.bfloat16).at[slot_place].set(copy_rows)
    )
    outgoing = outgoing.reshape(experts_all, capacity, width)
    sectioned = outgoing.reshape(seq_count, head_count, local_count * capacity, width)
    arrived = one_exchange(sectioned, ("seq", "head"), ("seq", "head"), (0, 1), (0, 1))
    slot_batch = arrived.reshape(experts_all, capacity, width)
    slot_count = slot_batch.shape[1]
    sources = experts_all // local_count
    grouped = (
        slot_batch.reshape(sources, local_count, slot_count, width)
        .transpose(1, 0, 2, 3)
        .reshape(local_count, sources * slot_count, width)
    )
    gate_proj = jnp.einsum("erd,edf->erf", grouped, w_gate, preferred_element_type=jnp.float32)
    up_proj = jnp.einsum("erd,edf->erf", grouped, w_up, preferred_element_type=jnp.float32)
    hidden = (jax.nn.silu(gate_proj) * up_proj).astype(jnp.bfloat16)
    result = jnp.einsum("erf,efd->erd", hidden, w_down, preferred_element_type=jnp.float32).astype(
        jnp.bfloat16
    )
    finished = (
        result.reshape(local_count, sources, slot_count, width)
        .transpose(1, 0, 2, 3)
        .reshape(experts_all, slot_count, width)
        .reshape(seq_count, head_count, local_count * capacity, width)
    )
    returned = one_exchange(finished, ("seq", "head"), ("seq", "head"), (0, 1), (0, 1)).reshape(
        experts_all * capacity, width
    )
    gathered = returned[slot_place].reshape(rows_here, top_count, width)
    mixing = route_weights / jnp.sum(route_weights, axis=1, keepdims=True)
    expert_sum = jnp.sum(gathered.astype(jnp.float32) * mixing[:, :, None], axis=1)
    return (residual + expert_sum).astype(jnp.bfloat16)


def solution(mesh):
    placed = (
        P("seq", None),
        P(),
        P(None, "head"),
        P(None, "head"),
        P(None, "head"),
        P(),
        P(),
        P("head", None),
        P(),
        P(("seq", "head"), None),
        P(("seq", "head"), None),
        P(("seq", "head"), None, None),
        P(("seq", "head"), None, None),
        P(("seq", "head"), None, None),
    )
    return jax.shard_map(
        body, mesh=mesh, in_specs=placed, out_specs=P(("seq", "head"), None), check_vma=False
    )
```

```python
import functools

import jax
import jax.numpy as jnp
from jax import lax
from jax.experimental import pallas as pl
from jax.experimental.pallas import tpu as pltpu
from jax.sharding import PartitionSpec as P

MESH = pl.DeviceIdType.MESH
EPSILON = 1e-06
THETA = 1000000.0
LOG2E = 1.4426950408889634
GROUP = 4
CAPACITY = 6


def attention_kernel(
    seq_count, heads, rows, dim, kv_ref, q_ref, out_ref, kvbuf, m_s, l_s, acc, send_sem, recv_sem, own_sem
):
    i = lax.axis_index("seq")
    h = lax.axis_index("head")
    barrier = pltpu.get_barrier_semaphore()

    def greet(j, c):
        @pl.when(j != i)
        def _():
            pl.semaphore_signal(barrier, inc=1, device_id=(j, h), device_id_type=MESH)

        return c

    lax.fori_loop(0, seq_count, greet, 0)
    own = pltpu.make_async_copy(kv_ref, kvbuf.at[i], own_sem)
    own.start()
    first_group = i // GROUP
    for u in range(GROUP):

        @pl.when(first_group * GROUP + u > i)
        def _():
            kvbuf[first_group * GROUP + u] = jnp.zeros(kvbuf.shape[1:], kvbuf.dtype)

    pl.semaphore_wait(barrier, seq_count - 1)

    def push(peer):
        return pltpu.make_async_remote_copy(
            src_ref=kv_ref,
            dst_ref=kvbuf.at[i],
            send_sem=send_sem.at[peer],
            recv_sem=recv_sem.at[i],
            device_id=(peer, h),
            device_id_type=MESH,
        )

    def arrival(source):
        return pltpu.make_async_remote_copy(
            src_ref=kv_ref,
            dst_ref=kvbuf.at[source],
            send_sem=send_sem.at[source],
            recv_sem=recv_sem.at[source],
            device_id=(source, h),
            device_id_type=MESH,
        )

    def start(t, c):
        peer = lax.rem(i + t * 13, seq_count)

        @pl.when(peer > i)
        def _():
            push(peer).start()

        return c

    lax.fori_loop(1, seq_count, start, 0)
    own.wait()
    scale = dim ** (-0.5) * LOG2E

    def group(g, masked):
        for u in range(GROUP):

            @pl.when(g * GROUP + u < i)
            def _():
                arrival(g * GROUP + u).wait_recv()

        keys = jnp.concatenate([kvbuf[g * GROUP + u, 0:rows, :] for u in range(GROUP)], axis=0)
        halves = [
            kvbuf[g * GROUP + u, rows + dim * w : rows + dim * (w + 1), :]
            for u in range(GROUP)
            for w in range(rows // dim)
        ]
        values = jnp.concatenate(halves, axis=1)
        values = jnp.concatenate([values, jnp.ones((16, values.shape[1]), values.dtype)], axis=0)
        scores = jnp.dot(keys, q_ref[...], preferred_element_type=jnp.float32)
        if masked:
            key_at = lax.broadcasted_iota(jnp.int32, scores.shape, 0)
            query_at = lax.broadcasted_iota(jnp.int32, scores.shape, 1) % rows + (i - g * GROUP) * rows
            scores = jnp.where(key_at <= query_at, scores, -1e30)
        top = jnp.max(scores, axis=0, keepdims=True)
        if not masked:
            top = jnp.maximum(top, m_s[...])
        weights = jnp.exp2(scores * scale - top * scale)
        mixed = jnp.dot(values, weights.astype(jnp.bfloat16), preferred_element_type=jnp.float32)
        if masked:
            l_s[...] = mixed[dim : dim + 1]
            acc[...] = mixed[:dim]
        else:
            shrink = jnp.exp2((m_s[...] - top) * scale)
            l_s[...] = l_s[...] * shrink + mixed[dim : dim + 1]
            acc[...] = acc[...] * shrink + mixed[:dim]
        m_s[...] = top

    group(first_group, True)

    def earlier(t, c):
        group(first_group - t, False)
        return c

    lax.fori_loop(1, first_group + 1, earlier, 0)
    for head in range(heads):
        columns = slice(head * rows, (head + 1) * rows)
        part = acc[:, columns] / l_s[:, columns]
        out_ref[:, head * dim : (head + 1) * dim] = part.T.astype(jnp.bfloat16)

    def finish(peer, c):
        @pl.when(peer > i)
        def _():
            push(peer).wait_send()

        return c

    lax.fori_loop(0, seq_count, finish, 0)


def attention(kv, q, seq_count, heads, rows, dim):
    return pl.pallas_call(
        functools.partial(attention_kernel, seq_count, heads, rows, dim),
        out_shape=jax.ShapeDtypeStruct((rows, heads * dim), jnp.bfloat16),
        in_specs=[pl.BlockSpec(memory_space=pltpu.VMEM)] * 2,
        out_specs=pl.BlockSpec(memory_space=pltpu.VMEM),
        scratch_shapes=[
            pltpu.VMEM((seq_count,) + kv.shape, jnp.bfloat16),
            pltpu.VMEM((1, heads * rows), jnp.float32),
            pltpu.VMEM((1, heads * rows), jnp.float32),
            pltpu.VMEM((dim, heads * rows), jnp.float32),
            pltpu.SemaphoreType.DMA((seq_count,)),
            pltpu.SemaphoreType.DMA((seq_count,)),
            pltpu.SemaphoreType.DMA,
        ],
        compiler_params=pltpu.CompilerParams(
            collective_id=0, has_side_effects=True, vmem_limit_bytes=50 << 20
        ),
        name="attention",
    )(kv, q)


def cut_along(array, dim, devices):
    dims = array.shape
    blocks = array.reshape(*dims[:dim], devices, dims[dim] // devices, *dims[dim + 1 :])
    return jnp.moveaxis(blocks, dim, 0)


def rms_scale(vectors, gain_vector):
    mean_sq = jnp.mean(vectors * vectors, axis=-1, keepdims=True)
    return vectors * lax.rsqrt(mean_sq + EPSILON) * gain_vector


def rotate(vectors, positions):
    half_dim = vectors.shape[-1] // 2
    frequency = THETA ** (-jnp.arange(half_dim, dtype=jnp.float32) * 2.0 / vectors.shape[-1])
    angles = positions[:, None] * frequency[None, :]
    cosine_table = jnp.cos(angles)[:, None, :]
    sine_table = jnp.sin(angles)[:, None, :]
    front_half = vectors[..., :half_dim]
    back_half = vectors[..., half_dim:]
    return jnp.concatenate(
        [
            front_half * cosine_table - back_half * sine_table,
            back_half * cosine_table + front_half * sine_table,
        ],
        axis=-1,
    )


def neighbour(s, h, step, sign):
    z, x, y, core = s // 8, lax.rem(s // 2, 4), lax.rem(s, 2) * 2 + h // 2, lax.rem(h, 2)
    turn = lax.rem(step * 37, 128)
    z = lax.rem(z + sign * (turn // 32) + 4, 4)
    x = lax.rem(x + sign * lax.rem(turn // 8, 4) + 4, 4)
    y = lax.rem(y + sign * lax.rem(turn // 2, 4) + 4, 4)
    core = lax.rem(core + lax.rem(turn, 2), 2)
    return z * 8 + x * 2 + y // 2, lax.rem(y, 2) * 2 + core


def expert_kernel(
    cap,
    chunks,
    idx_ref,
    slot_ref,
    mix_ref,
    own_ref,
    part_ref,
    gain_ref,
    gate_hbm,
    up_hbm,
    down_hbm,
    out_ref,
    gate,
    up,
    down,
    wide,
    home,
    tiles,
    outgoing,
    arrived,
    batch,
    results,
    returned,
    weight_sem,
    send_out,
    recv_out,
    send_back,
    recv_back,
):
    s = lax.axis_index("seq")
    h = lax.axis_index("head")
    me = s * 4 + h
    count = 128
    rows, width = own_ref.shape
    cuts = width // 128
    barrier = pltpu.get_barrier_semaphore()

    def greet(t, c):
        pl.semaphore_signal(barrier, inc=1, device_id=neighbour(s, h, t, 1), device_id_type=MESH)
        return c

    lax.fori_loop(1, count, greet, 0)
    loads = [
        pltpu.make_async_copy(hbm, vmem, weight_sem.at[n])
        for n, (hbm, vmem) in enumerate(((gate_hbm, gate), (up_hbm, up), (down_hbm, down)))
    ]
    for load in loads:
        load.start()
    residual = own_ref[...].astype(jnp.float32)
    for n in range(part_ref.shape[0]):
        residual = residual + part_ref[n].astype(jnp.float32)
    mean_sq = jnp.mean(residual * residual, axis=-1, keepdims=True)
    routed = residual * lax.rsqrt(mean_sq + EPSILON) * gain_ref[...]
    span = rows * cuts
    for c in range(cuts):
        columns = slice(c * 128, (c + 1) * 128)
        home[pl.ds(c, rows, stride=cuts), :] = residual[:, columns]
        wide[pl.ds(c, rows, stride=cuts), :] = routed[:, columns]
    tiles[...] = wide[0:span, :].astype(jnp.bfloat16).reshape(tiles.shape)
    pl.semaphore_wait(barrier, count - 1)

    def fill(t, target, ref, at):
        for c in range(cap):
            token = idx_ref[target * cap + c]
            ref[at * cap + c] = tiles[token]

    def part(ref, t):
        return ref.at[pl.ds(t * cap, cap)]

    def dispatch(t):
        return pltpu.make_async_remote_copy(
            src_ref=part(outgoing, t),
            dst_ref=part(arrived, t),
            send_sem=send_out.at[t],
            recv_sem=recv_out.at[t],
            device_id=neighbour(s, h, t, 1),
            device_id_type=MESH,
        )

    def give_back(t):
        return pltpu.make_async_remote_copy(
            src_ref=part(results, t),
            dst_ref=part(returned, me),
            send_sem=send_back.at[t],
            recv_sem=recv_back.at[me],
            device_id=neighbour(s, h, t, -1),
            device_id_type=MESH,
        )

    def come_back(t):
        ts, th = neighbour(s, h, t, 1)
        expert = ts * 4 + th
        return pltpu.make_async_remote_copy(
            src_ref=part(results, t),
            dst_ref=part(returned, expert),
            send_sem=send_back.at[t],
            recv_sem=recv_back.at[expert],
            device_id=(ts, th),
            device_id_type=MESH,
        )

    def post(t, c):
        ts, th = neighbour(s, h, t, 1)
        fill(t, ts * 4 + th, outgoing, t)
        dispatch(t).start()
        return c

    lax.fori_loop(1, count, post, 0)
    fill(0, me, arrived, 0)
    for load in loads:
        load.wait()
    each = count // chunks
    size = each * cap

    def work(k, c):
        def await_one(t, c):
            @pl.when(t > 0)
            def _():
                dispatch(t).wait_recv()

            return c

        lax.fori_loop(k * each, (k + 1) * each, await_one, 0)
        place = pl.ds(k * size, size)
        wide[...] = arrived[place].astype(jnp.float32).reshape(wide.shape)
        for c in range(cuts):
            batch[:, c * 128 : (c + 1) * 128] = wide[pl.ds(c, size, stride=cuts), :].astype(jnp.bfloat16)
        gate_proj = jnp.dot(batch[...], gate[...], preferred_element_type=jnp.float32)
        up_proj = jnp.dot(batch[...], up[...], preferred_element_type=jnp.float32)
        hidden = (gate_proj / (1.0 + jnp.exp(-gate_proj)) * up_proj).astype(jnp.bfloat16)
        result = jnp.dot(hidden, down[...], preferred_element_type=jnp.float32)
        for c in range(cuts):
            wide[pl.ds(c, size, stride=cuts), :] = result[:, c * 128 : (c + 1) * 128]
        results[place] = wide[...].astype(jnp.bfloat16).reshape(size, cuts, 128)

        def answer(t, c):
            @pl.when(t > 0)
            def _():
                give_back(t).start()

            return c

        lax.fori_loop(k * each, (k + 1) * each, answer, 0)
        return c

    lax.fori_loop(0, chunks, work, 0)
    returned[pl.ds(me * cap, cap)] = results[0:cap]

    def settle(t, c):
        come_back(t).wait_recv()
        return c

    lax.fori_loop(1, count, settle, 0)
    top = mix_ref.shape[0] // rows

    def combine(t, c):
        place = pl.ds(pl.multiple_of(t * cuts, cuts), cuts)
        total = jnp.zeros((cuts, 128), jnp.float32)
        for k in range(top):
            row = returned[slot_ref[t * top + k]]
            total = total + row.astype(jnp.float32) * mix_ref[t * top + k]
        home[place, :] = home[place, :] + total
        return c

    lax.fori_loop(0, rows, combine, 0)
    for c in range(cuts):
        out_ref[:, c * 128 : (c + 1) * 128] = home[pl.ds(c, rows, stride=cuts), :].astype(jnp.bfloat16)

    def finish(t, c):
        dispatch(t).wait_send()
        give_back(t).wait_send()
        return c

    lax.fori_loop(1, count, finish, 0)


def experts(idx, slot, mix, own, parts, gain, w_gate, w_up, w_down, cap):
    rows, width = own.shape
    depth, hidden = w_gate.shape
    cuts = width // 128
    count = 128
    chunks = 4
    size = count * cap // chunks
    smem = pl.BlockSpec(memory_space=pltpu.SMEM)
    vmem = pl.BlockSpec(memory_space=pltpu.VMEM)
    hbm = pl.BlockSpec(memory_space=pl.ANY)
    tiled = pltpu.VMEM((count * cap, cuts, 128), jnp.bfloat16)
    return pl.pallas_call(
        functools.partial(expert_kernel, cap, chunks),
        out_shape=jax.ShapeDtypeStruct((rows, width), jnp.bfloat16),
        in_specs=[smem, smem, smem, vmem, vmem, vmem, hbm, hbm, hbm],
        out_specs=vmem,
        scratch_shapes=[
            pltpu.VMEM((depth, hidden), jnp.bfloat16),
            pltpu.VMEM((depth, hidden), jnp.bfloat16),
            pltpu.VMEM((hidden, depth), jnp.bfloat16),
            pltpu.VMEM((size * cuts, 128), jnp.float32),
            pltpu.VMEM((rows * cuts, 128), jnp.float32),
            pltpu.VMEM((rows, cuts, 128), jnp.bfloat16),
            tiled,
            tiled,
            pltpu.VMEM((size, width), jnp.bfloat16),
            tiled,
            tiled,
            pltpu.SemaphoreType.DMA((3,)),
            pltpu.SemaphoreType.DMA((count,)),
            pltpu.SemaphoreType.DMA((count,)),
            pltpu.SemaphoreType.DMA((count,)),
            pltpu.SemaphoreType.DMA((count,)),
        ],
        compiler_params=pltpu.CompilerParams(
            collective_id=1, has_side_effects=True, vmem_limit_bytes=50 << 20
        ),
        name="experts",
    )(idx, slot, mix, own, parts, gain, w_gate, w_up, w_down)


def body(
    tokens,
    input_gain,
    w_query,
    w_key,
    w_value,
    query_gain,
    key_gain,
    w_out,
    post_gain,
    expert_ids,
    route_weights,
    w_gate,
    w_up,
    w_down,
):
    tok_rows, width = tokens.shape
    head_dim = query_gain.shape[0]
    heads_here = w_query.shape[1] // head_dim
    seq_count = lax.axis_size("seq")
    seq_index = lax.axis_index("seq")
    head_count = lax.axis_size("head")
    head_index = lax.axis_index("head")
    normed = rms_scale(tokens.astype(jnp.float32), input_gain).astype(jnp.bfloat16)
    offset = seq_index * tok_rows
    positions = (offset + jnp.arange(tok_rows, dtype=jnp.int32)).astype(jnp.float32)
    queries = jnp.dot(normed, w_query, preferred_element_type=jnp.float32).reshape(
        tok_rows, heads_here, head_dim
    )
    queries = rotate(rms_scale(queries, query_gain), positions).astype(jnp.bfloat16)
    key_rows = jnp.dot(normed, w_key, preferred_element_type=jnp.float32).reshape(
        tok_rows, 1, head_dim
    )
    key_rows = (
        rotate(rms_scale(key_rows, key_gain), positions)
        .astype(jnp.bfloat16)
        .reshape(tok_rows, head_dim)
    )
    value_rows = jnp.dot(normed, w_value, preferred_element_type=jnp.float32).astype(jnp.bfloat16)
    queries = queries.transpose(2, 1, 0).reshape(head_dim, heads_here * tok_rows)
    value_t = value_rows.T.reshape(head_dim, tok_rows // head_dim, head_dim)
    value_t = value_t.transpose(1, 0, 2).reshape(tok_rows, head_dim)
    kv_block = jnp.concatenate([key_rows, value_t], axis=0)
    attended = attention(kv_block, queries, seq_count, heads_here, tok_rows, head_dim)
    rows_here = tok_rows // head_count
    own_rows = lax.dynamic_slice_in_dim(tokens, head_index * rows_here, rows_here, 0)
    products = jnp.dot(attended, w_out, preferred_element_type=jnp.float32).astype(jnp.bfloat16)
    parts = lax.all_to_all(
        cut_along(products, 0, head_count), "head", split_axis=0, concat_axis=0, tiled=True
    )
    experts_all = w_gate.shape[0] * seq_count * head_count
    top_count = expert_ids.shape[1]
    onehot = expert_ids[:, :, None] == jnp.arange(experts_all, dtype=jnp.int32)
    named = jnp.any(onehot, axis=1)
    earlier = (jnp.arange(rows_here)[:, None] > jnp.arange(rows_here)[None, :]).astype(jnp.bfloat16)
    rank = jnp.dot(earlier, named.astype(jnp.bfloat16), preferred_element_type=jnp.float32)
    rank = rank.astype(jnp.int32)
    slot = expert_ids * CAPACITY + jnp.sum(jnp.where(onehot, rank[:, None, :], 0), axis=2)
    chosen = named[:, :, None] & (rank[:, :, None] == jnp.arange(CAPACITY, dtype=jnp.int32))
    idx = jnp.sum(jnp.where(chosen, jnp.arange(rows_here, dtype=jnp.int32)[:, None, None], 0), axis=0)
    mixing = route_weights / jnp.sum(route_weights, axis=1, keepdims=True)
    return experts(
        idx.reshape(-1),
        slot.reshape(-1),
        mixing.reshape(-1),
        own_rows,
        parts,
        post_gain.reshape(1, -1),
        w_gate[0],
        w_up[0],
        w_down[0],
        CAPACITY,
    )


def solution(mesh):
    placed = (
        P("seq", None),
        P(),
        P(None, "head"),
        P(None, "head"),
        P(None, "head"),
        P(),
        P(),
        P("head", None),
        P(),
        P(("seq", "head"), None),
        P(("seq", "head"), None),
        P(("seq", "head"), None, None),
        P(("seq", "head"), None, None),
        P(("seq", "head"), None, None),
    )
    return jax.shard_map(
        body, mesh=mesh, in_specs=placed, out_specs=P(("seq", "head"), None), check_vma=False
    )
```

```python
import functools

import jax
import jax.numpy as jnp
from jax import lax
from jax.experimental import pallas as pl
from jax.experimental.pallas import tpu as pltpu
from jax.sharding import PartitionSpec as P

MESH = pl.DeviceIdType.MESH
EPSILON = 1e-06
THETA = 1000000.0
LOG2E = 1.4426950408889634
GROUP = 4
CAPACITY = 6


def attention_kernel(
    heads, rows, dim, k_ref, v_ref, q_ref, out_ref, kbuf, vbuf, m_s, l_s, acc, send_k, send_v, recv_k, recv_v
):
    i = lax.axis_index("seq")
    h = lax.axis_index("head")
    count = lax.axis_size("seq")
    plane = count // 4
    z, p = i // plane, lax.rem(i, plane)
    last = i // GROUP
    for u in range(GROUP):

        @pl.when(last * GROUP + u > i)
        def _():
            kbuf[last * GROUP + u] = jnp.zeros(kbuf.shape[1:], kbuf.dtype)
            vbuf[last * GROUP + u] = jnp.zeros(vbuf.shape[1:], vbuf.dtype)

    kbuf[i] = k_ref[...]
    vbuf[i] = v_ref[...]
    barrier = pltpu.get_barrier_semaphore()

    def greet(t, c):
        pl.semaphore_signal(
            barrier, inc=1, device_id=(lax.rem(i + t, count), h), device_id_type=MESH
        )
        return c

    lax.fori_loop(1, count, greet, 0)
    pl.semaphore_wait(barrier, count - 1)

    def copy(buf, send, recv, at, source, zt, pt):
        return pltpu.make_async_remote_copy(
            src_ref=buf.at[source],
            dst_ref=buf.at[source],
            send_sem=send.at[at],
            recv_sem=recv.at[source],
            device_id=(zt * plane + pt, h),
            device_id_type=MESH,
        )

    def k_column(zt):
        return copy(kbuf, send_k, recv_k, count + zt, i, zt, p)

    def k_plane(source, pt):
        return copy(kbuf, send_k, recv_k, source // plane * plane + pt, source, z, pt)

    def v_plane(pt):
        return copy(vbuf, send_v, recv_v, count + pt, i, z, pt)

    def v_column(source, zt):
        return copy(vbuf, send_v, recv_v, lax.rem(source, plane) * 4 + zt, source, zt, p)

    def peer(t):
        return lax.rem(p + t, plane)

    def columns(act):
        def one(zt, c):
            act(zt)
            return c

        lax.fori_loop(z + 1, 4, one, 0)

    def peers(act):
        def one(t, c):
            act(peer(t))
            return c

        lax.fori_loop(1, plane, one, 0)

    def when(cond, act):
        @pl.when(cond)
        def _():
            act()

    columns(lambda zt: k_column(zt).start())
    peers(lambda pt: when((z < 3) | (pt > p), lambda: v_plane(pt).start()))
    peers(lambda pt: when(pt > p, lambda: k_plane(i, pt).start()))
    columns(lambda zt: v_column(i, zt).start())

    def pass_k(t, c):
        source = (z - t) * plane + p
        k_plane(source, p).wait_recv()
        peers(lambda pt: k_plane(source, pt).start())
        return c

    lax.fori_loop(1, z + 1, pass_k, 0)

    def pass_v(pt):
        source = z * plane + pt
        v_column(source, z).wait_recv()
        columns(lambda zt: v_column(source, zt).start())

    peers(lambda pt: when(z < 3, lambda: pass_v(pt)))
    scale = dim ** (-0.5) * LOG2E

    def group(g, masked):
        for u in range(GROUP):
            source = g * GROUP + u
            when((source < i) & (lax.rem(source, plane) != p), lambda: k_plane(source, p).wait_recv())
            when(
                (source < i) & ((source // plane != z) | (z == 3)),
                lambda: v_column(source, z).wait_recv(),
            )
        keys = jnp.concatenate([kbuf[g * GROUP + u] for u in range(GROUP)], axis=0)
        halves = [
            vbuf[g * GROUP + u, dim * w : dim * (w + 1), :]
            for u in range(GROUP)
            for w in range(rows // dim)
        ]
        values = jnp.concatenate(halves, axis=1)
        values = jnp.concatenate([values, jnp.ones((16, values.shape[1]), values.dtype)], axis=0)
        scores = jnp.dot(keys, q_ref[...], preferred_element_type=jnp.float32)
        if masked:
            key_at = lax.broadcasted_iota(jnp.int32, scores.shape, 0)
            query_at = lax.broadcasted_iota(jnp.int32, scores.shape, 1) % rows + (i - g * GROUP) * rows
            scores = jnp.where(key_at <= query_at, scores, -1e30)
        top = jnp.max(scores, axis=0, keepdims=True)
        if not masked:
            top = jnp.maximum(top, m_s[...])
        weights = jnp.exp2(scores * scale - top * scale)
        mixed = jnp.dot(values, weights.astype(jnp.bfloat16), preferred_element_type=jnp.float32)
        if masked:
            l_s[...] = mixed[dim : dim + 1]
            acc[...] = mixed[:dim]
        else:
            shrink = jnp.exp2((m_s[...] - top) * scale)
            l_s[...] = l_s[...] * shrink + mixed[dim : dim + 1]
            acc[...] = acc[...] * shrink + mixed[:dim]
        m_s[...] = top

    group(last, True)

    def earlier(t, c):
        group(last - t, False)
        return c

    lax.fori_loop(1, last + 1, earlier, 0)
    for head in range(heads):
        columns_here = slice(head * rows, (head + 1) * rows)
        part = acc[:, columns_here] / l_s[:, columns_here]
        out_ref[:, head * dim : (head + 1) * dim] = part.T.astype(jnp.bfloat16)
    columns(lambda zt: k_column(zt).wait_send())
    peers(lambda pt: when((z < 3) | (pt > p), lambda: v_plane(pt).wait_send()))
    peers(lambda pt: when(pt > p, lambda: k_plane(i, pt).wait_send()))
    columns(lambda zt: v_column(i, zt).wait_send())

    def passed_k(t, c):
        peers(lambda pt: k_plane((z - t) * plane + p, pt).wait_send())
        return c

    lax.fori_loop(1, z + 1, passed_k, 0)
    peers(lambda pt: columns(lambda zt: v_column(z * plane + pt, zt).wait_send()))


def attention(k, v, q, seq_count, heads, rows, dim):
    return pl.pallas_call(
        functools.partial(attention_kernel, heads, rows, dim),
        out_shape=jax.ShapeDtypeStruct((rows, heads * dim), jnp.bfloat16),
        in_specs=[pl.BlockSpec(memory_space=pltpu.VMEM)] * 3,
        out_specs=pl.BlockSpec(memory_space=pltpu.VMEM),
        scratch_shapes=[
            pltpu.VMEM((seq_count,) + k.shape, jnp.bfloat16),
            pltpu.VMEM((seq_count,) + v.shape, jnp.bfloat16),
            pltpu.VMEM((1, heads * rows), jnp.float32),
            pltpu.VMEM((1, heads * rows), jnp.float32),
            pltpu.VMEM((dim, heads * rows), jnp.float32),
            pltpu.SemaphoreType.DMA((seq_count + 4,)),
            pltpu.SemaphoreType.DMA((seq_count + 8,)),
            pltpu.SemaphoreType.DMA((seq_count,)),
            pltpu.SemaphoreType.DMA((seq_count,)),
        ],
        compiler_params=pltpu.CompilerParams(
            collective_id=0, has_side_effects=True, vmem_limit_bytes=50 << 20
        ),
        name="attention",
    )(k, v, q)


def cut_along(array, dim, devices):
    dims = array.shape
    blocks = array.reshape(*dims[:dim], devices, dims[dim] // devices, *dims[dim + 1 :])
    return jnp.moveaxis(blocks, dim, 0)


def rms_scale(vectors, gain_vector):
    mean_sq = jnp.mean(vectors * vectors, axis=-1, keepdims=True)
    return vectors * lax.rsqrt(mean_sq + EPSILON) * gain_vector


def rotate(vectors, positions):
    half_dim = vectors.shape[-1] // 2
    frequency = THETA ** (-jnp.arange(half_dim, dtype=jnp.float32) * 2.0 / vectors.shape[-1])
    angles = positions[:, None] * frequency[None, :]
    cosine_table = jnp.cos(angles)[:, None, :]
    sine_table = jnp.sin(angles)[:, None, :]
    front_half = vectors[..., :half_dim]
    back_half = vectors[..., half_dim:]
    return jnp.concatenate(
        [
            front_half * cosine_table - back_half * sine_table,
            back_half * cosine_table + front_half * sine_table,
        ],
        axis=-1,
    )


def neighbour(s, h, step, sign):
    z, x, y, core = s // 8, lax.rem(s // 2, 4), lax.rem(s, 2) * 2 + h // 2, lax.rem(h, 2)
    turn = lax.rem(step * 37, 128)
    z = lax.rem(z + sign * (turn // 32) + 4, 4)
    x = lax.rem(x + sign * lax.rem(turn // 8, 4) + 4, 4)
    y = lax.rem(y + sign * lax.rem(turn // 2, 4) + 4, 4)
    core = lax.rem(core + lax.rem(turn, 2), 2)
    return z * 8 + x * 2 + y // 2, lax.rem(y, 2) * 2 + core


def expert_kernel(
    cap,
    chunks,
    idx_ref,
    slot_ref,
    mix_ref,
    own_ref,
    part_ref,
    gain_ref,
    gate_hbm,
    up_hbm,
    down_hbm,
    out_ref,
    gate,
    up,
    down,
    wide,
    home,
    tiles,
    outgoing,
    arrived,
    batch,
    results,
    returned,
    weight_sem,
    send_out,
    recv_out,
    send_back,
    recv_back,
):
    s = lax.axis_index("seq")
    h = lax.axis_index("head")
    me = s * 4 + h
    count = 128
    rows, width = own_ref.shape
    cuts = width // 128
    barrier = pltpu.get_barrier_semaphore()

    def greet(t, c):
        pl.semaphore_signal(barrier, inc=1, device_id=neighbour(s, h, t, 1), device_id_type=MESH)
        return c

    lax.fori_loop(1, count, greet, 0)
    loads = [
        pltpu.make_async_copy(hbm, vmem, weight_sem.at[n])
        for n, (hbm, vmem) in enumerate(((gate_hbm, gate), (up_hbm, up), (down_hbm, down)))
    ]
    for load in loads:
        load.start()
    residual = own_ref[...].astype(jnp.float32)
    for n in range(part_ref.shape[0]):
        residual = residual + part_ref[n].astype(jnp.float32)
    mean_sq = jnp.mean(residual * residual, axis=-1, keepdims=True)
    routed = residual * lax.rsqrt(mean_sq + EPSILON) * gain_ref[...]
    span = rows * cuts
    for c in range(cuts):
        columns = slice(c * 128, (c + 1) * 128)
        home[pl.ds(c, rows, stride=cuts), :] = residual[:, columns]
        wide[pl.ds(c, rows, stride=cuts), :] = routed[:, columns]
    tiles[...] = wide[0:span, :].astype(jnp.bfloat16).reshape(tiles.shape)
    pl.semaphore_wait(barrier, count - 1)

    def fill(t, target, ref, at):
        for c in range(cap):
            token = idx_ref[target * cap + c]
            ref[at * cap + c] = tiles[token]

    def part(ref, t):
        return ref.at[pl.ds(t * cap, cap)]

    def dispatch(t):
        return pltpu.make_async_remote_copy(
            src_ref=part(outgoing, t),
            dst_ref=part(arrived, t),
            send_sem=send_out.at[t],
            recv_sem=recv_out.at[t],
            device_id=neighbour(s, h, t, 1),
            device_id_type=MESH,
        )

    def give_back(t):
        return pltpu.make_async_remote_copy(
            src_ref=part(results, t),
            dst_ref=part(returned, me),
            send_sem=send_back.at[t],
            recv_sem=recv_back.at[me],
            device_id=neighbour(s, h, t, -1),
            device_id_type=MESH,
        )

    def come_back(t):
        ts, th = neighbour(s, h, t, 1)
        expert = ts * 4 + th
        return pltpu.make_async_remote_copy(
            src_ref=part(results, t),
            dst_ref=part(returned, expert),
            send_sem=send_back.at[t],
            recv_sem=recv_back.at[expert],
            device_id=(ts, th),
            device_id_type=MESH,
        )

    def post(t, c):
        ts, th = neighbour(s, h, t, 1)
        fill(t, ts * 4 + th, outgoing, t)
        dispatch(t).start()
        return c

    lax.fori_loop(1, count, post, 0)
    fill(0, me, arrived, 0)
    for load in loads:
        load.wait()
    each = count // chunks
    size = each * cap

    def work(k, c):
        def await_one(t, c):
            @pl.when(t > 0)
            def _():
                dispatch(t).wait_recv()

            return c

        lax.fori_loop(k * each, (k + 1) * each, await_one, 0)
        place = pl.ds(k * size, size)
        wide[...] = arrived[place].astype(jnp.float32).reshape(wide.shape)
        for c in range(cuts):
            batch[:, c * 128 : (c + 1) * 128] = wide[pl.ds(c, size, stride=cuts), :].astype(jnp.bfloat16)
        gate_proj = jnp.dot(batch[...], gate[...], preferred_element_type=jnp.float32)
        up_proj = jnp.dot(batch[...], up[...], preferred_element_type=jnp.float32)
        hidden = (gate_proj / (1.0 + jnp.exp(-gate_proj)) * up_proj).astype(jnp.bfloat16)
        result = jnp.dot(hidden, down[...], preferred_element_type=jnp.float32)
        for c in range(cuts):
            wide[pl.ds(c, size, stride=cuts), :] = result[:, c * 128 : (c + 1) * 128]
        results[place] = wide[...].astype(jnp.bfloat16).reshape(size, cuts, 128)

        def answer(t, c):
            @pl.when(t > 0)
            def _():
                give_back(t).start()

            return c

        lax.fori_loop(k * each, (k + 1) * each, answer, 0)
        return c

    lax.fori_loop(0, chunks, work, 0)
    returned[pl.ds(me * cap, cap)] = results[0:cap]

    def settle(t, c):
        come_back(t).wait_recv()
        return c

    lax.fori_loop(1, count, settle, 0)
    top = mix_ref.shape[0] // rows

    def combine(t, c):
        place = pl.ds(pl.multiple_of(t * cuts, cuts), cuts)
        total = jnp.zeros((cuts, 128), jnp.float32)
        for k in range(top):
            row = returned[slot_ref[t * top + k]]
            total = total + row.astype(jnp.float32) * mix_ref[t * top + k]
        home[place, :] = home[place, :] + total
        return c

    lax.fori_loop(0, rows, combine, 0)
    for c in range(cuts):
        out_ref[:, c * 128 : (c + 1) * 128] = home[pl.ds(c, rows, stride=cuts), :].astype(jnp.bfloat16)

    def finish(t, c):
        dispatch(t).wait_send()
        give_back(t).wait_send()
        return c

    lax.fori_loop(1, count, finish, 0)


def experts(idx, slot, mix, own, parts, gain, w_gate, w_up, w_down, cap):
    rows, width = own.shape
    depth, hidden = w_gate.shape
    cuts = width // 128
    count = 128
    chunks = 4
    size = count * cap // chunks
    smem = pl.BlockSpec(memory_space=pltpu.SMEM)
    vmem = pl.BlockSpec(memory_space=pltpu.VMEM)
    hbm = pl.BlockSpec(memory_space=pl.ANY)
    tiled = pltpu.VMEM((count * cap, cuts, 128), jnp.bfloat16)
    return pl.pallas_call(
        functools.partial(expert_kernel, cap, chunks),
        out_shape=jax.ShapeDtypeStruct((rows, width), jnp.bfloat16),
        in_specs=[smem, smem, smem, vmem, vmem, vmem, hbm, hbm, hbm],
        out_specs=vmem,
        scratch_shapes=[
            pltpu.VMEM((depth, hidden), jnp.bfloat16),
            pltpu.VMEM((depth, hidden), jnp.bfloat16),
            pltpu.VMEM((hidden, depth), jnp.bfloat16),
            pltpu.VMEM((size * cuts, 128), jnp.float32),
            pltpu.VMEM((rows * cuts, 128), jnp.float32),
            pltpu.VMEM((rows, cuts, 128), jnp.bfloat16),
            tiled,
            tiled,
            pltpu.VMEM((size, width), jnp.bfloat16),
            tiled,
            tiled,
            pltpu.SemaphoreType.DMA((3,)),
            pltpu.SemaphoreType.DMA((count,)),
            pltpu.SemaphoreType.DMA((count,)),
            pltpu.SemaphoreType.DMA((count,)),
            pltpu.SemaphoreType.DMA((count,)),
        ],
        compiler_params=pltpu.CompilerParams(
            collective_id=1, has_side_effects=True, vmem_limit_bytes=50 << 20
        ),
        name="experts",
    )(idx, slot, mix, own, parts, gain, w_gate, w_up, w_down)


def body(
    tokens,
    input_gain,
    w_query,
    w_key,
    w_value,
    query_gain,
    key_gain,
    w_out,
    post_gain,
    expert_ids,
    route_weights,
    w_gate,
    w_up,
    w_down,
):
    tok_rows, width = tokens.shape
    head_dim = query_gain.shape[0]
    heads_here = w_query.shape[1] // head_dim
    seq_count = lax.axis_size("seq")
    seq_index = lax.axis_index("seq")
    head_count = lax.axis_size("head")
    head_index = lax.axis_index("head")
    normed = rms_scale(tokens.astype(jnp.float32), input_gain).astype(jnp.bfloat16)
    offset = seq_index * tok_rows
    positions = (offset + jnp.arange(tok_rows, dtype=jnp.int32)).astype(jnp.float32)
    queries = jnp.dot(normed, w_query, preferred_element_type=jnp.float32).reshape(
        tok_rows, heads_here, head_dim
    )
    queries = rotate(rms_scale(queries, query_gain), positions).astype(jnp.bfloat16)
    key_rows = jnp.dot(normed, w_key, preferred_element_type=jnp.float32).reshape(
        tok_rows, 1, head_dim
    )
    key_rows = (
        rotate(rms_scale(key_rows, key_gain), positions)
        .astype(jnp.bfloat16)
        .reshape(tok_rows, head_dim)
    )
    value_rows = jnp.dot(normed, w_value, preferred_element_type=jnp.float32).astype(jnp.bfloat16)
    queries = queries.transpose(2, 1, 0).reshape(head_dim, heads_here * tok_rows)
    value_t = value_rows.T.reshape(head_dim, tok_rows // head_dim, head_dim)
    value_t = value_t.transpose(1, 0, 2).reshape(tok_rows, head_dim)
    attended = attention(key_rows, value_t, queries, seq_count, heads_here, tok_rows, head_dim)
    rows_here = tok_rows // head_count
    own_rows = lax.dynamic_slice_in_dim(tokens, head_index * rows_here, rows_here, 0)
    products = jnp.dot(attended, w_out, preferred_element_type=jnp.float32).astype(jnp.bfloat16)
    parts = lax.all_to_all(
        cut_along(products, 0, head_count), "head", split_axis=0, concat_axis=0, tiled=True
    )
    experts_all = w_gate.shape[0] * seq_count * head_count
    top_count = expert_ids.shape[1]
    onehot = expert_ids[:, :, None] == jnp.arange(experts_all, dtype=jnp.int32)
    named = jnp.any(onehot, axis=1)
    earlier = (jnp.arange(rows_here)[:, None] > jnp.arange(rows_here)[None, :]).astype(jnp.bfloat16)
    rank = jnp.dot(earlier, named.astype(jnp.bfloat16), preferred_element_type=jnp.float32)
    rank = rank.astype(jnp.int32)
    slot = expert_ids * CAPACITY + jnp.sum(jnp.where(onehot, rank[:, None, :], 0), axis=2)
    chosen = named[:, :, None] & (rank[:, :, None] == jnp.arange(CAPACITY, dtype=jnp.int32))
    idx = jnp.sum(jnp.where(chosen, jnp.arange(rows_here, dtype=jnp.int32)[:, None, None], 0), axis=0)
    mixing = route_weights / jnp.sum(route_weights, axis=1, keepdims=True)
    return experts(
        idx.reshape(-1),
        slot.reshape(-1),
        mixing.reshape(-1),
        own_rows,
        parts,
        post_gain.reshape(1, -1),
        w_gate[0],
        w_up[0],
        w_down[0],
        CAPACITY,
    )


def solution(mesh):
    placed = (
        P("seq", None),
        P(),
        P(None, "head"),
        P(None, "head"),
        P(None, "head"),
        P(),
        P(),
        P("head", None),
        P(),
        P(("seq", "head"), None),
        P(("seq", "head"), None),
        P(("seq", "head"), None, None),
        P(("seq", "head"), None, None),
        P(("seq", "head"), None, None),
    )
    return jax.shard_map(
        body, mesh=mesh, in_specs=placed, out_specs=P(("seq", "head"), None), check_vma=False
    )
```

```python
import functools

import jax
import jax.numpy as jnp
from jax import lax
from jax.experimental import pallas as pl
from jax.experimental.pallas import tpu as pltpu
from jax.sharding import PartitionSpec as P

MESH = pl.DeviceIdType.MESH
EPSILON = 1e-06
THETA = 1000000.0
LOG2E = 1.4426950408889634
GROUP = 4
CAPACITY = 6


def front_kernel(
    heads,
    dim,
    tok_ref,
    in_gain,
    wk_ref,
    wv_ref,
    q_gain,
    k_gain,
    cos_ref,
    sin_ref,
    wq_hbm,
    wo_hbm,
    out_ref,
    wq,
    wo,
    normed,
    q_t,
    kbuf,
    vbuf,
    m_s,
    l_s,
    acc,
    attended,
    product,
    kept,
    pair_out,
    pair_in,
    chip_out,
    chip_in,
    weight_sem,
    send_k,
    send_v,
    recv_k,
    recv_v,
    send_pair,
    recv_pair,
    send_chip,
    recv_chip,
):
    i = lax.axis_index("seq")
    h = lax.axis_index("head")
    rows, width = tok_ref.shape
    count = lax.axis_size("seq")
    plane = count // 4
    z, p = i // plane, lax.rem(i, plane)
    last = i // GROUP
    y_lo, core = h // 2, lax.rem(h, 2)
    partner = y_lo * 2 + 1 - core
    mate = (1 - y_lo) * 2 + core
    loads = [
        pltpu.make_async_copy(wq_hbm, wq, weight_sem.at[0]),
        pltpu.make_async_copy(wo_hbm, wo, weight_sem.at[1]),
    ]
    for load in loads:
        load.start()
    for u in range(GROUP):

        @pl.when(last * GROUP + u > i)
        def _():
            kbuf[last * GROUP + u] = jnp.zeros(kbuf.shape[1:], kbuf.dtype)
            vbuf[last * GROUP + u] = jnp.zeros(vbuf.shape[1:], vbuf.dtype)

    barrier = pltpu.get_barrier_semaphore()

    def greet(t, c):
        pl.semaphore_signal(
            barrier, inc=1, device_id=(lax.rem(i + t, count), h), device_id_type=MESH
        )
        return c

    lax.fori_loop(1, count, greet, 0)
    for other in (partner, mate):
        pl.semaphore_signal(barrier, inc=1, device_id=(i, other), device_id_type=MESH)

    def turned(vectors, gain):
        mean_sq = jnp.mean(vectors * vectors, axis=-1, keepdims=True)
        vectors = vectors * lax.rsqrt(mean_sq + EPSILON) * gain
        return vectors * cos_ref[...] + pltpu.roll(vectors, dim // 2, 1) * sin_ref[...]

    tokens = tok_ref[...].astype(jnp.float32)
    mean_sq = jnp.mean(tokens * tokens, axis=-1, keepdims=True)
    normed[...] = (tokens * lax.rsqrt(mean_sq + EPSILON) * in_gain[...]).astype(jnp.bfloat16)
    key = jnp.dot(normed[...], wk_ref[...], preferred_element_type=jnp.float32)
    kbuf[i] = turned(key, k_gain[...]).astype(jnp.bfloat16)
    value = jnp.dot(normed[...], wv_ref[...], preferred_element_type=jnp.float32)
    for w in range(rows // dim):
        vbuf[i, dim * w : dim * (w + 1), :] = value[dim * w : dim * (w + 1)].T.astype(jnp.bfloat16)
    pl.semaphore_wait(barrier, count + 1)

    def copy(buf, send, recv, at, source, zt, pt):
        return pltpu.make_async_remote_copy(
            src_ref=buf.at[source],
            dst_ref=buf.at[source],
            send_sem=send.at[at],
            recv_sem=recv.at[source],
            device_id=(zt * plane + pt, h),
            device_id_type=MESH,
        )

    def k_column(zt):
        return copy(kbuf, send_k, recv_k, count + zt, i, zt, p)

    def k_plane(source, pt):
        return copy(kbuf, send_k, recv_k, source // plane * plane + pt, source, z, pt)

    def v_plane(pt):
        return copy(vbuf, send_v, recv_v, count + pt, i, z, pt)

    def v_column(source, zt):
        return copy(vbuf, send_v, recv_v, lax.rem(source, plane) * 4 + zt, source, zt, p)

    def columns(act):
        def one(zt, c):
            act(zt)
            return c

        lax.fori_loop(z + 1, 4, one, 0)

    def peers(act):
        def one(t, c):
            act(lax.rem(p + t, plane))
            return c

        lax.fori_loop(1, plane, one, 0)

    def when(cond, act):
        @pl.when(cond)
        def _():
            act()

    columns(lambda zt: k_column(zt).start())
    peers(lambda pt: when((z < 3) | (pt > p), lambda: v_plane(pt).start()))
    peers(lambda pt: when(pt > p, lambda: k_plane(i, pt).start()))
    columns(lambda zt: v_column(i, zt).start())
    loads[0].wait()
    for two in range(heads // 2):
        both = jnp.dot(
            normed[...], wq[:, two * 2 * dim : (two + 1) * 2 * dim], preferred_element_type=jnp.float32
        )
        for w in range(2):
            head = two * 2 + w
            query = turned(both[:, w * dim : (w + 1) * dim], q_gain[...])
            q_t[:, head * rows : (head + 1) * rows] = query.T.astype(jnp.bfloat16)

    def pass_k(t, c):
        source = (z - t) * plane + p
        k_plane(source, p).wait_recv()
        peers(lambda pt: k_plane(source, pt).start())
        return c

    lax.fori_loop(1, z + 1, pass_k, 0)

    def pass_v(pt):
        source = z * plane + pt
        v_column(source, z).wait_recv()
        columns(lambda zt: v_column(source, zt).start())

    peers(lambda pt: when(z < 3, lambda: pass_v(pt)))
    scale = dim ** (-0.5) * LOG2E

    def group(g, masked):
        for u in range(GROUP):
            source = g * GROUP + u
            when((source < i) & (lax.rem(source, plane) != p), lambda: k_plane(source, p).wait_recv())
            when(
                (source < i) & ((source // plane != z) | (z == 3)),
                lambda: v_column(source, z).wait_recv(),
            )
        keys = jnp.concatenate([kbuf[g * GROUP + u] for u in range(GROUP)], axis=0)
        halves = [
            vbuf[g * GROUP + u, dim * w : dim * (w + 1), :]
            for u in range(GROUP)
            for w in range(rows // dim)
        ]
        values = jnp.concatenate(halves, axis=1)
        values = jnp.concatenate([values, jnp.ones((16, values.shape[1]), values.dtype)], axis=0)
        scores = jnp.dot(keys, q_t[...], preferred_element_type=jnp.float32)
        if masked:
            key_at = lax.broadcasted_iota(jnp.int32, scores.shape, 0)
            query_at = lax.broadcasted_iota(jnp.int32, scores.shape, 1) % rows + (i - g * GROUP) * rows
            scores = jnp.where(key_at <= query_at, scores, -1e30)
        top = jnp.max(scores, axis=0, keepdims=True)
        if not masked:
            top = jnp.maximum(top, m_s[...])
        weights = jnp.exp2(scores * scale - top * scale)
        mixed = jnp.dot(values, weights.astype(jnp.bfloat16), preferred_element_type=jnp.float32)
        if masked:
            l_s[...] = mixed[dim : dim + 1]
            acc[...] = mixed[:dim]
        else:
            shrink = jnp.exp2((m_s[...] - top) * scale)
            l_s[...] = l_s[...] * shrink + mixed[dim : dim + 1]
            acc[...] = acc[...] * shrink + mixed[:dim]
        m_s[...] = top

    group(last, True)

    def earlier(t, c):
        group(last - t, False)
        return c

    lax.fori_loop(1, last + 1, earlier, 0)
    for head in range(heads):
        columns_here = slice(head * rows, (head + 1) * rows)
        part = acc[:, columns_here] / l_s[:, columns_here]
        attended[:, head * dim : (head + 1) * dim] = part.T.astype(jnp.bfloat16)
    loads[1].wait()
    chunks = pair_out.shape[0]
    wide = width // chunks
    own = rows // 4

    def block(r):
        return pl.ds(pl.multiple_of(r * own, own), own)

    def to_partner(n):
        return pltpu.make_async_remote_copy(
            src_ref=pair_out.at[n],
            dst_ref=pair_in.at[n],
            send_sem=send_pair.at[n],
            recv_sem=recv_pair.at[n],
            device_id=(i, partner),
            device_id_type=MESH,
        )

    def to_mate(n):
        return pltpu.make_async_remote_copy(
            src_ref=chip_out.at[n],
            dst_ref=chip_in.at[n],
            send_sem=send_chip.at[n],
            recv_sem=recv_chip.at[n],
            device_id=(i, mate),
            device_id_type=MESH,
        )

    def sum_pair(n):
        at = slice(n * wide, (n + 1) * wide)
        to_partner(n).wait_recv()
        far = kept[pl.ds(pl.multiple_of((1 - y_lo) * own, own), own), at]
        far = far + pair_in[n, pl.ds(pl.multiple_of((1 - y_lo) * own, own), own), :].astype(jnp.float32)
        chip_out[n] = far.astype(jnp.bfloat16)
        to_mate(n).start()
        near = kept[pl.ds(pl.multiple_of(y_lo * own, own), own), at]
        near = near + pair_in[n, pl.ds(pl.multiple_of(y_lo * own, own), own), :].astype(jnp.float32)
        out_ref[:, at] = near + tok_ref[block(h), at].astype(jnp.float32)

    for n in range(chunks):
        at = slice(n * wide, (n + 1) * wide)
        product[...] = jnp.dot(attended[...], wo[:, at], preferred_element_type=jnp.float32)
        for half in range(2):
            pair_out[n, half * own : (half + 1) * own, :] = product[
                block(half * 2 + 1 - core), :
            ].astype(jnp.bfloat16)
        to_partner(n).start()
        for half in range(2):
            kept[half * own : (half + 1) * own, at] = product[block(half * 2 + core), :]
        if n > 0:
            sum_pair(n - 1)
    sum_pair(chunks - 1)
    for n in range(chunks):
        at = slice(n * wide, (n + 1) * wide)
        to_mate(n).wait_recv()
        out_ref[:, at] = out_ref[:, at] + chip_in[n].astype(jnp.float32)
    columns(lambda zt: k_column(zt).wait_send())
    peers(lambda pt: when((z < 3) | (pt > p), lambda: v_plane(pt).wait_send()))
    peers(lambda pt: when(pt > p, lambda: k_plane(i, pt).wait_send()))
    columns(lambda zt: v_column(i, zt).wait_send())

    def passed_k(t, c):
        peers(lambda pt: k_plane((z - t) * plane + p, pt).wait_send())
        return c

    lax.fori_loop(1, z + 1, passed_k, 0)
    peers(lambda pt: columns(lambda zt: v_column(z * plane + pt, zt).wait_send()))
    for n in range(chunks):
        to_partner(n).wait_send()
        to_mate(n).wait_send()


def front(tokens, in_gain, wk, wv, q_gain, k_gain, cosine, sine, wq, wo, seq_count):
    rows, width = tokens.shape
    dim = wk.shape[1]
    heads = wq.shape[1] // dim
    own = rows // 4
    chunks = 4
    wide = width // chunks
    vmem = pl.BlockSpec(memory_space=pltpu.VMEM)
    hbm = pl.BlockSpec(memory_space=pl.ANY)
    return pl.pallas_call(
        functools.partial(front_kernel, heads, dim),
        out_shape=jax.ShapeDtypeStruct((own, width), jnp.float32),
        in_specs=[vmem] * 8 + [hbm] * 2,
        out_specs=vmem,
        scratch_shapes=[
            pltpu.VMEM(wq.shape, jnp.bfloat16),
            pltpu.VMEM(wo.shape, jnp.bfloat16),
            pltpu.VMEM(tokens.shape, jnp.bfloat16),
            pltpu.VMEM((dim, heads * rows), jnp.bfloat16),
            pltpu.VMEM((seq_count, rows, dim), jnp.bfloat16),
            pltpu.VMEM((seq_count, rows, dim), jnp.bfloat16),
            pltpu.VMEM((1, heads * rows), jnp.float32),
            pltpu.VMEM((1, heads * rows), jnp.float32),
            pltpu.VMEM((dim, heads * rows), jnp.float32),
            pltpu.VMEM((rows, heads * dim), jnp.bfloat16),
            pltpu.VMEM((rows, wide), jnp.float32),
            pltpu.VMEM((2 * own, width), jnp.float32),
            pltpu.VMEM((chunks, 2 * own, wide), jnp.bfloat16),
            pltpu.VMEM((chunks, 2 * own, wide), jnp.bfloat16),
            pltpu.VMEM((chunks, own, wide), jnp.bfloat16),
            pltpu.VMEM((chunks, own, wide), jnp.bfloat16),
            pltpu.SemaphoreType.DMA((2,)),
            pltpu.SemaphoreType.DMA((seq_count + 4,)),
            pltpu.SemaphoreType.DMA((seq_count + 8,)),
            pltpu.SemaphoreType.DMA((seq_count,)),
            pltpu.SemaphoreType.DMA((seq_count,)),
            pltpu.SemaphoreType.DMA((chunks,)),
            pltpu.SemaphoreType.DMA((chunks,)),
            pltpu.SemaphoreType.DMA((chunks,)),
            pltpu.SemaphoreType.DMA((chunks,)),
        ],
        compiler_params=pltpu.CompilerParams(
            collective_id=0, has_side_effects=True, vmem_limit_bytes=50 << 20
        ),
        name="front",
    )(tokens, in_gain, wk, wv, q_gain, k_gain, cosine, sine, wq, wo)


def neighbour(s, h, step, sign):
    z, x, y, core = s // 8, lax.rem(s // 2, 4), lax.rem(s, 2) * 2 + h // 2, lax.rem(h, 2)
    turn = lax.rem(step * 37, 128)
    z = lax.rem(z + sign * (turn // 32) + 4, 4)
    x = lax.rem(x + sign * lax.rem(turn // 8, 4) + 4, 4)
    y = lax.rem(y + sign * lax.rem(turn // 2, 4) + 4, 4)
    core = lax.rem(core + lax.rem(turn, 2), 2)
    return z * 8 + x * 2 + y // 2, lax.rem(y, 2) * 2 + core


def expert_kernel(
    cap,
    chunks,
    idx_ref,
    slot_ref,
    mix_ref,
    own_ref,
    gain_ref,
    gate_hbm,
    up_hbm,
    down_hbm,
    out_ref,
    gate,
    up,
    down,
    wide,
    home,
    tiles,
    outgoing,
    arrived,
    batch,
    results,
    returned,
    weight_sem,
    send_out,
    recv_out,
    send_back,
    recv_back,
):
    s = lax.axis_index("seq")
    h = lax.axis_index("head")
    me = s * 4 + h
    count = 128
    rows, width = own_ref.shape
    cuts = width // 128
    barrier = pltpu.get_barrier_semaphore()

    def greet(t, c):
        pl.semaphore_signal(barrier, inc=1, device_id=neighbour(s, h, t, 1), device_id_type=MESH)
        return c

    lax.fori_loop(1, count, greet, 0)
    loads = [
        pltpu.make_async_copy(hbm, vmem, weight_sem.at[n])
        for n, (hbm, vmem) in enumerate(((gate_hbm, gate), (up_hbm, up), (down_hbm, down)))
    ]
    for load in loads:
        load.start()
    residual = own_ref[...]
    mean_sq = jnp.mean(residual * residual, axis=-1, keepdims=True)
    routed = residual * lax.rsqrt(mean_sq + EPSILON) * gain_ref[...]
    span = rows * cuts
    for c in range(cuts):
        columns = slice(c * 128, (c + 1) * 128)
        home[pl.ds(c, rows, stride=cuts), :] = residual[:, columns]
        wide[pl.ds(c, rows, stride=cuts), :] = routed[:, columns]
    tiles[...] = wide[0:span, :].astype(jnp.bfloat16).reshape(tiles.shape)
    pl.semaphore_wait(barrier, count - 1)

    def fill(t, target, ref, at):
        for c in range(cap):
            token = idx_ref[target * cap + c]
            ref[at * cap + c] = tiles[token]

    def part(ref, t):
        return ref.at[pl.ds(t * cap, cap)]

    def dispatch(t):
        return pltpu.make_async_remote_copy(
            src_ref=part(outgoing, t),
            dst_ref=part(arrived, t),
            send_sem=send_out.at[t],
            recv_sem=recv_out.at[t],
            device_id=neighbour(s, h, t, 1),
            device_id_type=MESH,
        )

    def give_back(t):
        return pltpu.make_async_remote_copy(
            src_ref=part(results, t),
            dst_ref=part(returned, me),
            send_sem=send_back.at[t],
            recv_sem=recv_back.at[me],
            device_id=neighbour(s, h, t, -1),
            device_id_type=MESH,
        )

    def come_back(t):
        ts, th = neighbour(s, h, t, 1)
        expert = ts * 4 + th
        return pltpu.make_async_remote_copy(
            src_ref=part(results, t),
            dst_ref=part(returned, expert),
            send_sem=send_back.at[t],
            recv_sem=recv_back.at[expert],
            device_id=(ts, th),
            device_id_type=MESH,
        )

    def post(t, c):
        ts, th = neighbour(s, h, t, 1)
        fill(t, ts * 4 + th, outgoing, t)
        dispatch(t).start()
        return c

    lax.fori_loop(1, count, post, 0)
    fill(0, me, arrived, 0)
    for load in loads:
        load.wait()
    each = count // chunks
    size = each * cap

    def work(k, c):
        def await_one(t, c):
            @pl.when(t > 0)
            def _():
                dispatch(t).wait_recv()

            return c

        lax.fori_loop(k * each, (k + 1) * each, await_one, 0)
        place = pl.ds(k * size, size)
        wide[...] = arrived[place].astype(jnp.float32).reshape(wide.shape)
        for c in range(cuts):
            batch[:, c * 128 : (c + 1) * 128] = wide[pl.ds(c, size, stride=cuts), :].astype(jnp.bfloat16)
        gate_proj = jnp.dot(batch[...], gate[...], preferred_element_type=jnp.float32)
        up_proj = jnp.dot(batch[...], up[...], preferred_element_type=jnp.float32)
        hidden = (gate_proj / (1.0 + jnp.exp(-gate_proj)) * up_proj).astype(jnp.bfloat16)
        result = jnp.dot(hidden, down[...], preferred_element_type=jnp.float32)
        for c in range(cuts):
            wide[pl.ds(c, size, stride=cuts), :] = result[:, c * 128 : (c + 1) * 128]
        results[place] = wide[...].astype(jnp.bfloat16).reshape(size, cuts, 128)

        def answer(t, c):
            @pl.when(t > 0)
            def _():
                give_back(t).start()

            return c

        lax.fori_loop(k * each, (k + 1) * each, answer, 0)
        return c

    lax.fori_loop(0, chunks, work, 0)
    returned[pl.ds(me * cap, cap)] = results[0:cap]

    def settle(t, c):
        come_back(t).wait_recv()
        return c

    lax.fori_loop(1, count, settle, 0)
    top = mix_ref.shape[0] // rows

    def combine(t, c):
        place = pl.ds(pl.multiple_of(t * cuts, cuts), cuts)
        total = jnp.zeros((cuts, 128), jnp.float32)
        for k in range(top):
            row = returned[slot_ref[t * top + k]]
            total = total + row.astype(jnp.float32) * mix_ref[t * top + k]
        home[place, :] = home[place, :] + total
        return c

    lax.fori_loop(0, rows, combine, 0)
    for c in range(cuts):
        out_ref[:, c * 128 : (c + 1) * 128] = home[pl.ds(c, rows, stride=cuts), :].astype(jnp.bfloat16)

    def finish(t, c):
        dispatch(t).wait_send()
        give_back(t).wait_send()
        return c

    lax.fori_loop(1, count, finish, 0)


def experts(idx, slot, mix, own, gain, w_gate, w_up, w_down, cap):
    rows, width = own.shape
    depth, hidden = w_gate.shape
    cuts = width // 128
    count = 128
    chunks = 4
    size = count * cap // chunks
    smem = pl.BlockSpec(memory_space=pltpu.SMEM)
    vmem = pl.BlockSpec(memory_space=pltpu.VMEM)
    hbm = pl.BlockSpec(memory_space=pl.ANY)
    tiled = pltpu.VMEM((count * cap, cuts, 128), jnp.bfloat16)
    return pl.pallas_call(
        functools.partial(expert_kernel, cap, chunks),
        out_shape=jax.ShapeDtypeStruct((rows, width), jnp.bfloat16),
        in_specs=[smem, smem, smem, vmem, vmem, hbm, hbm, hbm],
        out_specs=vmem,
        scratch_shapes=[
            pltpu.VMEM((depth, hidden), jnp.bfloat16),
            pltpu.VMEM((depth, hidden), jnp.bfloat16),
            pltpu.VMEM((hidden, depth), jnp.bfloat16),
            pltpu.VMEM((size * cuts, 128), jnp.float32),
            pltpu.VMEM((rows * cuts, 128), jnp.float32),
            pltpu.VMEM((rows, cuts, 128), jnp.bfloat16),
            tiled,
            tiled,
            pltpu.VMEM((size, width), jnp.bfloat16),
            tiled,
            tiled,
            pltpu.SemaphoreType.DMA((3,)),
            pltpu.SemaphoreType.DMA((count,)),
            pltpu.SemaphoreType.DMA((count,)),
            pltpu.SemaphoreType.DMA((count,)),
            pltpu.SemaphoreType.DMA((count,)),
        ],
        compiler_params=pltpu.CompilerParams(
            collective_id=1, has_side_effects=True, vmem_limit_bytes=50 << 20
        ),
        name="experts",
    )(idx, slot, mix, own, gain, w_gate, w_up, w_down)


def body(
    tokens,
    input_gain,
    w_query,
    w_key,
    w_value,
    query_gain,
    key_gain,
    w_out,
    post_gain,
    expert_ids,
    route_weights,
    w_gate,
    w_up,
    w_down,
):
    tok_rows = tokens.shape[0]
    head_dim = query_gain.shape[0]
    seq_count = lax.axis_size("seq")
    head_count = lax.axis_size("head")
    half_dim = head_dim // 2
    positions = (lax.axis_index("seq") * tok_rows + jnp.arange(tok_rows, dtype=jnp.int32)).astype(jnp.float32)
    frequency = THETA ** (-jnp.arange(half_dim, dtype=jnp.float32) * 2.0 / head_dim)
    angles = positions[:, None] * frequency[None, :]
    cosine, sine = jnp.cos(angles), jnp.sin(angles)
    residual = front(
        tokens,
        input_gain.reshape(1, -1),
        w_key,
        w_value,
        query_gain.reshape(1, -1),
        key_gain.reshape(1, -1),
        jnp.concatenate([cosine, cosine], axis=1),
        jnp.concatenate([-sine, sine], axis=1),
        w_query,
        w_out,
        seq_count,
    )
    rows_here = residual.shape[0]
    experts_all = w_gate.shape[0] * seq_count * head_count
    top_count = expert_ids.shape[1]
    onehot = expert_ids[:, :, None] == jnp.arange(experts_all, dtype=jnp.int32)
    named = jnp.any(onehot, axis=1)
    earlier = (jnp.arange(rows_here)[:, None] > jnp.arange(rows_here)[None, :]).astype(jnp.bfloat16)
    rank = jnp.dot(earlier, named.astype(jnp.bfloat16), preferred_element_type=jnp.float32)
    rank = rank.astype(jnp.int32)
    slot = expert_ids * CAPACITY + jnp.sum(jnp.where(onehot, rank[:, None, :], 0), axis=2)
    chosen = named[:, :, None] & (rank[:, :, None] == jnp.arange(CAPACITY, dtype=jnp.int32))
    idx = jnp.sum(jnp.where(chosen, jnp.arange(rows_here, dtype=jnp.int32)[:, None, None], 0), axis=0)
    mixing = route_weights / jnp.sum(route_weights, axis=1, keepdims=True)
    return experts(
        idx.reshape(-1),
        slot.reshape(-1),
        mixing.reshape(-1),
        residual,
        post_gain.reshape(1, -1),
        w_gate[0],
        w_up[0],
        w_down[0],
        CAPACITY,
    )


def solution(mesh):
    placed = (
        P("seq", None),
        P(),
        P(None, "head"),
        P(None, "head"),
        P(None, "head"),
        P(),
        P(),
        P("head", None),
        P(),
        P(("seq", "head"), None),
        P(("seq", "head"), None),
        P(("seq", "head"), None, None),
        P(("seq", "head"), None, None),
        P(("seq", "head"), None, None),
    )
    return jax.shard_map(
        body, mesh=mesh, in_specs=placed, out_specs=P(("seq", "head"), None), check_vma=False
    )
```

```python
import functools

import jax
import jax.numpy as jnp
from jax import lax
from jax.experimental import pallas as pl
from jax.experimental.pallas import tpu as pltpu
from jax.sharding import PartitionSpec as P

MESH = pl.DeviceIdType.MESH
EPSILON = 1e-06
THETA = 1000000.0
LOG2E = 1.4426950408889634
GROUP = 4
CAPACITY = 6


def neighbour(s, h, step):
    z, x, y, core = s // 8, lax.rem(s // 2, 4), lax.rem(s, 2) * 2 + h // 2, lax.rem(h, 2)
    turn = lax.rem(step * 37, 128)
    z = lax.rem(z + turn // 32, 4)
    x = lax.rem(x + lax.rem(turn // 8, 4), 4)
    y = lax.rem(y + lax.rem(turn // 2, 4), 4)
    core = lax.rem(core + lax.rem(turn, 2), 2)
    return z * 8 + x * 2 + y // 2, lax.rem(y, 2) * 2 + core


def layer_kernel(
    heads,
    dim,
    cap,
    in_gain,
    post_gain,
    q_gain,
    k_gain,
    cos_ref,
    sin_ref,
    ids_ref,
    score_ref,
    tok_hbm,
    wk_hbm,
    wv_hbm,
    wq_hbm,
    wo_hbm,
    gate_hbm,
    up_hbm,
    down_hbm,
    out_ref,
    tok_ref,
    wk_ref,
    wv_ref,
    wq,
    wo,
    up,
    normed,
    q_t,
    kbuf,
    vbuf,
    m_s,
    l_s,
    acc,
    attended,
    product,
    kept,
    pair_out,
    pair_in,
    chip_out,
    chip_in,
    residual,
    slot_v,
    mix_v,
    idx_v,
    slot_s,
    mix_s,
    idx_s,
    wide_rows,
    home,
    tiles,
    outgoing,
    arrived,
    batch,
    returned,
    load_sem,
    send_k,
    send_v,
    recv_k,
    recv_v,
    send_pair,
    recv_pair,
    send_chip,
    recv_chip,
    send_out,
    recv_out,
    send_back,
    recv_back,
):
    i = lax.axis_index("seq")
    h = lax.axis_index("head")
    rows, width = tok_ref.shape
    own = rows // 4
    count = lax.axis_size("seq")
    plane = count // 4
    z, p = i // plane, lax.rem(i, plane)
    last = i // GROUP
    y_lo, core = h // 2, lax.rem(h, 2)
    partner = y_lo * 2 + 1 - core
    mate = (1 - y_lo) * 2 + core
    me = i * 4 + h
    devices = count * 4
    hidden_width = up.shape[1]
    gate, down = wq.at[:, 0:hidden_width], wo.at[0:hidden_width, :]

    def load(hbm, vmem, n):
        return pltpu.make_async_copy(hbm, vmem, load_sem.at[n])

    first_loads = [
        load(tok_hbm, tok_ref, 0),
        load(wk_hbm, wk_ref, 1),
        load(wv_hbm, wv_ref, 2),
        load(wq_hbm, wq, 3),
        load(wo_hbm, wo, 4),
        load(up_hbm, up, 5),
    ]
    for one in first_loads:
        one.start()
    for u in range(GROUP):

        @pl.when(last * GROUP + u > i)
        def _():
            kbuf[last * GROUP + u] = jnp.zeros(kbuf.shape[1:], kbuf.dtype)
            vbuf[last * GROUP + u] = jnp.zeros(vbuf.shape[1:], vbuf.dtype)

    barrier = pltpu.get_barrier_semaphore()

    def greet(t, c):
        other = lax.rem(me + t, devices)
        pl.semaphore_signal(
            barrier, inc=1, device_id=(other // 4, lax.rem(other, 4)), device_id_type=MESH
        )
        return c

    lax.fori_loop(1, devices, greet, 0)

    def turned(vectors, gain):
        mean_sq = jnp.mean(vectors * vectors, axis=-1, keepdims=True)
        vectors = vectors * lax.rsqrt(mean_sq + EPSILON) * gain
        return vectors * cos_ref[...] + pltpu.roll(vectors, dim // 2, 1) * sin_ref[...]

    first_loads[0].wait()
    tokens = tok_ref[...].astype(jnp.float32)
    mean_sq = jnp.mean(tokens * tokens, axis=-1, keepdims=True)
    normed[...] = (tokens * lax.rsqrt(mean_sq + EPSILON) * in_gain[...]).astype(jnp.bfloat16)
    first_loads[1].wait()
    key = jnp.dot(normed[...], wk_ref[...], preferred_element_type=jnp.float32)
    kbuf[i] = turned(key, k_gain[...]).astype(jnp.bfloat16)
    first_loads[2].wait()
    value = jnp.dot(normed[...], wv_ref[...], preferred_element_type=jnp.float32)
    for w in range(rows // dim):
        vbuf[i, dim * w : dim * (w + 1), :] = value[dim * w : dim * (w + 1)].T.astype(jnp.bfloat16)
    pl.semaphore_wait(barrier, devices - 1)

    def copy(buf, send, recv, at, source, zt, pt):
        return pltpu.make_async_remote_copy(
            src_ref=buf.at[source],
            dst_ref=buf.at[source],
            send_sem=send.at[at],
            recv_sem=recv.at[source],
            device_id=(zt * plane + pt, h),
            device_id_type=MESH,
        )

    def k_column(zt):
        return copy(kbuf, send_k, recv_k, count + zt, i, zt, p)

    def k_plane(source, pt):
        return copy(kbuf, send_k, recv_k, source // plane * plane + pt, source, z, pt)

    def v_plane(pt):
        return copy(vbuf, send_v, recv_v, count + pt, i, z, pt)

    def v_column(source, zt):
        return copy(vbuf, send_v, recv_v, lax.rem(source, plane) * 4 + zt, source, zt, p)

    def columns(act):
        def one(zt, c):
            act(zt)
            return c

        lax.fori_loop(z + 1, 4, one, 0)

    def peers(act):
        def one(t, c):
            act(lax.rem(p + t, plane))
            return c

        lax.fori_loop(1, plane, one, 0)

    def when(cond, act):
        @pl.when(cond)
        def _():
            act()

    columns(lambda zt: k_column(zt).start())
    peers(lambda pt: when((z < 3) | (pt > p), lambda: v_plane(pt).start()))
    peers(lambda pt: when(pt > p, lambda: k_plane(i, pt).start()))
    columns(lambda zt: v_column(i, zt).start())
    first_loads[3].wait()
    for two in range(heads // 2):
        both = jnp.dot(
            normed[...], wq[:, two * 2 * dim : (two + 1) * 2 * dim], preferred_element_type=jnp.float32
        )
        for w in range(2):
            head = two * 2 + w
            query = turned(both[:, w * dim : (w + 1) * dim], q_gain[...])
            q_t[:, head * rows : (head + 1) * rows] = query.T.astype(jnp.bfloat16)

    load(gate_hbm, gate, 3).start()
    ids = ids_ref[...]
    lane = lax.broadcasted_iota(jnp.int32, (own, devices), 1)
    hits = [ids[:, n : n + 1] == lane for n in range(ids.shape[1])]
    named = sum(jnp.where(hit, 1.0, 0.0) for hit in hits)
    order = [lax.broadcasted_iota(jnp.int32, (own, own), n) for n in range(2)]
    earlier_rows = jnp.where(order[0] > order[1], 1.0, 0.0).astype(jnp.bfloat16)
    rank = jnp.dot(earlier_rows, named.astype(jnp.bfloat16), preferred_element_type=jnp.float32)
    scores_in = score_ref[...]
    mixing = scores_in / jnp.sum(scores_in, axis=1, keepdims=True)
    slots = jnp.zeros((own, devices), jnp.int32)
    mixes = jnp.zeros((own, devices), jnp.float32)
    for n, hit in enumerate(hits):
        place = jnp.sum(jnp.where(hit, rank, 0.0), axis=1, keepdims=True).astype(jnp.int32)
        slots = jnp.where(lane == n, ids[:, n : n + 1] * cap + place, slots)
        mixes = jnp.where(lane == n, mixing[:, n : n + 1], mixes)
    slot_v[...] = slots
    mix_v[...] = mixes
    idx_v[...] = jnp.zeros(idx_v.shape, jnp.int32)
    token_at = lax.broadcasted_iota(jnp.int32, (own, devices), 0).astype(jnp.float32)
    for c in range(cap):
        chosen = (rank == c) & (named > 0)
        row = jnp.sum(jnp.where(chosen, token_at, 0.0), axis=0, keepdims=True)
        idx_v[c : c + 1, :] = row.astype(jnp.int32)
    tables = [load(slot_v, slot_s, 6), load(mix_v, mix_s, 7), load(idx_v, idx_s, 8)]
    for one in tables:
        one.start()

    def pass_k(t, c):
        source = (z - t) * plane + p
        k_plane(source, p).wait_recv()
        peers(lambda pt: k_plane(source, pt).start())
        return c

    lax.fori_loop(1, z + 1, pass_k, 0)

    def pass_v(pt):
        source = z * plane + pt
        v_column(source, z).wait_recv()
        columns(lambda zt: v_column(source, zt).start())

    peers(lambda pt: when(z < 3, lambda: pass_v(pt)))
    scale = dim ** (-0.5) * LOG2E

    def group(g, masked):
        for u in range(GROUP):
            source = g * GROUP + u
            when((source < i) & (lax.rem(source, plane) != p), lambda: k_plane(source, p).wait_recv())
            when(
                (source < i) & ((source // plane != z) | (z == 3)),
                lambda: v_column(source, z).wait_recv(),
            )
        keys = jnp.concatenate([kbuf[g * GROUP + u] for u in range(GROUP)], axis=0)
        halves = [
            vbuf[g * GROUP + u, dim * w : dim * (w + 1), :]
            for u in range(GROUP)
            for w in range(rows // dim)
        ]
        values = jnp.concatenate(halves, axis=1)
        values = jnp.concatenate([values, jnp.ones((16, values.shape[1]), values.dtype)], axis=0)
        scores = jnp.dot(keys, q_t[...], preferred_element_type=jnp.float32)
        if masked:
            key_at = lax.broadcasted_iota(jnp.int32, scores.shape, 0)
            query_at = lax.broadcasted_iota(jnp.int32, scores.shape, 1) % rows + (i - g * GROUP) * rows
            scores = jnp.where(key_at <= query_at, scores, -1e30)
        top = jnp.max(scores, axis=0, keepdims=True)
        if not masked:
            top = jnp.maximum(top, m_s[...])
        weights = jnp.exp2(scores * scale - top * scale)
        mixed = jnp.dot(values, weights.astype(jnp.bfloat16), preferred_element_type=jnp.float32)
        if masked:
            l_s[...] = mixed[dim : dim + 1]
            acc[...] = mixed[:dim]
        else:
            shrink = jnp.exp2((m_s[...] - top) * scale)
            l_s[...] = l_s[...] * shrink + mixed[dim : dim + 1]
            acc[...] = acc[...] * shrink + mixed[:dim]
        m_s[...] = top

    group(last, True)

    def earlier(t, c):
        group(last - t, False)
        return c

    lax.fori_loop(1, last + 1, earlier, 0)
    for head in range(heads):
        columns_here = slice(head * rows, (head + 1) * rows)
        part = acc[:, columns_here] / l_s[:, columns_here]
        attended[:, head * dim : (head + 1) * dim] = part.T.astype(jnp.bfloat16)
    first_loads[4].wait()
    chunks = pair_out.shape[0]
    wide = width // chunks

    def block(r):
        return pl.ds(pl.multiple_of(r * own, own), own)

    def to_partner(n):
        return pltpu.make_async_remote_copy(
            src_ref=pair_out.at[n],
            dst_ref=pair_in.at[n],
            send_sem=send_pair.at[n],
            recv_sem=recv_pair.at[n],
            device_id=(i, partner),
            device_id_type=MESH,
        )

    def to_mate(n):
        return pltpu.make_async_remote_copy(
            src_ref=chip_out.at[n],
            dst_ref=chip_in.at[n],
            send_sem=send_chip.at[n],
            recv_sem=recv_chip.at[n],
            device_id=(i, mate),
            device_id_type=MESH,
        )

    def sum_pair(n):
        at = slice(n * wide, (n + 1) * wide)
        to_partner(n).wait_recv()
        far = kept[pl.ds(pl.multiple_of((1 - y_lo) * own, own), own), at]
        far = far + pair_in[n, pl.ds(pl.multiple_of((1 - y_lo) * own, own), own), :].astype(jnp.float32)
        chip_out[n] = far.astype(jnp.bfloat16)
        to_mate(n).start()
        near = kept[pl.ds(pl.multiple_of(y_lo * own, own), own), at]
        near = near + pair_in[n, pl.ds(pl.multiple_of(y_lo * own, own), own), :].astype(jnp.float32)
        residual[:, at] = near + tok_ref[block(h), at].astype(jnp.float32)

    for n in range(chunks):
        at = slice(n * wide, (n + 1) * wide)
        product[...] = jnp.dot(attended[...], wo[:, at], preferred_element_type=jnp.float32)
        for half in range(2):
            pair_out[n, half * own : (half + 1) * own, :] = product[
                block(half * 2 + 1 - core), :
            ].astype(jnp.bfloat16)
        to_partner(n).start()
        for half in range(2):
            kept[half * own : (half + 1) * own, at] = product[block(half * 2 + core), :]
        if n > 0:
            sum_pair(n - 1)
    sum_pair(chunks - 1)
    for n in range(chunks):
        at = slice(n * wide, (n + 1) * wide)
        to_mate(n).wait_recv()
        residual[:, at] = residual[:, at] + chip_in[n].astype(jnp.float32)
    load(down_hbm, down, 4).start()
    cuts = width // 128
    mean_sq = jnp.mean(residual[...] * residual[...], axis=-1, keepdims=True)
    scale_rows = lax.rsqrt(mean_sq + EPSILON)
    for c in range(cuts):
        at = slice(c * 128, (c + 1) * 128)
        home[pl.ds(c, own, stride=cuts), :] = residual[:, at]
        wide_rows[pl.ds(c, own, stride=cuts), :] = residual[:, at] * scale_rows * post_gain[:, at]
    tiles[...] = wide_rows[0 : own * cuts, :].astype(jnp.bfloat16).reshape(tiles.shape)
    for one in tables:
        one.wait()

    def fill(target, ref, at):
        for c in range(cap):
            ref[at * cap + c] = tiles[jnp.clip(idx_s[c, target], 0, own - 1)]

    def part(ref, t):
        return ref.at[pl.ds(t * cap, cap)]

    def dispatch(t):
        return pltpu.make_async_remote_copy(
            src_ref=part(outgoing, t),
            dst_ref=part(arrived, me),
            send_sem=send_out.at[t],
            recv_sem=recv_out.at[me],
            device_id=neighbour(i, h, t),
            device_id_type=MESH,
        )

    def between(source):
        return pltpu.make_async_remote_copy(
            src_ref=part(arrived, source),
            dst_ref=part(arrived, source),
            send_sem=send_back.at[source],
            recv_sem=recv_out.at[source],
            device_id=(source // 4, lax.rem(source, 4)),
            device_id_type=MESH,
        )

    def give_back(source):
        return pltpu.make_async_remote_copy(
            src_ref=part(arrived, source),
            dst_ref=part(returned, me),
            send_sem=send_back.at[source],
            recv_sem=recv_back.at[me],
            device_id=(source // 4, lax.rem(source, 4)),
            device_id_type=MESH,
        )

    def come_back(expert):
        return pltpu.make_async_remote_copy(
            src_ref=part(arrived, expert),
            dst_ref=part(returned, expert),
            send_sem=send_back.at[expert],
            recv_sem=recv_back.at[expert],
            device_id=(expert // 4, lax.rem(expert, 4)),
            device_id_type=MESH,
        )

    def post(t, c):
        ts, th = neighbour(i, h, t)
        fill(ts * 4 + th, outgoing, t)
        dispatch(t).start()
        return c

    lax.fori_loop(1, devices, post, 0)
    fill(me, arrived, me)
    first_loads[5].wait()
    load(gate_hbm, gate, 3).wait()
    load(down_hbm, down, 4).wait()
    size = batch.shape[0]
    each = size // cap

    def work(k, c):
        def await_one(t, c):
            source = k * each + t
            when(source != me, lambda: between(source).wait_recv())
            return c

        lax.fori_loop(0, each, await_one, 0)
        place = pl.ds(k * size, size)
        wide_rows[...] = arrived[place].astype(jnp.float32).reshape(wide_rows.shape)
        for c in range(cuts):
            batch[:, c * 128 : (c + 1) * 128] = wide_rows[pl.ds(c, size, stride=cuts), :].astype(
                jnp.bfloat16
            )
        gate_proj = jnp.dot(batch[...], gate[...], preferred_element_type=jnp.float32)
        up_proj = jnp.dot(batch[...], up[...], preferred_element_type=jnp.float32)
        hidden = (gate_proj / (1.0 + jnp.exp(-gate_proj)) * up_proj).astype(jnp.bfloat16)
        result = jnp.dot(hidden, down[...], preferred_element_type=jnp.float32)
        for c in range(cuts):
            wide_rows[pl.ds(c, size, stride=cuts), :] = result[:, c * 128 : (c + 1) * 128]
        arrived[place] = wide_rows[...].astype(jnp.bfloat16).reshape(size, cuts, 128)

        def answer(t, c):
            source = k * each + lax.rem(t * 13 + me, each)
            when(source != me, lambda: give_back(source).start())
            return c

        lax.fori_loop(0, each, answer, 0)
        return c

    lax.fori_loop(0, devices // each, work, 0)
    returned[pl.ds(me * cap, cap)] = arrived[pl.ds(me * cap, cap)]

    def settle(expert, c):
        when(expert != me, lambda: come_back(expert).wait_recv())
        return c

    lax.fori_loop(0, devices, settle, 0)

    def combine(t, c):
        place = pl.ds(pl.multiple_of(t * cuts, cuts), cuts)
        total = jnp.zeros((cuts, 128), jnp.float32)
        for n in range(ids_ref.shape[1]):
            total = total + returned[jnp.clip(slot_s[t, n], 0, devices * cap - 1)].astype(jnp.float32) * mix_s[t, n]
        home[place, :] = home[place, :] + total
        return c

    lax.fori_loop(0, own, combine, 0)
    for c in range(cuts):
        out_ref[:, c * 128 : (c + 1) * 128] = home[pl.ds(c, own, stride=cuts), :].astype(jnp.bfloat16)

    columns(lambda zt: k_column(zt).wait_send())
    peers(lambda pt: when((z < 3) | (pt > p), lambda: v_plane(pt).wait_send()))
    peers(lambda pt: when(pt > p, lambda: k_plane(i, pt).wait_send()))
    columns(lambda zt: v_column(i, zt).wait_send())

    def passed_k(t, c):
        peers(lambda pt: k_plane((z - t) * plane + p, pt).wait_send())
        return c

    lax.fori_loop(1, z + 1, passed_k, 0)
    peers(lambda pt: columns(lambda zt: v_column(z * plane + pt, zt).wait_send()))
    for n in range(chunks):
        to_partner(n).wait_send()
        to_mate(n).wait_send()

    def finish(t, c):
        dispatch(t).wait_send()
        return c

    lax.fori_loop(1, devices, finish, 0)

    def finish_back(source, c):
        when(source != me, lambda: give_back(source).wait_send())
        return c

    lax.fori_loop(0, devices, finish_back, 0)


def layer(small, large, seq_count, cap):
    tokens, wk, wv, wq, wo, gate, up, down = large
    rows, width = tokens.shape
    dim = wk.shape[1]
    heads = wq.shape[1] // dim
    own = rows // 4
    devices = seq_count * 4
    chunks = 4
    wide = width // chunks
    cuts = width // 128
    size = devices * cap // 4
    bf16, f32 = jnp.bfloat16, jnp.float32
    vmem = pl.BlockSpec(memory_space=pltpu.VMEM)
    hbm = pl.BlockSpec(memory_space=pl.ANY)
    dma = pltpu.SemaphoreType.DMA
    return pl.pallas_call(
        functools.partial(layer_kernel, heads, dim, cap),
        out_shape=jax.ShapeDtypeStruct((own, width), bf16),
        in_specs=[vmem] * len(small) + [hbm] * len(large),
        out_specs=vmem,
        scratch_shapes=[
            pltpu.VMEM(tokens.shape, bf16),
            pltpu.VMEM(wk.shape, bf16),
            pltpu.VMEM(wv.shape, bf16),
            pltpu.VMEM(wq.shape, bf16),
            pltpu.VMEM(wo.shape, bf16),
            pltpu.VMEM(up.shape, bf16),
            pltpu.VMEM(tokens.shape, bf16),
            pltpu.VMEM((dim, heads * rows), bf16),
            pltpu.VMEM((seq_count, rows, dim), bf16),
            pltpu.VMEM((seq_count, rows, dim), bf16),
            pltpu.VMEM((1, heads * rows), f32),
            pltpu.VMEM((1, heads * rows), f32),
            pltpu.VMEM((dim, heads * rows), f32),
            pltpu.VMEM((rows, heads * dim), bf16),
            pltpu.VMEM((rows, wide), f32),
            pltpu.VMEM((2 * own, width), f32),
            pltpu.VMEM((chunks, 2 * own, wide), bf16),
            pltpu.VMEM((chunks, 2 * own, wide), bf16),
            pltpu.VMEM((chunks, own, wide), bf16),
            pltpu.VMEM((chunks, own, wide), bf16),
            pltpu.VMEM((own, width), f32),
            pltpu.VMEM((own, devices), jnp.int32),
            pltpu.VMEM((own, devices), f32),
            pltpu.VMEM((8, devices), jnp.int32),
            pltpu.SMEM((own, devices), jnp.int32),
            pltpu.SMEM((own, devices), f32),
            pltpu.SMEM((8, devices), jnp.int32),
            pltpu.VMEM((size * cuts, 128), f32),
            pltpu.VMEM((own * cuts, 128), f32),
            pltpu.VMEM((own, cuts, 128), bf16),
            pltpu.VMEM((devices * cap, cuts, 128), bf16),
            pltpu.VMEM((devices * cap, cuts, 128), bf16),
            pltpu.VMEM((size, width), bf16),
            pltpu.VMEM((devices * cap, cuts, 128), bf16),
            dma((9,)),
            dma((seq_count + 4,)),
            dma((seq_count + 8,)),
            dma((seq_count,)),
            dma((seq_count,)),
            dma((chunks,)),
            dma((chunks,)),
            dma((chunks,)),
            dma((chunks,)),
            dma((devices,)),
            dma((devices,)),
            dma((devices,)),
            dma((devices,)),
        ],
        compiler_params=pltpu.CompilerParams(
            collective_id=0, has_side_effects=True, vmem_limit_bytes=60 << 20
        ),
        name="layer",
    )(*small, *large)


def body(
    tokens,
    input_gain,
    w_query,
    w_key,
    w_value,
    query_gain,
    key_gain,
    w_out,
    post_gain,
    expert_ids,
    route_weights,
    w_gate,
    w_up,
    w_down,
):
    tok_rows = tokens.shape[0]
    head_dim = query_gain.shape[0]
    seq_count = lax.axis_size("seq")
    half_dim = head_dim // 2
    positions = (lax.axis_index("seq") * tok_rows + jnp.arange(tok_rows, dtype=jnp.int32)).astype(jnp.float32)
    frequency = THETA ** (-jnp.arange(half_dim, dtype=jnp.float32) * 2.0 / head_dim)
    angles = positions[:, None] * frequency[None, :]
    cosine, sine = jnp.cos(angles), jnp.sin(angles)
    small = (
        input_gain.reshape(1, -1),
        post_gain.reshape(1, -1),
        query_gain.reshape(1, -1),
        key_gain.reshape(1, -1),
        jnp.concatenate([cosine, cosine], axis=1),
        jnp.concatenate([-sine, sine], axis=1),
        expert_ids,
        route_weights,
    )
    large = (tokens, w_key, w_value, w_query, w_out, w_gate[0], w_up[0], w_down[0])
    return layer(small, large, seq_count, CAPACITY)


def solution(mesh):
    placed = (
        P("seq", None),
        P(),
        P(None, "head"),
        P(None, "head"),
        P(None, "head"),
        P(),
        P(),
        P("head", None),
        P(),
        P(("seq", "head"), None),
        P(("seq", "head"), None),
        P(("seq", "head"), None, None),
        P(("seq", "head"), None, None),
        P(("seq", "head"), None, None),
    )
    return jax.shard_map(
        body, mesh=mesh, in_specs=placed, out_specs=P(("seq", "head"), None), check_vma=False
    )
```

```python
import functools

import jax
import jax.numpy as jnp
from jax import lax
from jax.experimental import pallas as pl
from jax.experimental.pallas import tpu as pltpu
from jax.sharding import PartitionSpec as P

MESH = pl.DeviceIdType.MESH
EPSILON = 1e-06
THETA = 1000000.0
LOG2E = 1.4426950408889634
GROUP = 4
CAPACITY = 6


def neighbour(s, h, step, sign):
    z, x, y, core = s // 8, lax.rem(s // 2, 4), lax.rem(s, 2) * 2 + h // 2, lax.rem(h, 2)
    turn = lax.rem(step * 37, 128)
    z = lax.rem(z + sign * (turn // 32) + 4, 4)
    x = lax.rem(x + sign * lax.rem(turn // 8, 4) + 4, 4)
    y = lax.rem(y + sign * lax.rem(turn // 2, 4) + 4, 4)
    core = lax.rem(core + lax.rem(turn, 2), 2)
    return z * 8 + x * 2 + y // 2, lax.rem(y, 2) * 2 + core


def layer_kernel(
    heads,
    dim,
    cap,
    in_gain,
    post_gain,
    q_gain,
    k_gain,
    cos_ref,
    sin_ref,
    ids_ref,
    score_ref,
    tok_hbm,
    wk_hbm,
    wv_hbm,
    wq_hbm,
    wo_hbm,
    gate_hbm,
    up_hbm,
    down_hbm,
    out_ref,
    tok_ref,
    wk_ref,
    wv_ref,
    wq,
    wo,
    up,
    normed,
    q_t,
    kbuf,
    vbuf,
    m_s,
    l_s,
    acc,
    attended,
    product,
    kept,
    pair_out,
    pair_in,
    chip_out,
    chip_in,
    residual,
    slot_v,
    mix_v,
    idx_v,
    slot_s,
    mix_s,
    idx_s,
    wide_rows,
    home,
    tiles,
    outgoing,
    arrived,
    batch,
    returned,
    load_sem,
    send_k,
    send_v,
    recv_k,
    recv_v,
    send_pair,
    recv_pair,
    send_chip,
    recv_chip,
    send_out,
    recv_out,
    send_back,
    recv_back,
    gate_sem,
):
    i = lax.axis_index("seq")
    h = lax.axis_index("head")
    rows, width = tok_ref.shape
    own = rows // 4
    count = lax.axis_size("seq")
    plane = count // 4
    z, p = i // plane, lax.rem(i, plane)
    last = i // GROUP
    y_lo, core = h // 2, lax.rem(h, 2)
    partner = y_lo * 2 + 1 - core
    mate = (1 - y_lo) * 2 + core
    me = i * 4 + h
    devices = count * 4
    hidden_width = up.shape[1]
    gate, down = wq.at[:, 0:hidden_width], wo.at[0:hidden_width, :]

    def load(hbm, vmem, n):
        return pltpu.make_async_copy(hbm, vmem, load_sem.at[n])

    first_loads = [
        load(tok_hbm, tok_ref, 0),
        load(wk_hbm, wk_ref, 1),
        load(wv_hbm, wv_ref, 2),
        load(wq_hbm, wq, 3),
        load(wo_hbm, wo, 4),
        load(up_hbm, up, 5),
    ]
    for one in first_loads:
        one.start()
    for u in range(GROUP):

        @pl.when(last * GROUP + u > i)
        def _():
            kbuf[last * GROUP + u] = jnp.zeros(kbuf.shape[1:], kbuf.dtype)
            vbuf[last * GROUP + u] = jnp.zeros(vbuf.shape[1:], vbuf.dtype)

    barrier = pltpu.get_barrier_semaphore()

    def greet(t, c):
        other = lax.rem(me + t, devices)
        pl.semaphore_signal(
            barrier, inc=1, device_id=(other // 4, lax.rem(other, 4)), device_id_type=MESH
        )
        return c

    lax.fori_loop(1, devices, greet, 0)

    def turned(vectors, gain):
        mean_sq = jnp.mean(vectors * vectors, axis=-1, keepdims=True)
        vectors = vectors * lax.rsqrt(mean_sq + EPSILON) * gain
        return vectors * cos_ref[...] + pltpu.roll(vectors, dim // 2, 1) * sin_ref[...]

    first_loads[0].wait()
    tokens = tok_ref[...].astype(jnp.float32)
    mean_sq = jnp.mean(tokens * tokens, axis=-1, keepdims=True)
    normed[...] = (tokens * lax.rsqrt(mean_sq + EPSILON) * in_gain[...]).astype(jnp.bfloat16)
    first_loads[1].wait()
    key = jnp.dot(normed[...], wk_ref[...], preferred_element_type=jnp.float32)
    kbuf[i] = turned(key, k_gain[...]).astype(jnp.bfloat16)
    first_loads[2].wait()
    value = jnp.dot(normed[...], wv_ref[...], preferred_element_type=jnp.float32)
    for w in range(rows // dim):
        vbuf[i, dim * w : dim * (w + 1), :] = value[dim * w : dim * (w + 1)].T.astype(jnp.bfloat16)
    pl.semaphore_wait(barrier, devices - 1)

    def copy(buf, send, recv, at, source, zt, pt):
        return pltpu.make_async_remote_copy(
            src_ref=buf.at[source],
            dst_ref=buf.at[source],
            send_sem=send.at[at],
            recv_sem=recv.at[source],
            device_id=(zt * plane + pt, h),
            device_id_type=MESH,
        )

    def k_column(zt):
        return copy(kbuf, send_k, recv_k, count + zt, i, zt, p)

    def k_plane(source, pt):
        return copy(kbuf, send_k, recv_k, source // plane * plane + pt, source, z, pt)

    def v_plane(pt):
        return copy(vbuf, send_v, recv_v, count + pt, i, z, pt)

    def v_column(source, zt):
        return copy(vbuf, send_v, recv_v, lax.rem(source, plane) * 4 + zt, source, zt, p)

    def columns(act):
        def one(zt, c):
            act(zt)
            return c

        lax.fori_loop(z + 1, 4, one, 0)

    def peers(act):
        def one(t, c):
            act(lax.rem(p + t, plane))
            return c

        lax.fori_loop(1, plane, one, 0)

    def when(cond, act):
        @pl.when(cond)
        def _():
            act()

    columns(lambda zt: k_column(zt).start())
    peers(lambda pt: when((z < 3) | (pt > p), lambda: v_plane(pt).start()))
    peers(lambda pt: when(pt > p, lambda: k_plane(i, pt).start()))
    columns(lambda zt: v_column(i, zt).start())
    first_loads[3].wait()
    for two in range(heads // 2):
        both = jnp.dot(
            normed[...], wq[:, two * 2 * dim : (two + 1) * 2 * dim], preferred_element_type=jnp.float32
        )
        for w in range(2):
            head = two * 2 + w
            query = turned(both[:, w * dim : (w + 1) * dim], q_gain[...])
            q_t[:, head * rows : (head + 1) * rows] = query.T.astype(jnp.bfloat16)

    load(gate_hbm, gate, 3).start()
    ids = ids_ref[...].astype(jnp.float32).T.astype(jnp.int32)
    lane = lax.broadcasted_iota(jnp.int32, (own, devices), 1)
    hits = [ids[:, n : n + 1] == lane for n in range(ids.shape[1])]
    named = sum(jnp.where(hit, 1.0, 0.0) for hit in hits)
    order = [lax.broadcasted_iota(jnp.int32, (own, own), n) for n in range(2)]
    earlier_rows = jnp.where(order[0] > order[1], 1.0, 0.0).astype(jnp.bfloat16)
    rank = jnp.dot(earlier_rows, named.astype(jnp.bfloat16), preferred_element_type=jnp.float32)
    scores_in = score_ref[...].T
    mixing = scores_in / jnp.sum(scores_in, axis=1, keepdims=True)
    slots = jnp.zeros((own, devices), jnp.int32)
    mixes = jnp.zeros((own, devices), jnp.float32)
    for n, hit in enumerate(hits):
        place = jnp.sum(jnp.where(hit, rank, 0.0), axis=1, keepdims=True).astype(jnp.int32)
        slots = jnp.where(lane == n, ids[:, n : n + 1] * cap + place, slots)
        mixes = jnp.where(lane == n, mixing[:, n : n + 1], mixes)
    slot_v[...] = slots
    mix_v[...] = mixes
    idx_v[...] = jnp.zeros(idx_v.shape, jnp.int32)
    token_at = lax.broadcasted_iota(jnp.int32, (own, devices), 0).astype(jnp.float32)
    for c in range(cap):
        chosen = (rank == c) & (named > 0)
        row = jnp.sum(jnp.where(chosen, token_at, 0.0), axis=0, keepdims=True)
        idx_v[c : c + 1, :] = row.astype(jnp.int32)
    tables = [load(slot_v, slot_s, 6), load(mix_v, mix_s, 7), load(idx_v, idx_s, 8)]
    for one in tables:
        one.start()

    def pass_k(t, c):
        source = (z - t) * plane + p
        k_plane(source, p).wait_recv()
        peers(lambda pt: k_plane(source, pt).start())
        return c

    lax.fori_loop(1, z + 1, pass_k, 0)

    def pass_v(pt):
        source = z * plane + pt
        v_column(source, z).wait_recv()
        columns(lambda zt: v_column(source, zt).start())

    peers(lambda pt: when(z < 3, lambda: pass_v(pt)))
    scale = dim ** (-0.5) * LOG2E

    def arrive(g):
        for u in range(GROUP):
            source = g * GROUP + u
            when((source < i) & (lax.rem(source, plane) != p), lambda: k_plane(source, p).wait_recv())
            when(
                (source < i) & ((source // plane != z) | (z == 3)),
                lambda: v_column(source, z).wait_recv(),
            )

    def group(g, masked):
        keys = jnp.concatenate([kbuf[g * GROUP + u] for u in range(GROUP)], axis=0)
        halves = [
            vbuf[g * GROUP + u, dim * w : dim * (w + 1), :]
            for u in range(GROUP)
            for w in range(rows // dim)
        ]
        values = jnp.concatenate(halves, axis=1)
        values = jnp.concatenate([values, jnp.ones((16, values.shape[1]), values.dtype)], axis=0)
        scores = jnp.dot(keys, q_t[...], preferred_element_type=jnp.float32)
        if masked:
            key_at = lax.broadcasted_iota(jnp.int32, scores.shape, 0)
            query_at = lax.broadcasted_iota(jnp.int32, scores.shape, 1) % rows + (i - g * GROUP) * rows
            scores = jnp.where(key_at <= query_at, scores, -1e30)
        top = jnp.max(scores, axis=0, keepdims=True)
        if not masked:
            top = jnp.maximum(top, m_s[...])
        weights = jnp.exp2(scores * scale - top * scale)
        mixed = jnp.dot(values, weights.astype(jnp.bfloat16), preferred_element_type=jnp.float32)
        if masked:
            l_s[...] = mixed[dim : dim + 1]
            acc[...] = mixed[:dim]
        else:
            shrink = jnp.exp2((m_s[...] - top) * scale)
            l_s[...] = l_s[...] * shrink + mixed[dim : dim + 1]
            acc[...] = acc[...] * shrink + mixed[:dim]
        m_s[...] = top

    def open_gate():
        def tell(t, c):
            other = lax.rem(me + t, devices)
            pl.semaphore_signal(
                gate_sem, inc=1, device_id=(other // 4, lax.rem(other, 4)), device_id_type=MESH
            )
            return c

        lax.fori_loop(1, devices, tell, 0)

    arrive(last)
    group(last, True)

    def earlier(t, c):
        arrive(last - t)
        group(last - t, False)
        return c

    lax.fori_loop(1, last + 1, earlier, 0)
    for head in range(heads):
        columns_here = slice(head * rows, (head + 1) * rows)
        part = acc[:, columns_here] / l_s[:, columns_here]
        attended[:, head * dim : (head + 1) * dim] = part.T.astype(jnp.bfloat16)
    first_loads[4].wait()
    chunks = pair_out.shape[0]
    wide = width // chunks

    def block(r):
        return pl.ds(pl.multiple_of(r * own, own), own)

    def to_partner(n):
        return pltpu.make_async_remote_copy(
            src_ref=pair_out.at[n],
            dst_ref=pair_in.at[n],
            send_sem=send_pair.at[n],
            recv_sem=recv_pair.at[n],
            device_id=(i, partner),
            device_id_type=MESH,
        )

    def to_mate(n):
        return pltpu.make_async_remote_copy(
            src_ref=chip_out.at[n],
            dst_ref=chip_in.at[n],
            send_sem=send_chip.at[n],
            recv_sem=recv_chip.at[n],
            device_id=(i, mate),
            device_id_type=MESH,
        )

    def sum_pair(n):
        at = slice(n * wide, (n + 1) * wide)
        to_partner(n).wait_recv()
        far = kept[pl.ds(pl.multiple_of((1 - y_lo) * own, own), own), at]
        far = far + pair_in[n, pl.ds(pl.multiple_of((1 - y_lo) * own, own), own), :].astype(jnp.float32)
        chip_out[n] = far.astype(jnp.bfloat16)
        to_mate(n).start()
        near = kept[pl.ds(pl.multiple_of(y_lo * own, own), own), at]
        near = near + pair_in[n, pl.ds(pl.multiple_of(y_lo * own, own), own), :].astype(jnp.float32)
        residual[:, at] = near + tok_ref[block(h), at].astype(jnp.float32)

    for n in range(chunks):
        at = slice(n * wide, (n + 1) * wide)
        product[...] = jnp.dot(attended[...], wo[:, at], preferred_element_type=jnp.float32)
        for half in range(2):
            pair_out[n, half * own : (half + 1) * own, :] = product[
                block(half * 2 + 1 - core), :
            ].astype(jnp.bfloat16)
        to_partner(n).start()
        for half in range(2):
            kept[half * own : (half + 1) * own, at] = product[block(half * 2 + core), :]
        if n > 0:
            sum_pair(n - 1)
    sum_pair(chunks - 1)
    for n in range(chunks):
        at = slice(n * wide, (n + 1) * wide)
        to_mate(n).wait_recv()
        residual[:, at] = residual[:, at] + chip_in[n].astype(jnp.float32)
    load(down_hbm, down, 4).start()
    cuts = width // 128
    mean_sq = jnp.mean(residual[...] * residual[...], axis=-1, keepdims=True)
    scale_rows = lax.rsqrt(mean_sq + EPSILON)
    for c in range(cuts):
        at = slice(c * 128, (c + 1) * 128)
        home[pl.ds(c, own, stride=cuts), :] = residual[:, at]
        wide_rows[pl.ds(c, own, stride=cuts), :] = residual[:, at] * scale_rows * post_gain[:, at]
    tiles[...] = wide_rows[0 : own * cuts, :].astype(jnp.bfloat16).reshape(tiles.shape)
    for one in tables:
        one.wait()

    def fill(target, ref, at):
        for c in range(cap):
            ref[at * cap + c] = tiles[jnp.clip(idx_s[c, target], 0, own - 1)]

    def part(ref, t):
        return ref.at[pl.ds(t * cap, cap)]

    def dispatch(t):
        return pltpu.make_async_remote_copy(
            src_ref=part(outgoing, t),
            dst_ref=part(arrived, t),
            send_sem=send_out.at[t],
            recv_sem=recv_out.at[t],
            device_id=neighbour(i, h, t, 1),
            device_id_type=MESH,
        )

    def give_back(t):
        return pltpu.make_async_remote_copy(
            src_ref=part(arrived, t),
            dst_ref=part(returned, me),
            send_sem=send_back.at[t],
            recv_sem=recv_back.at[me],
            device_id=neighbour(i, h, t, -1),
            device_id_type=MESH,
        )

    def come_back(expert):
        return pltpu.make_async_remote_copy(
            src_ref=part(arrived, expert),
            dst_ref=part(returned, expert),
            send_sem=send_back.at[expert],
            recv_sem=recv_back.at[expert],
            device_id=(expert // 4, lax.rem(expert, 4)),
            device_id_type=MESH,
        )

    def post(t, c):
        ts, th = neighbour(i, h, t, 1)
        fill(ts * 4 + th, outgoing, t)
        dispatch(t).start()
        return c

    when(z == 3, open_gate)
    pl.semaphore_wait(gate_sem, jnp.where(z == 3, devices // 4 - 1, devices // 4))
    lax.fori_loop(1, devices, post, 0)
    fill(me, arrived, 0)
    first_loads[5].wait()
    load(gate_hbm, gate, 3).wait()
    load(down_hbm, down, 4).wait()
    size = batch.shape[0]
    each = size // cap

    def work(k, c):
        def await_one(t, c):
            step = k * each + t
            when(step > 0, lambda: dispatch(step).wait_recv())
            return c

        lax.fori_loop(0, each, await_one, 0)
        place = pl.ds(k * size, size)
        wide_rows[...] = arrived[place].astype(jnp.float32).reshape(wide_rows.shape)
        for c in range(cuts):
            batch[:, c * 128 : (c + 1) * 128] = wide_rows[pl.ds(c, size, stride=cuts), :].astype(
                jnp.bfloat16
            )
        gate_proj = jnp.dot(batch[...], gate[...], preferred_element_type=jnp.float32)
        up_proj = jnp.dot(batch[...], up[...], preferred_element_type=jnp.float32)
        hidden = (gate_proj / (1.0 + jnp.exp(-gate_proj)) * up_proj).astype(jnp.bfloat16)
        result = jnp.dot(hidden, down[...], preferred_element_type=jnp.float32)
        for c in range(cuts):
            wide_rows[pl.ds(c, size, stride=cuts), :] = result[:, c * 128 : (c + 1) * 128]
        arrived[place] = wide_rows[...].astype(jnp.bfloat16).reshape(size, cuts, 128)

        def answer(t, c):
            step = k * each + t
            when(step > 0, lambda: give_back(step).start())
            return c

        lax.fori_loop(0, each, answer, 0)
        return c

    lax.fori_loop(0, devices // each, work, 0)
    returned[pl.ds(me * cap, cap)] = arrived[0:cap]

    def settle(expert, c):
        when(expert != me, lambda: come_back(expert).wait_recv())
        return c

    lax.fori_loop(0, devices, settle, 0)

    def combine(t, c):
        place = pl.ds(pl.multiple_of(t * cuts, cuts), cuts)
        total = jnp.zeros((cuts, 128), jnp.float32)
        for n in range(ids_ref.shape[0]):
            total = total + returned[jnp.clip(slot_s[t, n], 0, devices * cap - 1)].astype(jnp.float32) * mix_s[t, n]
        home[place, :] = home[place, :] + total
        return c

    lax.fori_loop(0, own, combine, 0)
    for c in range(cuts):
        out_ref[:, c * 128 : (c + 1) * 128] = home[pl.ds(c, own, stride=cuts), :].astype(jnp.bfloat16)

    columns(lambda zt: k_column(zt).wait_send())
    peers(lambda pt: when((z < 3) | (pt > p), lambda: v_plane(pt).wait_send()))
    peers(lambda pt: when(pt > p, lambda: k_plane(i, pt).wait_send()))
    columns(lambda zt: v_column(i, zt).wait_send())

    def passed_k(t, c):
        peers(lambda pt: k_plane((z - t) * plane + p, pt).wait_send())
        return c

    lax.fori_loop(1, z + 1, passed_k, 0)
    peers(lambda pt: columns(lambda zt: v_column(z * plane + pt, zt).wait_send()))
    for n in range(chunks):
        to_partner(n).wait_send()
        to_mate(n).wait_send()

    def finish(t, c):
        dispatch(t).wait_send()
        give_back(t).wait_send()
        return c

    lax.fori_loop(1, devices, finish, 0)


def layer(small, large, seq_count, cap):
    tokens, wk, wv, wq, wo, gate, up, down = large
    rows, width = tokens.shape
    dim = wk.shape[1]
    heads = wq.shape[1] // dim
    own = rows // 4
    devices = seq_count * 4
    chunks = 4
    wide = width // chunks
    cuts = width // 128
    size = devices * cap // 4
    bf16, f32 = jnp.bfloat16, jnp.float32
    vmem = pl.BlockSpec(memory_space=pltpu.VMEM)
    hbm = pl.BlockSpec(memory_space=pl.ANY)
    dma = pltpu.SemaphoreType.DMA
    return pl.pallas_call(
        functools.partial(layer_kernel, heads, dim, cap),
        out_shape=jax.ShapeDtypeStruct((own, width), bf16),
        in_specs=[vmem] * len(small) + [hbm] * len(large),
        out_specs=vmem,
        scratch_shapes=[
            pltpu.VMEM(tokens.shape, bf16),
            pltpu.VMEM(wk.shape, bf16),
            pltpu.VMEM(wv.shape, bf16),
            pltpu.VMEM(wq.shape, bf16),
            pltpu.VMEM(wo.shape, bf16),
            pltpu.VMEM(up.shape, bf16),
            pltpu.VMEM(tokens.shape, bf16),
            pltpu.VMEM((dim, heads * rows), bf16),
            pltpu.VMEM((seq_count, rows, dim), bf16),
            pltpu.VMEM((seq_count, rows, dim), bf16),
            pltpu.VMEM((1, heads * rows), f32),
            pltpu.VMEM((1, heads * rows), f32),
            pltpu.VMEM((dim, heads * rows), f32),
            pltpu.VMEM((rows, heads * dim), bf16),
            pltpu.VMEM((rows, wide), f32),
            pltpu.VMEM((2 * own, width), f32),
            pltpu.VMEM((chunks, 2 * own, wide), bf16),
            pltpu.VMEM((chunks, 2 * own, wide), bf16),
            pltpu.VMEM((chunks, own, wide), bf16),
            pltpu.VMEM((chunks, own, wide), bf16),
            pltpu.VMEM((own, width), f32),
            pltpu.VMEM((own, devices), jnp.int32),
            pltpu.VMEM((own, devices), f32),
            pltpu.VMEM((8, devices), jnp.int32),
            pltpu.SMEM((own, devices), jnp.int32),
            pltpu.SMEM((own, devices), f32),
            pltpu.SMEM((8, devices), jnp.int32),
            pltpu.VMEM((size * cuts, 128), f32),
            pltpu.VMEM((own * cuts, 128), f32),
            pltpu.VMEM((own, cuts, 128), bf16),
            pltpu.VMEM((devices * cap, cuts, 128), bf16),
            pltpu.VMEM((devices * cap, cuts, 128), bf16),
            pltpu.VMEM((size, width), bf16),
            pltpu.VMEM((devices * cap, cuts, 128), bf16),
            dma((9,)),
            dma((seq_count + 4,)),
            dma((seq_count + 8,)),
            dma((seq_count,)),
            dma((seq_count,)),
            dma((chunks,)),
            dma((chunks,)),
            dma((chunks,)),
            dma((chunks,)),
            dma((devices,)),
            dma((devices,)),
            dma((devices,)),
            dma((devices,)),
            pltpu.SemaphoreType.REGULAR,
        ],
        compiler_params=pltpu.CompilerParams(
            collective_id=0, has_side_effects=True, vmem_limit_bytes=50 << 20
        ),
        name="layer",
    )(*small, *large)


def body(
    tokens,
    input_gain,
    w_query,
    w_key,
    w_value,
    query_gain,
    key_gain,
    w_out,
    post_gain,
    expert_ids,
    route_weights,
    w_gate,
    w_up,
    w_down,
):
    tok_rows = tokens.shape[0]
    head_dim = query_gain.shape[0]
    seq_count = lax.axis_size("seq")
    half_dim = head_dim // 2
    positions = (lax.axis_index("seq") * tok_rows + jnp.arange(tok_rows, dtype=jnp.int32)).astype(jnp.float32)
    frequency = THETA ** (-jnp.arange(half_dim, dtype=jnp.float32) * 2.0 / head_dim)
    angles = positions[:, None] * frequency[None, :]
    cosine, sine = jnp.cos(angles), jnp.sin(angles)
    small = (
        input_gain.reshape(1, -1),
        post_gain.reshape(1, -1),
        query_gain.reshape(1, -1),
        key_gain.reshape(1, -1),
        jnp.concatenate([cosine, cosine], axis=1),
        jnp.concatenate([-sine, sine], axis=1),
        expert_ids.T,
        route_weights.T,
    )
    large = (tokens, w_key, w_value, w_query, w_out, w_gate[0], w_up[0], w_down[0])
    return layer(small, large, seq_count, CAPACITY)


def solution(mesh):
    placed = (
        P("seq", None),
        P(),
        P(None, "head"),
        P(None, "head"),
        P(None, "head"),
        P(),
        P(),
        P("head", None),
        P(),
        P(("seq", "head"), None),
        P(("seq", "head"), None),
        P(("seq", "head"), None, None),
        P(("seq", "head"), None, None),
        P(("seq", "head"), None, None),
    )
    return jax.shard_map(
        body, mesh=mesh, in_specs=placed, out_specs=P(("seq", "head"), None), check_vma=False
    )
```

```python
import functools

import jax
import jax.numpy as jnp
from jax import lax
from jax.experimental import pallas as pl
from jax.experimental.pallas import tpu as pltpu
from jax.sharding import PartitionSpec as P

MESH = pl.DeviceIdType.MESH
EPSILON = 1e-06
THETA = 1000000.0
LOG2E = 1.4426950408889634
GROUP = 4
CAPACITY = 6


def neighbour(s, h, step, sign):
    z, x, y, core = s // 8, lax.rem(s // 2, 4), lax.rem(s, 2) * 2 + h // 2, lax.rem(h, 2)
    turn = lax.rem(step * 37, 128)
    z = lax.rem(z + sign * (turn // 32) + 4, 4)
    x = lax.rem(x + sign * lax.rem(turn // 8, 4) + 4, 4)
    y = lax.rem(y + sign * lax.rem(turn // 2, 4) + 4, 4)
    core = lax.rem(core + lax.rem(turn, 2), 2)
    return z * 8 + x * 2 + y // 2, lax.rem(y, 2) * 2 + core


def layer_kernel(
    heads,
    dim,
    cap,
    in_gain,
    post_gain,
    q_gain,
    k_gain,
    cos_ref,
    sin_ref,
    ids_ref,
    score_ref,
    tok_hbm,
    wk_hbm,
    wv_hbm,
    wq_hbm,
    wo_hbm,
    gate_hbm,
    up_hbm,
    down_hbm,
    out_ref,
    tok_ref,
    wk_ref,
    wv_ref,
    wq,
    wo,
    up,
    normed,
    q_t,
    kbuf,
    vbuf,
    m_s,
    l_s,
    acc,
    attended,
    product,
    kept,
    pair_out,
    pair_in,
    chip_out,
    chip_in,
    residual,
    slot_v,
    mix_v,
    idx_v,
    slot_s,
    mix_s,
    idx_s,
    wide_rows,
    home,
    tiles,
    outgoing,
    arrived,
    batch,
    returned,
    load_sem,
    send_k,
    send_v,
    recv_k,
    recv_v,
    send_pair,
    recv_pair,
    send_chip,
    recv_chip,
    send_out,
    recv_out,
    send_back,
    recv_back,
    gate_sem,
):
    i = lax.axis_index("seq")
    h = lax.axis_index("head")
    rows, width = tok_ref.shape
    own = rows // 4
    count = lax.axis_size("seq")
    plane = count // 4
    z, p = i // plane, lax.rem(i, plane)
    last = i // GROUP
    y_lo, core = h // 2, lax.rem(h, 2)
    partner = y_lo * 2 + 1 - core
    mate = (1 - y_lo) * 2 + core
    me = i * 4 + h
    devices = count * 4
    hidden_width = up.shape[1]
    gate, down = wq.at[:, 0:hidden_width], wo.at[0:hidden_width, :]

    def load(hbm, vmem, n):
        return pltpu.make_async_copy(hbm, vmem, load_sem.at[n])

    first_loads = [
        load(tok_hbm, tok_ref, 0),
        load(wk_hbm, wk_ref, 1),
        load(wv_hbm, wv_ref, 2),
        load(wq_hbm, wq, 3),
        load(wo_hbm, wo, 4),
        load(up_hbm, up, 5),
    ]
    for one in first_loads:
        one.start()
    for u in range(GROUP):

        @pl.when(last * GROUP + u > i)
        def _():
            kbuf[last * GROUP + u] = jnp.zeros(kbuf.shape[1:], kbuf.dtype)
            vbuf[last * GROUP + u] = jnp.zeros(vbuf.shape[1:], vbuf.dtype)

    barrier = pltpu.get_barrier_semaphore()

    def greet(t, c):
        other = lax.rem(me + t, devices)
        pl.semaphore_signal(
            barrier, inc=1, device_id=(other // 4, lax.rem(other, 4)), device_id_type=MESH
        )
        return c

    lax.fori_loop(1, devices, greet, 0)

    def turned(vectors, gain):
        mean_sq = jnp.mean(vectors * vectors, axis=-1, keepdims=True)
        vectors = vectors * lax.rsqrt(mean_sq + EPSILON) * gain
        return vectors * cos_ref[...] + pltpu.roll(vectors, dim // 2, 1) * sin_ref[...]

    first_loads[0].wait()
    tokens = tok_ref[...].astype(jnp.float32)
    mean_sq = jnp.mean(tokens * tokens, axis=-1, keepdims=True)
    normed[...] = (tokens * lax.rsqrt(mean_sq + EPSILON) * in_gain[...]).astype(jnp.bfloat16)
    first_loads[1].wait()
    key = jnp.dot(normed[...], wk_ref[...], preferred_element_type=jnp.float32)
    kbuf[i] = turned(key, k_gain[...]).astype(jnp.bfloat16)
    first_loads[2].wait()
    value = jnp.dot(normed[...], wv_ref[...], preferred_element_type=jnp.float32)
    for w in range(rows // dim):
        vbuf[i, dim * w : dim * (w + 1), :] = value[dim * w : dim * (w + 1)].T.astype(jnp.bfloat16)
    pl.semaphore_wait(barrier, devices - 1)

    def copy(buf, send, recv, at, source, zt, pt):
        return pltpu.make_async_remote_copy(
            src_ref=buf.at[source],
            dst_ref=buf.at[source],
            send_sem=send.at[at],
            recv_sem=recv.at[source],
            device_id=(zt * plane + pt, h),
            device_id_type=MESH,
        )

    def k_column(zt):
        return copy(kbuf, send_k, recv_k, count + zt, i, zt, p)

    def k_plane(source, pt):
        return copy(kbuf, send_k, recv_k, source // plane * plane + pt, source, z, pt)

    def v_plane(pt):
        return copy(vbuf, send_v, recv_v, count + pt, i, z, pt)

    def v_column(source, zt):
        return copy(vbuf, send_v, recv_v, lax.rem(source, plane) * 4 + zt, source, zt, p)

    def columns(act):
        def one(zt, c):
            act(zt)
            return c

        lax.fori_loop(z + 1, 4, one, 0)

    def peers(act):
        def one(t, c):
            act(lax.rem(p + t, plane))
            return c

        lax.fori_loop(1, plane, one, 0)

    def when(cond, act):
        @pl.when(cond)
        def _():
            act()

    columns(lambda zt: k_column(zt).start())
    peers(lambda pt: when((z < 3) | (pt > p), lambda: v_plane(pt).start()))
    peers(lambda pt: when(pt > p, lambda: k_plane(i, pt).start()))
    columns(lambda zt: v_column(i, zt).start())
    first_loads[3].wait()
    for two in range(heads // 2):
        both = jnp.dot(
            normed[...], wq[:, two * 2 * dim : (two + 1) * 2 * dim], preferred_element_type=jnp.float32
        )
        for w in range(2):
            head = two * 2 + w
            query = turned(both[:, w * dim : (w + 1) * dim], q_gain[...])
            q_t[:, head * rows : (head + 1) * rows] = query.T.astype(jnp.bfloat16)

    load(gate_hbm, gate, 3).start()
    ids = ids_ref[...].astype(jnp.float32).T.astype(jnp.int32)
    lane = lax.broadcasted_iota(jnp.int32, (own, devices), 1)
    hits = [ids[:, n : n + 1] == lane for n in range(ids.shape[1])]
    named = sum(jnp.where(hit, 1.0, 0.0) for hit in hits)
    order = [lax.broadcasted_iota(jnp.int32, (own, own), n) for n in range(2)]
    earlier_rows = jnp.where(order[0] > order[1], 1.0, 0.0).astype(jnp.bfloat16)
    rank = jnp.dot(earlier_rows, named.astype(jnp.bfloat16), preferred_element_type=jnp.float32)
    scores_in = score_ref[...].T
    mixing = scores_in / jnp.sum(scores_in, axis=1, keepdims=True)
    slots = jnp.zeros((own, devices), jnp.int32)
    mixes = jnp.zeros((own, devices), jnp.float32)
    for n, hit in enumerate(hits):
        place = jnp.sum(jnp.where(hit, rank, 0.0), axis=1, keepdims=True).astype(jnp.int32)
        slots = jnp.where(lane == n, ids[:, n : n + 1] * cap + place, slots)
        mixes = jnp.where(lane == n, mixing[:, n : n + 1], mixes)
    slot_v[...] = slots
    mix_v[...] = mixes
    idx_v[...] = jnp.zeros(idx_v.shape, jnp.int32)
    token_at = lax.broadcasted_iota(jnp.int32, (own, devices), 0).astype(jnp.float32)
    for c in range(cap):
        chosen = (rank == c) & (named > 0)
        row = jnp.sum(jnp.where(chosen, token_at, 0.0), axis=0, keepdims=True)
        idx_v[c : c + 1, :] = row.astype(jnp.int32)
    tables = [load(slot_v, slot_s, 6), load(mix_v, mix_s, 7), load(idx_v, idx_s, 8)]
    for one in tables:
        one.start()

    def pass_k(t, c):
        source = (z - t) * plane + p
        k_plane(source, p).wait_recv()
        peers(lambda pt: k_plane(source, pt).start())
        return c

    lax.fori_loop(1, z + 1, pass_k, 0)

    def pass_v(zt):
        def one(pt):
            source = z * plane + pt
            when(zt == z + 1, lambda: v_column(source, z).wait_recv())
            v_column(source, zt).start()

        peers(one)

    columns(pass_v)
    scale = dim ** (-0.5) * LOG2E

    def arrive(g):
        for u in range(GROUP):
            source = g * GROUP + u
            when((source < i) & (lax.rem(source, plane) != p), lambda: k_plane(source, p).wait_recv())
            when(
                (source < i) & ((source // plane != z) | (z == 3)),
                lambda: v_column(source, z).wait_recv(),
            )

    def group(g, masked):
        keys = jnp.concatenate([kbuf[g * GROUP + u] for u in range(GROUP)], axis=0)
        halves = [
            vbuf[g * GROUP + u, dim * w : dim * (w + 1), :]
            for u in range(GROUP)
            for w in range(rows // dim)
        ]
        values = jnp.concatenate(halves, axis=1)
        values = jnp.concatenate([values, jnp.ones((16, values.shape[1]), values.dtype)], axis=0)
        scores = jnp.dot(keys, q_t[...], preferred_element_type=jnp.float32)
        if masked:
            key_at = lax.broadcasted_iota(jnp.int32, scores.shape, 0)
            query_at = lax.broadcasted_iota(jnp.int32, scores.shape, 1) % rows + (i - g * GROUP) * rows
            scores = jnp.where(key_at <= query_at, scores, -1e30)
        top = jnp.max(scores, axis=0, keepdims=True)
        if not masked:
            top = jnp.maximum(top, m_s[...])
        weights = jnp.exp2(scores * scale - top * scale)
        mixed = jnp.dot(values, weights.astype(jnp.bfloat16), preferred_element_type=jnp.float32)
        if masked:
            l_s[...] = mixed[dim : dim + 1]
            acc[...] = mixed[:dim]
        else:
            shrink = jnp.exp2((m_s[...] - top) * scale)
            l_s[...] = l_s[...] * shrink + mixed[dim : dim + 1]
            acc[...] = acc[...] * shrink + mixed[:dim]
        m_s[...] = top

    def open_gate():
        def tell(t, c):
            other = lax.rem(me + t, devices)
            pl.semaphore_signal(
                gate_sem, inc=1, device_id=(other // 4, lax.rem(other, 4)), device_id_type=MESH
            )
            return c

        lax.fori_loop(1, devices, tell, 0)

    arrive(last)
    group(last, True)

    def earlier(t, c):
        arrive(last - t)
        group(last - t, False)
        return c

    lax.fori_loop(1, last + 1, earlier, 0)
    for head in range(heads):
        columns_here = slice(head * rows, (head + 1) * rows)
        part = acc[:, columns_here] / l_s[:, columns_here]
        attended[:, head * dim : (head + 1) * dim] = part.T.astype(jnp.bfloat16)
    first_loads[4].wait()
    chunks = pair_out.shape[0]
    wide = width // chunks

    def block(r):
        return pl.ds(pl.multiple_of(r * own, own), own)

    def to_partner(n):
        return pltpu.make_async_remote_copy(
            src_ref=pair_out.at[n],
            dst_ref=pair_in.at[n],
            send_sem=send_pair.at[n],
            recv_sem=recv_pair.at[n],
            device_id=(i, partner),
            device_id_type=MESH,
        )

    def to_mate(n):
        return pltpu.make_async_remote_copy(
            src_ref=chip_out.at[n],
            dst_ref=chip_in.at[n],
            send_sem=send_chip.at[n],
            recv_sem=recv_chip.at[n],
            device_id=(i, mate),
            device_id_type=MESH,
        )

    def sum_pair(n):
        at = slice(n * wide, (n + 1) * wide)
        to_partner(n).wait_recv()
        far = kept[pl.ds(pl.multiple_of((1 - y_lo) * own, own), own), at]
        far = far + pair_in[n, pl.ds(pl.multiple_of((1 - y_lo) * own, own), own), :].astype(jnp.float32)
        chip_out[n] = far.astype(jnp.bfloat16)
        to_mate(n).start()
        near = kept[pl.ds(pl.multiple_of(y_lo * own, own), own), at]
        near = near + pair_in[n, pl.ds(pl.multiple_of(y_lo * own, own), own), :].astype(jnp.float32)
        residual[:, at] = near + tok_ref[block(h), at].astype(jnp.float32)

    for n in range(chunks):
        at = slice(n * wide, (n + 1) * wide)
        product[...] = jnp.dot(attended[...], wo[:, at], preferred_element_type=jnp.float32)
        for half in range(2):
            pair_out[n, half * own : (half + 1) * own, :] = product[
                block(half * 2 + 1 - core), :
            ].astype(jnp.bfloat16)
        to_partner(n).start()
        for half in range(2):
            kept[half * own : (half + 1) * own, at] = product[block(half * 2 + core), :]
        if n > 0:
            sum_pair(n - 1)
    sum_pair(chunks - 1)
    for n in range(chunks):
        at = slice(n * wide, (n + 1) * wide)
        to_mate(n).wait_recv()
        residual[:, at] = residual[:, at] + chip_in[n].astype(jnp.float32)
    load(down_hbm, down, 4).start()
    cuts = width // 128
    mean_sq = jnp.mean(residual[...] * residual[...], axis=-1, keepdims=True)
    scale_rows = lax.rsqrt(mean_sq + EPSILON)
    for c in range(cuts):
        at = slice(c * 128, (c + 1) * 128)
        home[pl.ds(c, own, stride=cuts), :] = residual[:, at]
        wide_rows[pl.ds(c, own, stride=cuts), :] = residual[:, at] * scale_rows * post_gain[:, at]
    tiles[...] = wide_rows[0 : own * cuts, :].astype(jnp.bfloat16).reshape(tiles.shape)
    for one in tables:
        one.wait()

    def fill(target, ref, at):
        for c in range(cap):
            ref[at * cap + c] = tiles[jnp.clip(idx_s[c, target], 0, own - 1)]

    def part(ref, t):
        return ref.at[pl.ds(t * cap, cap)]

    def dispatch(t):
        return pltpu.make_async_remote_copy(
            src_ref=part(outgoing, t),
            dst_ref=part(arrived, t),
            send_sem=send_out.at[t],
            recv_sem=recv_out.at[t],
            device_id=neighbour(i, h, t, 1),
            device_id_type=MESH,
        )

    def give_back(t):
        return pltpu.make_async_remote_copy(
            src_ref=part(arrived, t),
            dst_ref=part(returned, me),
            send_sem=send_back.at[t],
            recv_sem=recv_back.at[me],
            device_id=neighbour(i, h, t, -1),
            device_id_type=MESH,
        )

    def come_back(expert):
        return pltpu.make_async_remote_copy(
            src_ref=part(arrived, expert),
            dst_ref=part(returned, expert),
            send_sem=send_back.at[expert],
            recv_sem=recv_back.at[expert],
            device_id=(expert // 4, lax.rem(expert, 4)),
            device_id_type=MESH,
        )

    def post(t, c):
        ts, th = neighbour(i, h, t, 1)
        fill(ts * 4 + th, outgoing, t)
        dispatch(t).start()
        return c

    when(z == 3, open_gate)
    pl.semaphore_wait(gate_sem, jnp.where(z == 3, devices // 4 - 1, devices // 4))
    lax.fori_loop(1, devices, post, 0)
    fill(me, arrived, 0)
    first_loads[5].wait()
    load(gate_hbm, gate, 3).wait()
    load(down_hbm, down, 4).wait()
    size = batch.shape[0]
    each = size // cap

    def work(k, c):
        def await_one(t, c):
            step = k * each + t
            when(step > 0, lambda: dispatch(step).wait_recv())
            return c

        lax.fori_loop(0, each, await_one, 0)
        place = pl.ds(k * size, size)
        wide_rows[...] = arrived[place].astype(jnp.float32).reshape(wide_rows.shape)
        for c in range(cuts):
            batch[:, c * 128 : (c + 1) * 128] = wide_rows[pl.ds(c, size, stride=cuts), :].astype(
                jnp.bfloat16
            )
        gate_proj = jnp.dot(batch[...], gate[...], preferred_element_type=jnp.float32)
        up_proj = jnp.dot(batch[...], up[...], preferred_element_type=jnp.float32)
        hidden = (gate_proj / (1.0 + jnp.exp(-gate_proj)) * up_proj).astype(jnp.bfloat16)
        result = jnp.dot(hidden, down[...], preferred_element_type=jnp.float32)
        for c in range(cuts):
            wide_rows[pl.ds(c, size, stride=cuts), :] = result[:, c * 128 : (c + 1) * 128]
        arrived[place] = wide_rows[...].astype(jnp.bfloat16).reshape(size, cuts, 128)

        def answer(t, c):
            step = k * each + t
            when(step > 0, lambda: give_back(step).start())
            return c

        lax.fori_loop(0, each, answer, 0)
        return c

    lax.fori_loop(0, devices // each, work, 0)
    returned[pl.ds(me * cap, cap)] = arrived[0:cap]

    def settle(expert, c):
        when(expert != me, lambda: come_back(expert).wait_recv())
        return c

    lax.fori_loop(0, devices, settle, 0)

    def combine(t, c):
        place = pl.ds(pl.multiple_of(t * cuts, cuts), cuts)
        total = jnp.zeros((cuts, 128), jnp.float32)
        for n in range(ids_ref.shape[0]):
            total = total + returned[jnp.clip(slot_s[t, n], 0, devices * cap - 1)].astype(jnp.float32) * mix_s[t, n]
        home[place, :] = home[place, :] + total
        return c

    lax.fori_loop(0, own, combine, 0)
    for c in range(cuts):
        out_ref[:, c * 128 : (c + 1) * 128] = home[pl.ds(c, own, stride=cuts), :].astype(jnp.bfloat16)

    columns(lambda zt: k_column(zt).wait_send())
    peers(lambda pt: when((z < 3) | (pt > p), lambda: v_plane(pt).wait_send()))
    peers(lambda pt: when(pt > p, lambda: k_plane(i, pt).wait_send()))
    columns(lambda zt: v_column(i, zt).wait_send())

    def passed_k(t, c):
        peers(lambda pt: k_plane((z - t) * plane + p, pt).wait_send())
        return c

    lax.fori_loop(1, z + 1, passed_k, 0)
    peers(lambda pt: columns(lambda zt: v_column(z * plane + pt, zt).wait_send()))
    for n in range(chunks):
        to_partner(n).wait_send()
        to_mate(n).wait_send()

    def finish(t, c):
        dispatch(t).wait_send()
        give_back(t).wait_send()
        return c

    lax.fori_loop(1, devices, finish, 0)


def layer(small, large, seq_count, cap):
    tokens, wk, wv, wq, wo, gate, up, down = large
    rows, width = tokens.shape
    dim = wk.shape[1]
    heads = wq.shape[1] // dim
    own = rows // 4
    devices = seq_count * 4
    chunks = 4
    wide = width // chunks
    cuts = width // 128
    size = devices * cap // 4
    bf16, f32 = jnp.bfloat16, jnp.float32
    vmem = pl.BlockSpec(memory_space=pltpu.VMEM)
    hbm = pl.BlockSpec(memory_space=pltpu.HBM)
    dma = pltpu.SemaphoreType.DMA
    return pl.pallas_call(
        functools.partial(layer_kernel, heads, dim, cap),
        out_shape=jax.ShapeDtypeStruct((own, width), bf16),
        in_specs=[vmem] * len(small) + [hbm] * len(large),
        out_specs=vmem,
        scratch_shapes=[
            pltpu.VMEM(tokens.shape, bf16),
            pltpu.VMEM(wk.shape, bf16),
            pltpu.VMEM(wv.shape, bf16),
            pltpu.VMEM(wq.shape, bf16),
            pltpu.VMEM(wo.shape, bf16),
            pltpu.VMEM(up.shape, bf16),
            pltpu.VMEM(tokens.shape, bf16),
            pltpu.VMEM((dim, heads * rows), bf16),
            pltpu.VMEM((seq_count, rows, dim), bf16),
            pltpu.VMEM((seq_count, rows, dim), bf16),
            pltpu.VMEM((1, heads * rows), f32),
            pltpu.VMEM((1, heads * rows), f32),
            pltpu.VMEM((dim, heads * rows), f32),
            pltpu.VMEM((rows, heads * dim), bf16),
            pltpu.VMEM((rows, wide), f32),
            pltpu.VMEM((2 * own, width), f32),
            pltpu.VMEM((chunks, 2 * own, wide), bf16),
            pltpu.VMEM((chunks, 2 * own, wide), bf16),
            pltpu.VMEM((chunks, own, wide), bf16),
            pltpu.VMEM((chunks, own, wide), bf16),
            pltpu.VMEM((own, width), f32),
            pltpu.VMEM((own, devices), jnp.int32),
            pltpu.VMEM((own, devices), f32),
            pltpu.VMEM((8, devices), jnp.int32),
            pltpu.SMEM((own, devices), jnp.int32),
            pltpu.SMEM((own, devices), f32),
            pltpu.SMEM((8, devices), jnp.int32),
            pltpu.VMEM((size * cuts, 128), f32),
            pltpu.VMEM((own * cuts, 128), f32),
            pltpu.VMEM((own, cuts, 128), bf16),
            pltpu.VMEM((devices * cap, cuts, 128), bf16),
            pltpu.VMEM((devices * cap, cuts, 128), bf16),
            pltpu.VMEM((size, width), bf16),
            pltpu.VMEM((devices * cap, cuts, 128), bf16),
            dma((9,)),
            dma((seq_count + 4,)),
            dma((seq_count + 8,)),
            dma((seq_count,)),
            dma((seq_count,)),
            dma((chunks,)),
            dma((chunks,)),
            dma((chunks,)),
            dma((chunks,)),
            dma((devices,)),
            dma((devices,)),
            dma((devices,)),
            dma((devices,)),
            pltpu.SemaphoreType.REGULAR,
        ],
        compiler_params=pltpu.CompilerParams(
            collective_id=0, has_side_effects=True, vmem_limit_bytes=60 << 20
        ),
        name="layer",
    )(*small, *large)


def body(
    tokens,
    input_gain,
    w_query,
    w_key,
    w_value,
    query_gain,
    key_gain,
    w_out,
    post_gain,
    expert_ids,
    route_weights,
    w_gate,
    w_up,
    w_down,
):
    tok_rows = tokens.shape[0]
    head_dim = query_gain.shape[0]
    seq_count = lax.axis_size("seq")
    half_dim = head_dim // 2
    positions = (lax.axis_index("seq") * tok_rows + jnp.arange(tok_rows, dtype=jnp.int32)).astype(jnp.float32)
    frequency = THETA ** (-jnp.arange(half_dim, dtype=jnp.float32) * 2.0 / head_dim)
    angles = positions[:, None] * frequency[None, :]
    cosine, sine = jnp.cos(angles), jnp.sin(angles)
    small = (
        input_gain.reshape(1, -1),
        post_gain.reshape(1, -1),
        query_gain.reshape(1, -1),
        key_gain.reshape(1, -1),
        jnp.concatenate([cosine, cosine], axis=1),
        jnp.concatenate([-sine, sine], axis=1),
        expert_ids.T,
        route_weights.T,
    )
    large = (tokens, w_key, w_value, w_query, w_out, w_gate[0], w_up[0], w_down[0])
    return layer(small, large, seq_count, CAPACITY)


def solution(mesh):
    placed = (
        P("seq", None),
        P(),
        P(None, "head"),
        P(None, "head"),
        P(None, "head"),
        P(),
        P(),
        P("head", None),
        P(),
        P(("seq", "head"), None),
        P(("seq", "head"), None),
        P(("seq", "head"), None, None),
        P(("seq", "head"), None, None),
        P(("seq", "head"), None, None),
    )
    return jax.shard_map(
        body, mesh=mesh, in_specs=placed, out_specs=P(("seq", "head"), None), check_vma=False
    )
```

```python
import functools

import jax
import jax.numpy as jnp
from jax import lax
from jax.experimental import pallas as pl
from jax.experimental.pallas import tpu as pltpu
from jax.sharding import PartitionSpec as P

MESH = pl.DeviceIdType.MESH
EPSILON = 1e-06
THETA = 1000000.0
LOG2E = 1.4426950408889634
GROUP = 4
CAPACITY = 6


def neighbour(s, h, step, sign):
    z, x, y, core = s // 8, lax.rem(s // 2, 4), lax.rem(s, 2) * 2 + h // 2, lax.rem(h, 2)
    turn = lax.rem(step * 37, 128)
    z = lax.rem(z + sign * (turn // 32) + 4, 4)
    x = lax.rem(x + sign * lax.rem(turn // 8, 4) + 4, 4)
    y = lax.rem(y + sign * lax.rem(turn // 2, 4) + 4, 4)
    core = lax.rem(core + lax.rem(turn, 2), 2)
    return z * 8 + x * 2 + y // 2, lax.rem(y, 2) * 2 + core


def layer_kernel(
    heads,
    dim,
    cap,
    cos_ref,
    sin_ref,
    in_gain_hbm,
    post_gain_hbm,
    q_gain_hbm,
    k_gain_hbm,
    ids_hbm,
    score_hbm,
    tok_hbm,
    wk_hbm,
    wv_hbm,
    wq_hbm,
    wo_hbm,
    gate_hbm,
    up_hbm,
    down_hbm,
    out_ref,
    in_gain,
    post_gain,
    q_gain,
    k_gain,
    ids_ref,
    score_ref,
    tok_ref,
    wk_ref,
    wv_ref,
    wq,
    wo,
    up,
    normed,
    q_t,
    kbuf,
    vbuf,
    m_s,
    l_s,
    acc,
    attended,
    product,
    kept,
    pair_out,
    pair_in,
    chip_out,
    chip_in,
    residual,
    slot_v,
    mix_v,
    idx_v,
    slot_s,
    mix_s,
    idx_s,
    wide_rows,
    home,
    tiles,
    outgoing,
    arrived,
    batch,
    returned,
    load_sem,
    send_k,
    send_v,
    recv_k,
    recv_v,
    send_pair,
    recv_pair,
    send_chip,
    recv_chip,
    send_out,
    recv_out,
    send_back,
    recv_back,
    gate_sem,
):
    i = lax.axis_index("seq")
    h = lax.axis_index("head")
    rows, width = tok_ref.shape
    own = rows // 4
    count = lax.axis_size("seq")
    plane = count // 4
    z, p = i // plane, lax.rem(i, plane)
    last = i // GROUP
    y_lo, core = h // 2, lax.rem(h, 2)
    partner = y_lo * 2 + 1 - core
    mate = (1 - y_lo) * 2 + core
    me = i * 4 + h
    devices = count * 4
    hidden_width = up.shape[1]
    gate, down = wq.at[:, 0:hidden_width], wo.at[0:hidden_width, :]

    def load(hbm, vmem, n):
        return pltpu.make_async_copy(hbm, vmem, load_sem.at[n])

    first_loads = [
        load(tok_hbm, tok_ref, 0),
        load(wk_hbm, wk_ref, 1),
        load(wv_hbm, wv_ref, 2),
        load(wq_hbm, wq, 3),
        load(wo_hbm, wo, 4),
        load(up_hbm, up, 5),
    ]
    small_loads = [
        load(in_gain_hbm, in_gain, 9),
        load(post_gain_hbm, post_gain, 10),
        load(q_gain_hbm, q_gain, 11),
        load(k_gain_hbm, k_gain, 12),
        load(ids_hbm, ids_ref, 13),
        load(score_hbm, score_ref, 14),
    ]
    for one in first_loads[0:3] + small_loads + first_loads[3:]:
        one.start()
    for u in range(GROUP):

        @pl.when(last * GROUP + u > i)
        def _():
            kbuf[last * GROUP + u] = jnp.zeros(kbuf.shape[1:], kbuf.dtype)
            vbuf[last * GROUP + u] = jnp.zeros(vbuf.shape[1:], vbuf.dtype)

    barrier = pltpu.get_barrier_semaphore()

    def greet(t, c):
        other = lax.rem(me + t, devices)
        pl.semaphore_signal(
            barrier, inc=1, device_id=(other // 4, lax.rem(other, 4)), device_id_type=MESH
        )
        return c

    lax.fori_loop(1, devices, greet, 0)

    def turned(vectors, gain):
        mean_sq = jnp.mean(vectors * vectors, axis=-1, keepdims=True)
        vectors = vectors * lax.rsqrt(mean_sq + EPSILON) * gain
        return vectors * cos_ref[...] + pltpu.roll(vectors, dim // 2, 1) * sin_ref[...]

    first_loads[0].wait()
    for one in small_loads:
        one.wait()
    tokens = tok_ref[...].astype(jnp.float32)
    mean_sq = jnp.mean(tokens * tokens, axis=-1, keepdims=True)
    normed[...] = (tokens * lax.rsqrt(mean_sq + EPSILON) * in_gain[...]).astype(jnp.bfloat16)
    first_loads[1].wait()
    key = jnp.dot(normed[...], wk_ref[...], preferred_element_type=jnp.float32)
    kbuf[i] = turned(key, k_gain[...]).astype(jnp.bfloat16)
    first_loads[2].wait()
    value = jnp.dot(normed[...], wv_ref[...], preferred_element_type=jnp.float32)
    for w in range(rows // dim):
        vbuf[i, dim * w : dim * (w + 1), :] = value[dim * w : dim * (w + 1)].T.astype(jnp.bfloat16)
    pl.semaphore_wait(barrier, devices - 1)

    def copy(buf, send, recv, at, source, zt, pt):
        return pltpu.make_async_remote_copy(
            src_ref=buf.at[source],
            dst_ref=buf.at[source],
            send_sem=send.at[at],
            recv_sem=recv.at[source],
            device_id=(zt * plane + pt, h),
            device_id_type=MESH,
        )

    def k_column(zt):
        return copy(kbuf, send_k, recv_k, count + zt, i, zt, p)

    def k_plane(source, pt):
        return copy(kbuf, send_k, recv_k, source // plane * plane + pt, source, z, pt)

    def v_plane(pt):
        return copy(vbuf, send_v, recv_v, count + pt, i, z, pt)

    def v_column(source, zt):
        return copy(vbuf, send_v, recv_v, lax.rem(source, plane) * 4 + zt, source, zt, p)

    def columns(act):
        def one(zt, c):
            act(zt)
            return c

        lax.fori_loop(z + 1, 4, one, 0)

    def peers(act):
        def one(t, c):
            act(lax.rem(p + t, plane))
            return c

        lax.fori_loop(1, plane, one, 0)

    def when(cond, act):
        @pl.when(cond)
        def _():
            act()

    columns(lambda zt: k_column(zt).start())
    peers(lambda pt: when((z < 3) | (pt > p), lambda: v_plane(pt).start()))
    peers(lambda pt: when(pt > p, lambda: k_plane(i, pt).start()))
    columns(lambda zt: v_column(i, zt).start())
    first_loads[3].wait()
    for two in range(heads // 2):
        both = jnp.dot(
            normed[...], wq[:, two * 2 * dim : (two + 1) * 2 * dim], preferred_element_type=jnp.float32
        )
        for w in range(2):
            head = two * 2 + w
            query = turned(both[:, w * dim : (w + 1) * dim], q_gain[...])
            q_t[:, head * rows : (head + 1) * rows] = query.T.astype(jnp.bfloat16)

    load(gate_hbm, gate, 3).start()
    def pass_k(t, c):
        source = (z - t) * plane + p
        k_plane(source, p).wait_recv()
        peers(lambda pt: k_plane(source, pt).start())
        return c

    lax.fori_loop(1, z + 1, pass_k, 0)

    def pass_v(zt):
        def one(pt):
            source = z * plane + pt
            when(zt == z + 1, lambda: v_column(source, z).wait_recv())
            v_column(source, zt).start()

        peers(one)

    columns(pass_v)
    ids = ids_ref[...].astype(jnp.float32).T.astype(jnp.int32)
    lane = lax.broadcasted_iota(jnp.int32, (own, devices), 1)
    hits = [ids[:, n : n + 1] == lane for n in range(ids.shape[1])]
    named = sum(jnp.where(hit, 1.0, 0.0) for hit in hits)
    order = [lax.broadcasted_iota(jnp.int32, (own, own), n) for n in range(2)]
    earlier_rows = jnp.where(order[0] > order[1], 1.0, 0.0).astype(jnp.bfloat16)
    rank = jnp.dot(earlier_rows, named.astype(jnp.bfloat16), preferred_element_type=jnp.float32)
    scores_in = score_ref[...].T
    mixing = scores_in / jnp.sum(scores_in, axis=1, keepdims=True)
    slots = jnp.zeros((own, devices), jnp.int32)
    mixes = jnp.zeros((own, devices), jnp.float32)
    for n, hit in enumerate(hits):
        place = jnp.sum(jnp.where(hit, rank, 0.0), axis=1, keepdims=True).astype(jnp.int32)
        slots = jnp.where(lane == n, ids[:, n : n + 1] * cap + place, slots)
        mixes = jnp.where(lane == n, mixing[:, n : n + 1], mixes)
    slot_v[...] = slots
    mix_v[...] = mixes
    idx_v[...] = jnp.zeros(idx_v.shape, jnp.int32)
    token_at = lax.broadcasted_iota(jnp.int32, (own, devices), 0).astype(jnp.float32)
    for c in range(cap):
        chosen = (rank == c) & (named > 0)
        row = jnp.sum(jnp.where(chosen, token_at, 0.0), axis=0, keepdims=True)
        idx_v[c : c + 1, :] = row.astype(jnp.int32)
    tables = [load(slot_v, slot_s, 6), load(mix_v, mix_s, 7), load(idx_v, idx_s, 8)]
    for one in tables:
        one.start()
    scale = dim ** (-0.5) * LOG2E

    def arrive(g):
        for u in range(GROUP):
            source = g * GROUP + u
            when((source < i) & (lax.rem(source, plane) != p), lambda: k_plane(source, p).wait_recv())
            when(
                (source < i) & ((source // plane != z) | (z == 3)),
                lambda: v_column(source, z).wait_recv(),
            )

    def group(g, masked):
        keys = jnp.concatenate([kbuf[g * GROUP + u] for u in range(GROUP)], axis=0)
        halves = [
            vbuf[g * GROUP + u, dim * w : dim * (w + 1), :]
            for u in range(GROUP)
            for w in range(rows // dim)
        ]
        values = jnp.concatenate(halves, axis=1)
        values = jnp.concatenate([values, jnp.ones((16, values.shape[1]), values.dtype)], axis=0)
        scores = jnp.dot(keys, q_t[...], preferred_element_type=jnp.float32)
        if masked:
            key_at = lax.broadcasted_iota(jnp.int32, scores.shape, 0)
            query_at = lax.broadcasted_iota(jnp.int32, scores.shape, 1) % rows + (i - g * GROUP) * rows
            scores = jnp.where(key_at <= query_at, scores, -1e30)
        top = jnp.max(scores, axis=0, keepdims=True)
        if not masked:
            top = jnp.maximum(top, m_s[...])
        weights = jnp.exp2(scores * scale - top * scale)
        mixed = jnp.dot(values, weights.astype(jnp.bfloat16), preferred_element_type=jnp.float32)
        if masked:
            l_s[...] = mixed[dim : dim + 1]
            acc[...] = mixed[:dim]
        else:
            shrink = jnp.exp2((m_s[...] - top) * scale)
            l_s[...] = l_s[...] * shrink + mixed[dim : dim + 1]
            acc[...] = acc[...] * shrink + mixed[:dim]
        m_s[...] = top

    def open_gate():
        def tell(t, c):
            other = lax.rem(me + t, devices)
            pl.semaphore_signal(
                gate_sem, inc=1, device_id=(other // 4, lax.rem(other, 4)), device_id_type=MESH
            )
            return c

        lax.fori_loop(1, devices, tell, 0)

    arrive(last)
    group(last, True)

    def earlier(t, c):
        arrive(last - t)
        group(last - t, False)
        return c

    lax.fori_loop(1, last + 1, earlier, 0)
    for head in range(heads):
        columns_here = slice(head * rows, (head + 1) * rows)
        part = acc[:, columns_here] / l_s[:, columns_here]
        attended[:, head * dim : (head + 1) * dim] = part.T.astype(jnp.bfloat16)
    first_loads[4].wait()
    chunks = pair_out.shape[0]
    wide = width // chunks

    def block(r):
        return pl.ds(pl.multiple_of(r * own, own), own)

    def to_partner(n):
        return pltpu.make_async_remote_copy(
            src_ref=pair_out.at[n],
            dst_ref=pair_in.at[n],
            send_sem=send_pair.at[n],
            recv_sem=recv_pair.at[n],
            device_id=(i, partner),
            device_id_type=MESH,
        )

    def to_mate(n):
        return pltpu.make_async_remote_copy(
            src_ref=chip_out.at[n],
            dst_ref=chip_in.at[n],
            send_sem=send_chip.at[n],
            recv_sem=recv_chip.at[n],
            device_id=(i, mate),
            device_id_type=MESH,
        )

    def sum_pair(n):
        at = slice(n * wide, (n + 1) * wide)
        to_partner(n).wait_recv()
        far = kept[pl.ds(pl.multiple_of((1 - y_lo) * own, own), own), at]
        far = far + pair_in[n, pl.ds(pl.multiple_of((1 - y_lo) * own, own), own), :].astype(jnp.float32)
        chip_out[n] = far.astype(jnp.bfloat16)
        to_mate(n).start()
        near = kept[pl.ds(pl.multiple_of(y_lo * own, own), own), at]
        near = near + pair_in[n, pl.ds(pl.multiple_of(y_lo * own, own), own), :].astype(jnp.float32)
        residual[:, at] = near + tok_ref[block(h), at].astype(jnp.float32)

    for n in range(chunks):
        at = slice(n * wide, (n + 1) * wide)
        product[...] = jnp.dot(attended[...], wo[:, at], preferred_element_type=jnp.float32)
        for half in range(2):
            pair_out[n, half * own : (half + 1) * own, :] = product[
                block(half * 2 + 1 - core), :
            ].astype(jnp.bfloat16)
        to_partner(n).start()
        for half in range(2):
            kept[half * own : (half + 1) * own, at] = product[block(half * 2 + core), :]
        if n > 0:
            sum_pair(n - 1)
    sum_pair(chunks - 1)
    for n in range(chunks):
        at = slice(n * wide, (n + 1) * wide)
        to_mate(n).wait_recv()
        residual[:, at] = residual[:, at] + chip_in[n].astype(jnp.float32)
    load(down_hbm, down, 4).start()
    cuts = width // 128
    mean_sq = jnp.mean(residual[...] * residual[...], axis=-1, keepdims=True)
    scale_rows = lax.rsqrt(mean_sq + EPSILON)
    for c in range(cuts):
        at = slice(c * 128, (c + 1) * 128)
        home[pl.ds(c, own, stride=cuts), :] = residual[:, at]
        wide_rows[pl.ds(c, own, stride=cuts), :] = residual[:, at] * scale_rows * post_gain[:, at]
    tiles[...] = wide_rows[0 : own * cuts, :].astype(jnp.bfloat16).reshape(tiles.shape)
    for one in tables:
        one.wait()

    def fill(target, ref, at):
        for c in range(cap):
            ref[at * cap + c] = tiles[jnp.clip(idx_s[c, target], 0, own - 1)]

    def part(ref, t):
        return ref.at[pl.ds(t * cap, cap)]

    def dispatch(t):
        return pltpu.make_async_remote_copy(
            src_ref=part(outgoing, t),
            dst_ref=part(arrived, t),
            send_sem=send_out.at[t],
            recv_sem=recv_out.at[t],
            device_id=neighbour(i, h, t, 1),
            device_id_type=MESH,
        )

    def give_back(t):
        return pltpu.make_async_remote_copy(
            src_ref=part(arrived, t),
            dst_ref=part(returned, me),
            send_sem=send_back.at[t],
            recv_sem=recv_back.at[me],
            device_id=neighbour(i, h, t, -1),
            device_id_type=MESH,
        )

    def come_back(expert):
        return pltpu.make_async_remote_copy(
            src_ref=part(arrived, expert),
            dst_ref=part(returned, expert),
            send_sem=send_back.at[expert],
            recv_sem=recv_back.at[expert],
            device_id=(expert // 4, lax.rem(expert, 4)),
            device_id_type=MESH,
        )

    def post(t, c):
        ts, th = neighbour(i, h, t, 1)
        fill(ts * 4 + th, outgoing, t)
        dispatch(t).start()
        return c

    when(z == 3, open_gate)
    pl.semaphore_wait(gate_sem, jnp.where(z == 3, devices // 4 - 1, devices // 4))
    lax.fori_loop(1, devices, post, 0)
    fill(me, arrived, 0)
    first_loads[5].wait()
    load(gate_hbm, gate, 3).wait()
    load(down_hbm, down, 4).wait()
    size = batch.shape[0]
    each = size // cap

    def work(k, c):
        def await_one(t, c):
            step = k * each + t
            when(step > 0, lambda: dispatch(step).wait_recv())
            return c

        lax.fori_loop(0, each, await_one, 0)
        place = pl.ds(k * size, size)
        wide_rows[...] = arrived[place].astype(jnp.float32).reshape(wide_rows.shape)
        for c in range(cuts):
            batch[:, c * 128 : (c + 1) * 128] = wide_rows[pl.ds(c, size, stride=cuts), :].astype(
                jnp.bfloat16
            )
        gate_proj = jnp.dot(batch[...], gate[...], preferred_element_type=jnp.float32)
        up_proj = jnp.dot(batch[...], up[...], preferred_element_type=jnp.float32)
        hidden = (gate_proj / (1.0 + jnp.exp(-gate_proj)) * up_proj).astype(jnp.bfloat16)
        result = jnp.dot(hidden, down[...], preferred_element_type=jnp.float32)
        for c in range(cuts):
            wide_rows[pl.ds(c, size, stride=cuts), :] = result[:, c * 128 : (c + 1) * 128]
        arrived[place] = wide_rows[...].astype(jnp.bfloat16).reshape(size, cuts, 128)

        def answer(t, c):
            step = k * each + t
            when(step > 0, lambda: give_back(step).start())
            return c

        lax.fori_loop(0, each, answer, 0)
        return c

    lax.fori_loop(0, devices // each, work, 0)
    returned[pl.ds(me * cap, cap)] = arrived[0:cap]

    columns(lambda zt: k_column(zt).wait_send())
    peers(lambda pt: when((z < 3) | (pt > p), lambda: v_plane(pt).wait_send()))
    peers(lambda pt: when(pt > p, lambda: k_plane(i, pt).wait_send()))
    columns(lambda zt: v_column(i, zt).wait_send())

    def passed_k(t, c):
        peers(lambda pt: k_plane((z - t) * plane + p, pt).wait_send())
        return c

    lax.fori_loop(1, z + 1, passed_k, 0)
    peers(lambda pt: columns(lambda zt: v_column(z * plane + pt, zt).wait_send()))
    for n in range(chunks):
        to_partner(n).wait_send()
        to_mate(n).wait_send()

    def finish(t, c):
        dispatch(t).wait_send()
        give_back(t).wait_send()
        return c

    lax.fori_loop(1, devices, finish, 0)

    def settle(expert, c):
        when(expert != me, lambda: come_back(expert).wait_recv())
        return c

    lax.fori_loop(0, devices, settle, 0)

    def combine_one(t):
        place = pl.ds(pl.multiple_of(t * cuts, cuts), cuts)
        total = jnp.zeros((cuts, 128), jnp.float32)
        for n in range(ids_ref.shape[0]):
            total = total + returned[jnp.clip(slot_s[t, n], 0, devices * cap - 1)].astype(jnp.float32) * mix_s[t, n]
        home[place, :] = home[place, :] + total

    def combine(t, c):
        for n in range(4):
            combine_one(t * 4 + n)
        return c

    lax.fori_loop(0, own // 4, combine, 0)
    for c in range(cuts):
        out_ref[:, c * 128 : (c + 1) * 128] = home[pl.ds(c, own, stride=cuts), :].astype(jnp.bfloat16)


def layer(small, large, seq_count, cap):
    tokens, wk, wv, wq, wo, gate, up, down = large
    rows, width = tokens.shape
    dim = wk.shape[1]
    heads = wq.shape[1] // dim
    own = rows // 4
    devices = seq_count * 4
    chunks = 4
    wide = width // chunks
    cuts = width // 128
    size = devices * cap // 4
    bf16, f32 = jnp.bfloat16, jnp.float32
    vmem = pl.BlockSpec(memory_space=pltpu.VMEM)
    hbm = pl.BlockSpec(memory_space=pltpu.HBM)
    dma = pltpu.SemaphoreType.DMA
    return pl.pallas_call(
        functools.partial(layer_kernel, heads, dim, cap),
        out_shape=jax.ShapeDtypeStruct((own, width), bf16),
        in_specs=[vmem] * 2 + [hbm] * (len(small) - 2 + len(large)),
        out_specs=vmem,
        scratch_shapes=[
            *(pltpu.VMEM(a.shape, a.dtype) for a in small[2:]),
            pltpu.VMEM(tokens.shape, bf16),
            pltpu.VMEM(wk.shape, bf16),
            pltpu.VMEM(wv.shape, bf16),
            pltpu.VMEM(wq.shape, bf16),
            pltpu.VMEM(wo.shape, bf16),
            pltpu.VMEM(up.shape, bf16),
            pltpu.VMEM(tokens.shape, bf16),
            pltpu.VMEM((dim, heads * rows), bf16),
            pltpu.VMEM((seq_count, rows, dim), bf16),
            pltpu.VMEM((seq_count, rows, dim), bf16),
            pltpu.VMEM((1, heads * rows), f32),
            pltpu.VMEM((1, heads * rows), f32),
            pltpu.VMEM((dim, heads * rows), f32),
            pltpu.VMEM((rows, heads * dim), bf16),
            pltpu.VMEM((rows, wide), f32),
            pltpu.VMEM((2 * own, width), f32),
            pltpu.VMEM((chunks, 2 * own, wide), bf16),
            pltpu.VMEM((chunks, 2 * own, wide), bf16),
            pltpu.VMEM((chunks, own, wide), bf16),
            pltpu.VMEM((chunks, own, wide), bf16),
            pltpu.VMEM((own, width), f32),
            pltpu.VMEM((own, devices), jnp.int32),
            pltpu.VMEM((own, devices), f32),
            pltpu.VMEM((8, devices), jnp.int32),
            pltpu.SMEM((own, devices), jnp.int32),
            pltpu.SMEM((own, devices), f32),
            pltpu.SMEM((8, devices), jnp.int32),
            pltpu.VMEM((size * cuts, 128), f32),
            pltpu.VMEM((own * cuts, 128), f32),
            pltpu.VMEM((own, cuts, 128), bf16),
            pltpu.VMEM((devices * cap, cuts, 128), bf16),
            pltpu.VMEM((devices * cap, cuts, 128), bf16),
            pltpu.VMEM((size, width), bf16),
            pltpu.VMEM((devices * cap, cuts, 128), bf16),
            dma((15,)),
            dma((seq_count + 4,)),
            dma((seq_count + 8,)),
            dma((seq_count,)),
            dma((seq_count,)),
            dma((chunks,)),
            dma((chunks,)),
            dma((chunks,)),
            dma((chunks,)),
            dma((devices,)),
            dma((devices,)),
            dma((devices,)),
            dma((devices,)),
            pltpu.SemaphoreType.REGULAR,
        ],
        compiler_params=pltpu.CompilerParams(
            collective_id=0, has_side_effects=True, vmem_limit_bytes=60 << 20
        ),
        name="layer",
    )(*small, *large)


def body(
    tokens,
    input_gain,
    w_query,
    w_key,
    w_value,
    query_gain,
    key_gain,
    w_out,
    post_gain,
    expert_ids,
    route_weights,
    w_gate,
    w_up,
    w_down,
):
    tok_rows = tokens.shape[0]
    head_dim = query_gain.shape[0]
    seq_count = lax.axis_size("seq")
    half_dim = head_dim // 2
    positions = (lax.axis_index("seq") * tok_rows + jnp.arange(tok_rows, dtype=jnp.int32)).astype(jnp.float32)
    frequency = THETA ** (-jnp.arange(half_dim, dtype=jnp.float32) * 2.0 / head_dim)
    angles = positions[:, None] * frequency[None, :]
    cosine, sine = jnp.cos(angles), jnp.sin(angles)
    small = (
        jnp.concatenate([cosine, cosine], axis=1),
        jnp.concatenate([-sine, sine], axis=1),
        input_gain.reshape(1, -1),
        post_gain.reshape(1, -1),
        query_gain.reshape(1, -1),
        key_gain.reshape(1, -1),
        expert_ids.T,
        route_weights.T,
    )
    large = (tokens, w_key, w_value, w_query, w_out, w_gate[0], w_up[0], w_down[0])
    return layer(small, large, seq_count, CAPACITY)


def solution(mesh):
    placed = (
        P("seq", None),
        P(),
        P(None, "head"),
        P(None, "head"),
        P(None, "head"),
        P(),
        P(),
        P("head", None),
        P(),
        P(("seq", "head"), None),
        P(("seq", "head"), None),
        P(("seq", "head"), None, None),
        P(("seq", "head"), None, None),
        P(("seq", "head"), None, None),
    )
    return jax.shard_map(
        body, mesh=mesh, in_specs=placed, out_specs=P(("seq", "head"), None), check_vma=False
    )
```

```python
import functools

import jax
import jax.numpy as jnp
from jax import lax
from jax.experimental import pallas as pl
from jax.experimental.pallas import tpu as pltpu
from jax.sharding import PartitionSpec as P

MESH = pl.DeviceIdType.MESH
EPSILON = 1e-06
THETA = 1000000.0
LOG2E = 1.4426950408889634
GROUP = 4
CAPACITY = 6


def neighbour(s, h, step, sign):
    z, x, y, core = s // 8, lax.rem(s // 2, 4), lax.rem(s, 2) * 2 + h // 2, lax.rem(h, 2)
    turn = lax.rem(step * 37, 128)
    z = lax.rem(z + sign * (turn // 32) + 4, 4)
    x = lax.rem(x + sign * lax.rem(turn // 8, 4) + 4, 4)
    y = lax.rem(y + sign * lax.rem(turn // 2, 4) + 4, 4)
    core = lax.rem(core + lax.rem(turn, 2), 2)
    return z * 8 + x * 2 + y // 2, lax.rem(y, 2) * 2 + core


def layer_kernel(
    heads,
    dim,
    cap,
    cos_ref,
    sin_ref,
    in_gain_hbm,
    post_gain_hbm,
    q_gain_hbm,
    k_gain_hbm,
    ids_hbm,
    score_hbm,
    tok_hbm,
    wk_hbm,
    wv_hbm,
    wq_hbm,
    wo_hbm,
    gate_hbm,
    up_hbm,
    down_hbm,
    out_ref,
    in_gain,
    post_gain,
    q_gain,
    k_gain,
    ids_ref,
    score_ref,
    tok_ref,
    wk_ref,
    wv_ref,
    wq,
    wo,
    up,
    normed,
    q_t,
    kbuf,
    vbuf,
    m_s,
    l_s,
    acc,
    attended,
    product,
    kept,
    pair_out,
    pair_in,
    chip_out,
    chip_in,
    residual,
    slot_v,
    mix_v,
    idx_v,
    slot_s,
    mix_s,
    idx_s,
    wide_rows,
    home,
    tiles,
    outgoing,
    arrived,
    batch,
    returned,
    load_sem,
    send_k,
    send_v,
    recv_k,
    recv_v,
    send_pair,
    recv_pair,
    send_chip,
    recv_chip,
    send_out,
    recv_out,
    send_back,
    recv_back,
    gate_sem,
):
    i = lax.axis_index("seq")
    h = lax.axis_index("head")
    rows, width = tok_ref.shape
    own = rows // 4
    count = lax.axis_size("seq")
    plane = count // 4
    z, p = i // plane, lax.rem(i, plane)
    last = i // GROUP
    y_lo, core = h // 2, lax.rem(h, 2)
    partner = y_lo * 2 + 1 - core
    mate = (1 - y_lo) * 2 + core
    me = i * 4 + h
    devices = count * 4
    hidden_width = up.shape[1]
    gate, down = wq.at[:, 0:hidden_width], wo.at[0:hidden_width, :]

    def load(hbm, vmem, n):
        return pltpu.make_async_copy(hbm, vmem, load_sem.at[n])

    first_loads = [
        load(tok_hbm, tok_ref, 0),
        load(wk_hbm, wk_ref, 1),
        load(wv_hbm, wv_ref, 2),
        load(wq_hbm, wq, 3),
        load(wo_hbm, wo, 4),
        load(up_hbm, up, 5),
    ]
    small_loads = [
        load(in_gain_hbm, in_gain, 9),
        load(post_gain_hbm, post_gain, 10),
        load(q_gain_hbm, q_gain, 11),
        load(k_gain_hbm, k_gain, 12),
        load(ids_hbm, ids_ref, 13),
        load(score_hbm, score_ref, 14),
    ]
    for one in first_loads[0:3] + small_loads + first_loads[3:]:
        one.start()
    for u in range(GROUP):

        @pl.when(last * GROUP + u > i)
        def _():
            kbuf[last * GROUP + u] = jnp.zeros(kbuf.shape[1:], kbuf.dtype)
            vbuf[last * GROUP + u] = jnp.zeros(vbuf.shape[1:], vbuf.dtype)

    barrier = pltpu.get_barrier_semaphore()

    def greet(t, c):
        other = lax.rem(me + t, devices)
        pl.semaphore_signal(
            barrier, inc=1, device_id=(other // 4, lax.rem(other, 4)), device_id_type=MESH
        )
        return c

    lax.fori_loop(1, devices, greet, 0)

    def turned(vectors, gain):
        mean_sq = jnp.mean(vectors * vectors, axis=-1, keepdims=True)
        vectors = vectors * lax.rsqrt(mean_sq + EPSILON) * gain
        return vectors * cos_ref[...] + pltpu.roll(vectors, dim // 2, 1) * sin_ref[...]

    first_loads[0].wait()
    for one in small_loads:
        one.wait()
    tokens = tok_ref[...].astype(jnp.float32)
    mean_sq = jnp.mean(tokens * tokens, axis=-1, keepdims=True)
    normed[...] = (tokens * lax.rsqrt(mean_sq + EPSILON) * in_gain[...]).astype(jnp.bfloat16)
    first_loads[1].wait()
    key = jnp.dot(normed[...], wk_ref[...], preferred_element_type=jnp.float32)
    kbuf[i] = turned(key, k_gain[...]).astype(jnp.bfloat16)
    first_loads[2].wait()
    value = jnp.dot(normed[...], wv_ref[...], preferred_element_type=jnp.float32)
    for w in range(rows // dim):
        vbuf[i, dim * w : dim * (w + 1), :] = value[dim * w : dim * (w + 1)].T.astype(jnp.bfloat16)
    pl.semaphore_wait(barrier, devices - 1)

    def copy(buf, send, recv, at, source, zt, pt):
        return pltpu.make_async_remote_copy(
            src_ref=buf.at[source],
            dst_ref=buf.at[source],
            send_sem=send.at[at],
            recv_sem=recv.at[source],
            device_id=(zt * plane + pt, h),
            device_id_type=MESH,
        )

    def k_column(zt):
        return copy(kbuf, send_k, recv_k, count + zt, i, zt, p)

    def k_plane(source, pt):
        return copy(kbuf, send_k, recv_k, source // plane * plane + pt, source, z, pt)

    def v_plane(pt):
        return copy(vbuf, send_v, recv_v, count + pt, i, z, pt)

    def v_column(source, zt):
        return copy(vbuf, send_v, recv_v, lax.rem(source, plane) * 4 + zt, source, zt, p)

    def columns(act):
        def one(zt, c):
            act(zt)
            return c

        lax.fori_loop(z + 1, 4, one, 0)

    def peers(act):
        def one(t, c):
            act(lax.rem(p + t, plane))
            return c

        lax.fori_loop(1, plane, one, 0)

    def when(cond, act):
        @pl.when(cond)
        def _():
            act()

    columns(lambda zt: k_column(zt).start())
    peers(lambda pt: when((z < 3) | (pt > p), lambda: v_plane(pt).start()))
    peers(lambda pt: when(pt > p, lambda: k_plane(i, pt).start()))
    columns(lambda zt: v_column(i, zt).start())
    first_loads[3].wait()
    for two in range(heads // 2):
        both = jnp.dot(
            normed[...], wq[:, two * 2 * dim : (two + 1) * 2 * dim], preferred_element_type=jnp.float32
        )
        for w in range(2):
            head = two * 2 + w
            query = turned(both[:, w * dim : (w + 1) * dim], q_gain[...])
            q_t[:, head * rows : (head + 1) * rows] = query.T.astype(jnp.bfloat16)

    load(gate_hbm, gate, 3).start()
    def pass_k(t, c):
        source = (z - t) * plane + p
        k_plane(source, p).wait_recv()
        peers(lambda pt: k_plane(source, pt).start())
        return c

    lax.fori_loop(1, z + 1, pass_k, 0)

    def pass_v(zt):
        def one(pt):
            source = z * plane + pt
            when(zt == z + 1, lambda: v_column(source, z).wait_recv())
            v_column(source, zt).start()

        peers(one)

    columns(pass_v)
    ids = ids_ref[...].astype(jnp.float32).T.astype(jnp.int32)
    lane = lax.broadcasted_iota(jnp.int32, (own, devices), 1)
    hits = [ids[:, n : n + 1] == lane for n in range(ids.shape[1])]
    named = sum(jnp.where(hit, 1.0, 0.0) for hit in hits)
    order = [lax.broadcasted_iota(jnp.int32, (own, own), n) for n in range(2)]
    earlier_rows = jnp.where(order[0] > order[1], 1.0, 0.0).astype(jnp.bfloat16)
    rank = jnp.dot(earlier_rows, named.astype(jnp.bfloat16), preferred_element_type=jnp.float32)
    scores_in = score_ref[...].T
    mixing = scores_in / jnp.sum(scores_in, axis=1, keepdims=True)
    slots = jnp.zeros((own, devices), jnp.int32)
    mixes = jnp.zeros((own, devices), jnp.float32)
    for n, hit in enumerate(hits):
        place = jnp.sum(jnp.where(hit, rank, 0.0), axis=1, keepdims=True).astype(jnp.int32)
        slots = jnp.where(lane == n, ids[:, n : n + 1] * cap + place, slots)
        mixes = jnp.where(lane == n, mixing[:, n : n + 1], mixes)
    slot_v[...] = slots
    mix_v[...] = mixes
    idx_v[...] = jnp.zeros(idx_v.shape, jnp.int32)
    token_at = lax.broadcasted_iota(jnp.int32, (own, devices), 0).astype(jnp.float32)
    for c in range(cap):
        chosen = (rank == c) & (named > 0)
        row = jnp.sum(jnp.where(chosen, token_at, 0.0), axis=0, keepdims=True)
        idx_v[c : c + 1, :] = row.astype(jnp.int32)
    tables = [load(slot_v, slot_s, 6), load(mix_v, mix_s, 7), load(idx_v, idx_s, 8)]
    for one in tables:
        one.start()
    scale = dim ** (-0.5) * LOG2E

    def arrive(g):
        for u in range(GROUP):
            source = g * GROUP + u
            when((source < i) & (lax.rem(source, plane) != p), lambda: k_plane(source, p).wait_recv())
            when(
                (source < i) & ((source // plane != z) | (z == 3)),
                lambda: v_column(source, z).wait_recv(),
            )

    def group(g, masked):
        keys = jnp.concatenate([kbuf[g * GROUP + u] for u in range(GROUP)], axis=0)
        halves = [
            vbuf[g * GROUP + u, dim * w : dim * (w + 1), :]
            for u in range(GROUP)
            for w in range(rows // dim)
        ]
        values = jnp.concatenate(halves, axis=1)
        values = jnp.concatenate([values, jnp.ones((16, values.shape[1]), values.dtype)], axis=0)
        scores = jnp.dot(keys, q_t[...], preferred_element_type=jnp.float32)
        if masked:
            key_at = lax.broadcasted_iota(jnp.int32, scores.shape, 0)
            query_at = lax.broadcasted_iota(jnp.int32, scores.shape, 1) % rows + (i - g * GROUP) * rows
            scores = jnp.where(key_at <= query_at, scores, -1e30)
        top = jnp.max(scores, axis=0, keepdims=True)
        if not masked:
            top = jnp.maximum(top, m_s[...])
        weights = jnp.exp2(scores * scale - top * scale)
        mixed = jnp.dot(values, weights.astype(jnp.bfloat16), preferred_element_type=jnp.float32)
        if masked:
            l_s[...] = mixed[dim : dim + 1]
            acc[...] = mixed[:dim]
        else:
            shrink = jnp.exp2((m_s[...] - top) * scale)
            l_s[...] = l_s[...] * shrink + mixed[dim : dim + 1]
            acc[...] = acc[...] * shrink + mixed[:dim]
        m_s[...] = top

    def open_gate():
        def tell(t, c):
            other = lax.rem(me + t, devices)
            pl.semaphore_signal(
                gate_sem, inc=1, device_id=(other // 4, lax.rem(other, 4)), device_id_type=MESH
            )
            return c

        lax.fori_loop(1, devices, tell, 0)

    arrive(last)
    group(last, True)

    def earlier(t, c):
        arrive(last - t)
        group(last - t, False)
        return c

    lax.fori_loop(1, last + 1, earlier, 0)
    for head in range(heads):
        columns_here = slice(head * rows, (head + 1) * rows)
        part = acc[:, columns_here] / l_s[:, columns_here]
        attended[:, head * dim : (head + 1) * dim] = part.T.astype(jnp.bfloat16)
    first_loads[4].wait()
    chunks = pair_out.shape[0]
    wide = width // chunks

    def block(r):
        return pl.ds(pl.multiple_of(r * own, own), own)

    def to_partner(n):
        return pltpu.make_async_remote_copy(
            src_ref=pair_out.at[n],
            dst_ref=pair_in.at[n],
            send_sem=send_pair.at[n],
            recv_sem=recv_pair.at[n],
            device_id=(i, partner),
            device_id_type=MESH,
        )

    def to_mate(n):
        return pltpu.make_async_remote_copy(
            src_ref=chip_out.at[n],
            dst_ref=chip_in.at[n],
            send_sem=send_chip.at[n],
            recv_sem=recv_chip.at[n],
            device_id=(i, mate),
            device_id_type=MESH,
        )

    def sum_pair(n):
        at = slice(n * wide, (n + 1) * wide)
        to_partner(n).wait_recv()
        far = kept[pl.ds(pl.multiple_of((1 - y_lo) * own, own), own), at]
        far = far + pair_in[n, pl.ds(pl.multiple_of((1 - y_lo) * own, own), own), :].astype(jnp.float32)
        chip_out[n] = far.astype(jnp.bfloat16)
        to_mate(n).start()
        near = kept[pl.ds(pl.multiple_of(y_lo * own, own), own), at]
        near = near + pair_in[n, pl.ds(pl.multiple_of(y_lo * own, own), own), :].astype(jnp.float32)
        residual[:, at] = near + tok_ref[block(h), at].astype(jnp.float32)

    for n in range(chunks):
        at = slice(n * wide, (n + 1) * wide)
        product[...] = jnp.dot(attended[...], wo[:, at], preferred_element_type=jnp.float32)
        for half in range(2):
            pair_out[n, half * own : (half + 1) * own, :] = product[
                block(half * 2 + 1 - core), :
            ].astype(jnp.bfloat16)
        to_partner(n).start()
        for half in range(2):
            kept[half * own : (half + 1) * own, at] = product[block(half * 2 + core), :]
        if n > 0:
            sum_pair(n - 1)
    sum_pair(chunks - 1)
    for n in range(chunks):
        at = slice(n * wide, (n + 1) * wide)
        to_mate(n).wait_recv()
        residual[:, at] = residual[:, at] + chip_in[n].astype(jnp.float32)
    load(down_hbm, down, 4).start()
    cuts = width // 128
    mean_sq = jnp.mean(residual[...] * residual[...], axis=-1, keepdims=True)
    scale_rows = lax.rsqrt(mean_sq + EPSILON)
    for c in range(cuts):
        at = slice(c * 128, (c + 1) * 128)
        home[pl.ds(c, own, stride=cuts), :] = residual[:, at]
        wide_rows[pl.ds(c, own, stride=cuts), :] = residual[:, at] * scale_rows * post_gain[:, at]
    tiles[...] = wide_rows[0 : own * cuts, :].astype(jnp.bfloat16).reshape(tiles.shape)
    for one in tables:
        one.wait()

    def fill(target, ref, at):
        for c in range(cap):
            ref[at * cap + c] = tiles[jnp.clip(idx_s[c, target], 0, own - 1)]

    def part(ref, t):
        return ref.at[pl.ds(t * cap, cap)]

    def dispatch(t):
        return pltpu.make_async_remote_copy(
            src_ref=part(outgoing, t),
            dst_ref=part(arrived, t),
            send_sem=send_out.at[t],
            recv_sem=recv_out.at[t],
            device_id=neighbour(i, h, t, 1),
            device_id_type=MESH,
        )

    def give_back(t):
        return pltpu.make_async_remote_copy(
            src_ref=part(arrived, t),
            dst_ref=part(returned, me),
            send_sem=send_back.at[t],
            recv_sem=recv_back.at[me],
            device_id=neighbour(i, h, t, -1),
            device_id_type=MESH,
        )

    def come_back(expert):
        return pltpu.make_async_remote_copy(
            src_ref=part(arrived, expert),
            dst_ref=part(returned, expert),
            send_sem=send_back.at[expert],
            recv_sem=recv_back.at[expert],
            device_id=(expert // 4, lax.rem(expert, 4)),
            device_id_type=MESH,
        )

    def post(t, c):
        ts, th = neighbour(i, h, t, 1)
        fill(ts * 4 + th, outgoing, t)
        dispatch(t).start()
        return c

    when(z == 3, open_gate)
    pl.semaphore_wait(gate_sem, jnp.where(z == 3, devices // 4 - 1, devices // 4))
    lax.fori_loop(1, devices, post, 0)
    fill(me, arrived, 0)
    first_loads[5].wait()
    load(gate_hbm, gate, 3).wait()
    load(down_hbm, down, 4).wait()
    size = batch.shape[0]
    each = size // cap

    def work(k, c):
        def await_one(t, c):
            step = k * each + t
            when(step > 0, lambda: dispatch(step).wait_recv())
            return c

        lax.fori_loop(0, each, await_one, 0)
        place = pl.ds(k * size, size)
        wide_rows[...] = arrived[place].astype(jnp.float32).reshape(wide_rows.shape)
        for c in range(cuts):
            batch[:, c * 128 : (c + 1) * 128] = wide_rows[pl.ds(c, size, stride=cuts), :].astype(
                jnp.bfloat16
            )
        gate_proj = jnp.dot(batch[...], gate[...], preferred_element_type=jnp.float32)
        up_proj = jnp.dot(batch[...], up[...], preferred_element_type=jnp.float32)
        hidden = (gate_proj / (1.0 + jnp.exp(-gate_proj)) * up_proj).astype(jnp.bfloat16)
        result = jnp.dot(hidden, down[...], preferred_element_type=jnp.float32)
        for c in range(cuts):
            wide_rows[pl.ds(c, size, stride=cuts), :] = result[:, c * 128 : (c + 1) * 128]
        arrived[place] = wide_rows[...].astype(jnp.bfloat16).reshape(size, cuts, 128)

        def answer(t, c):
            step = k * each + t
            when(step > 0, lambda: give_back(step).start())
            return c

        lax.fori_loop(0, each, answer, 0)
        return c

    lax.fori_loop(0, devices // each, work, 0)
    returned[pl.ds(me * cap, cap)] = arrived[0:cap]

    columns(lambda zt: k_column(zt).wait_send())
    peers(lambda pt: when((z < 3) | (pt > p), lambda: v_plane(pt).wait_send()))
    peers(lambda pt: when(pt > p, lambda: k_plane(i, pt).wait_send()))
    columns(lambda zt: v_column(i, zt).wait_send())

    def passed_k(t, c):
        peers(lambda pt: k_plane((z - t) * plane + p, pt).wait_send())
        return c

    lax.fori_loop(1, z + 1, passed_k, 0)
    peers(lambda pt: columns(lambda zt: v_column(z * plane + pt, zt).wait_send()))
    for n in range(chunks):
        to_partner(n).wait_send()
        to_mate(n).wait_send()

    def finish(t, c):
        dispatch(t).wait_send()
        give_back(t).wait_send()
        return c

    lax.fori_loop(1, devices, finish, 0)

    def settle(expert, c):
        when(expert != me, lambda: come_back(expert).wait_recv())
        return c

    lax.fori_loop(0, devices, settle, 0)

    def combine_one(t):
        place = pl.ds(pl.multiple_of(t * cuts, cuts), cuts)
        total = jnp.zeros((cuts, 128), jnp.float32)
        for n in range(ids_ref.shape[0]):
            total = total + returned[jnp.clip(slot_s[t, n], 0, devices * cap - 1)].astype(jnp.float32) * mix_s[t, n]
        home[place, :] = home[place, :] + total

    def combine(t, c):
        for n in range(4):
            combine_one(t * 4 + n)
        return c

    lax.fori_loop(0, own // 4, combine, 0)
    for c in range(cuts):
        out_ref[:, c * 128 : (c + 1) * 128] = home[pl.ds(c, own, stride=cuts), :].astype(jnp.bfloat16)


def layer(small, large, seq_count, cap):
    tokens, wk, wv, wq, wo, gate, up, down = large
    rows, width = tokens.shape
    dim = wk.shape[1]
    heads = wq.shape[1] // dim
    own = rows // 4
    devices = seq_count * 4
    chunks = 8
    wide = width // chunks
    cuts = width // 128
    size = devices * cap // 4
    bf16, f32 = jnp.bfloat16, jnp.float32
    vmem = pl.BlockSpec(memory_space=pltpu.VMEM)
    hbm = pl.BlockSpec(memory_space=pltpu.HBM)
    dma = pltpu.SemaphoreType.DMA
    return pl.pallas_call(
        functools.partial(layer_kernel, heads, dim, cap),
        out_shape=jax.ShapeDtypeStruct((own, width), bf16),
        in_specs=[vmem] * 2 + [hbm] * (len(small) - 2 + len(large)),
        out_specs=vmem,
        scratch_shapes=[
            *(pltpu.VMEM(a.shape, a.dtype) for a in small[2:]),
            pltpu.VMEM(tokens.shape, bf16),
            pltpu.VMEM(wk.shape, bf16),
            pltpu.VMEM(wv.shape, bf16),
            pltpu.VMEM(wq.shape, bf16),
            pltpu.VMEM(wo.shape, bf16),
            pltpu.VMEM(up.shape, bf16),
            pltpu.VMEM(tokens.shape, bf16),
            pltpu.VMEM((dim, heads * rows), bf16),
            pltpu.VMEM((seq_count, rows, dim), bf16),
            pltpu.VMEM((seq_count, rows, dim), bf16),
            pltpu.VMEM((1, heads * rows), f32),
            pltpu.VMEM((1, heads * rows), f32),
            pltpu.VMEM((dim, heads * rows), f32),
            pltpu.VMEM((rows, heads * dim), bf16),
            pltpu.VMEM((rows, wide), f32),
            pltpu.VMEM((2 * own, width), f32),
            pltpu.VMEM((chunks, 2 * own, wide), bf16),
            pltpu.VMEM((chunks, 2 * own, wide), bf16),
            pltpu.VMEM((chunks, own, wide), bf16),
            pltpu.VMEM((chunks, own, wide), bf16),
            pltpu.VMEM((own, width), f32),
            pltpu.VMEM((own, devices), jnp.int32),
            pltpu.VMEM((own, devices), f32),
            pltpu.VMEM((8, devices), jnp.int32),
            pltpu.SMEM((own, devices), jnp.int32),
            pltpu.SMEM((own, devices), f32),
            pltpu.SMEM((8, devices), jnp.int32),
            pltpu.VMEM((size * cuts, 128), f32),
            pltpu.VMEM((own * cuts, 128), f32),
            pltpu.VMEM((own, cuts, 128), bf16),
            pltpu.VMEM((devices * cap, cuts, 128), bf16),
            pltpu.VMEM((devices * cap, cuts, 128), bf16),
            pltpu.VMEM((size, width), bf16),
            pltpu.VMEM((devices * cap, cuts, 128), bf16),
            dma((15,)),
            dma((seq_count + 4,)),
            dma((seq_count + 8,)),
            dma((seq_count,)),
            dma((seq_count,)),
            dma((chunks,)),
            dma((chunks,)),
            dma((chunks,)),
            dma((chunks,)),
            dma((devices,)),
            dma((devices,)),
            dma((devices,)),
            dma((devices,)),
            pltpu.SemaphoreType.REGULAR,
        ],
        compiler_params=pltpu.CompilerParams(
            collective_id=0, has_side_effects=True, vmem_limit_bytes=60 << 20
        ),
        name="layer",
    )(*small, *large)


def body(
    tokens,
    input_gain,
    w_query,
    w_key,
    w_value,
    query_gain,
    key_gain,
    w_out,
    post_gain,
    expert_ids,
    route_weights,
    w_gate,
    w_up,
    w_down,
):
    tok_rows = tokens.shape[0]
    head_dim = query_gain.shape[0]
    seq_count = lax.axis_size("seq")
    half_dim = head_dim // 2
    positions = (lax.axis_index("seq") * tok_rows + jnp.arange(tok_rows, dtype=jnp.int32)).astype(jnp.float32)
    frequency = THETA ** (-(jnp.arange(head_dim) % half_dim).astype(jnp.float32) * 2.0 / head_dim)
    angles = positions[:, None] * frequency[None, :]
    sign = jnp.where(jnp.arange(head_dim) < half_dim, -1.0, 1.0).astype(jnp.float32)
    small = (
        jnp.cos(angles),
        jnp.sin(angles) * sign,
        input_gain.reshape(1, -1),
        post_gain.reshape(1, -1),
        query_gain.reshape(1, -1),
        key_gain.reshape(1, -1),
        expert_ids.T,
        route_weights.T,
    )
    large = (tokens, w_key, w_value, w_query, w_out, w_gate[0], w_up[0], w_down[0])
    return layer(small, large, seq_count, CAPACITY)


def solution(mesh):
    placed = (
        P("seq", None),
        P(),
        P(None, "head"),
        P(None, "head"),
        P(None, "head"),
        P(),
        P(),
        P("head", None),
        P(),
        P(("seq", "head"), None),
        P(("seq", "head"), None),
        P(("seq", "head"), None, None),
        P(("seq", "head"), None, None),
        P(("seq", "head"), None, None),
    )
    return jax.shard_map(
        body, mesh=mesh, in_specs=placed, out_specs=P(("seq", "head"), None), check_vma=False
    )
```
